256 devices in a mesh: row: 16 (over z, core), col: 8 (over y_lo, x), gz: 2 (over y_hi).
Axes of the slice: x: 4, y: 4 (y_hi: 2, y_lo: 2; y = y_hi * 2 + y_lo), z: 8, core: 2. Of those that a mesh axis runs over, the one named last changes fastest.
Arguments:
- initial_field: float32 [8, 64, 128, 256], P(None, 'row', 'col', 'gz'), may hold values from -6 to 6
- source_term: float32 [8, 64, 128, 256], P(None, 'row', 'col', 'gz'), may hold values from -6 to 6
- cell_class: int32 [64, 128, 256], P('row', 'col', 'gz'), may hold values from 0 to 15
- class_shift: float32 [16], replicated, may hold values from 0.05 to 4
- surface_cell: int32 [32768], P(('row', 'col', 'gz')), may hold values from 0 to 8191
- live_count: int32 [256], P(('row', 'col', 'gz')), may hold values from 1 to 128, 20480 in all
- panel_geometry: float32 [4, 32768], P(None, ('row', 'col', 'gz')), may hold values from 0.5 to 2
Outputs:
- final_field: float32 [8, 64, 128, 256], P(None, 'row', 'col', 'gz')
- boundary_potential: float32 [8, 32768], P(None, ('row', 'col', 'gz'))
The draws below stay inside these ranges and needn't reach their ends.
Inputs may be any that keep to these rules, and one draw needn't show every extreme that they name: Slots 0 to live_count[b] - 1 of brick b are in use; the counts sum to 20480. `surface_cell`: A cell index inside the panel's own brick, x * 16 * 128 + y * 128 + z.
All inputs are finite; a program needn't handle non-finite values. No bound on the sum of `live_count` on one device may be relied on, other than what follows from the above.
Results may differ from the reference program's by a relative error of at most 0.004.
Values may be sent and summed in bfloat16 or wider, within the bound.
No kernel may reach another device: no remote copies, remote signals or barrier semaphores. Data moves between devices by JAX's collectives and lax.ppermute only.
A program may use at most 128 MiB of HBM per device.

```python
import math
import jax
import jax.numpy as jnp
import numpy as np
from jax import lax

EXC = 8
CLASSES = 16
CX = 4
CY = 16
CZ = 128
SLOTS = 128
SWEEPS = 3
ROUNDS = 2
NX = 64
NY = 128
NZ = 256
PANELS = 32768
N_COL = 8
N_GZ = 2
DEVICES = 256


def plant(result, stream_key, smallest, largest):
    index_at = [jax.random.randint(jax.random.fold_in(stream_key, axis), (), 0, length) for axis, length in enumerate(result.shape)]
    widest = result.shape.index(max(result.shape))
    beside = index_at[:widest] + [(index_at[widest] + 1) % result.shape[widest]] + index_at[widest + 1:]
    return result.at[tuple(index_at)].set(smallest).at[tuple(beside)].set(largest)


def shard_levels(key, extent, pieces, smallest, high):
    loudness = 1.0
    for position, blocks in pieces:
        heights = jax.random.uniform(jax.random.fold_in(jax.random.fold_in(key, 6), position), (blocks,), jnp.float32, smallest / len(pieces), high / len(pieces))
        loudness = loudness * jnp.repeat(jnp.exp(heights), extent[position] // blocks).reshape((-1,) + (1,) * (len(extent) - 1 - position))
    return loudness


def split_up(count, total, most, lean):
    weights = [(1 << 20) // math.isqrt(grade ** lean) + 1 for grade in range(2, count + 1)]
    spare, holding = total - most - (count - 1), [1] * (count - 1)
    while spare > 0:
        candidates = [i for i in range(count - 1) if holding[i] < most]
        mass, budget = sum([weights[i] for i in candidates]), spare
        for i in candidates:
            extra = min(most - holding[i], max(1, budget * weights[i] // mass), spare)
            holding[i] = holding[i] + extra
            spare = spare - extra
    return np.array([most] + holding)


def uneven_parts(own_key, number_of, total, limit, slope):
    if number_of == 2:
        one = jax.random.randint(own_key, (), max(1, total - limit), min(limit, total - 1) + 1)
        return jnp.stack([one, total - one])
    tallies = jnp.asarray(split_up(number_of, total, limit, slope), jnp.int32)
    couples = (number_of - 1) // 2
    donor, receiver = tallies[1:1 + 2 * couples:2], tallies[2:2 + 2 * couples:2]
    room = jnp.minimum(donor - 1, limit - receiver)
    shifted = jax.random.randint(jax.random.fold_in(own_key, 1), (couples,), 0, 1 << 20) % (room + 1)
    tallies = tallies.at[1:1 + 2 * couples:2].set(donor - shifted).at[2:2 + 2 * couples:2].set(receiver + shifted)
    return tallies[jax.random.permutation(jax.random.fold_in(own_key, 2), number_of)]


def bell_draw(stream_key, extent, scale, most, cuts=(), held_as=jnp.bfloat16):
    values = jax.random.normal(stream_key, extent, jnp.float32) * scale
    if len(cuts) > 0:
        values = shard_levels(stream_key, extent, cuts, -0.22, 0.18) * values
    return jnp.clip(values, min=-most, max=most).astype(held_as)


def setup_inputs(seed: int = 0) -> dict:
    seeds = jax.random.split(jax.random.key(seed), 8)
    return {
        "initial_field": bell_draw(seeds[0], (EXC, NX, NY, NZ), 1.0, 6.0, ((1, 16), (2, 8), (3, 2)), jnp.float32),
        "source_term": bell_draw(seeds[1], (EXC, NX, NY, NZ), 1.0, 6.0, ((1, 16), (2, 8), (3, 2)), jnp.float32),
        "cell_class": plant(jax.random.randint(seeds[2], (NX, NY, NZ), 0, CLASSES), jax.random.fold_in(seeds[2], 1), 0, CLASSES - 1).astype(jnp.int32),
        "class_shift": jnp.clip(jnp.exp(jax.random.uniform(seeds[3], (CLASSES,), jnp.float32, math.log(0.05), math.log(4.0))), 0.05, 4.0),
        "surface_cell": plant(jax.random.randint(seeds[4], (PANELS,), 0, CX * CY * CZ), jax.random.fold_in(seeds[4], 1), 0, (CX * CY * CZ) - 1).astype(jnp.int32),
        "live_count": uneven_parts(seeds[5], DEVICES, PANELS * 5 // 8, SLOTS, 2).astype(jnp.int32),
        "panel_geometry": jnp.clip(0.5 + 1.5 * jax.random.uniform(seeds[6], (4, PANELS), jnp.float32) ** shard_levels(seeds[6], (4, PANELS), ((1, 256),), -0.2, 0.2), 0.5, 2.0),
    }


relax_weight = 0.8
wave_number = 25.0
soften = 0.05
coupling = 0.5

def neighbours(padded):
    total = padded[:, 2:, 1:-1, 1:-1] + padded[:, :-2, 1:-1, 1:-1]
    total = total + padded[:, 1:-1, 2:, 1:-1] + padded[:, 1:-1, :-2, 1:-1]
    total = total + padded[:, 1:-1, 1:-1, 2:] + padded[:, 1:-1, 1:-1, :-2]
    return total

def relax(state, padded, forcing, shift_field):
    diagonal = 6.0 + shift_field
    residual = forcing - (diagonal * state - neighbours(padded))
    return state + relax_weight * residual / diagonal

def kernel_tile(sources, targets, factor):
    delta_x = targets[0][None, :] - sources[0][:, None]
    delta_y = targets[1][None, :] - sources[1][:, None]
    delta_z = targets[2][None, :] - sources[2][:, None]
    distance = jnp.sqrt(delta_x * delta_x + delta_y * delta_y + delta_z * delta_z)
    values = sources[3][:, None] * jnp.cos(wave_number * distance) / (distance + soften)
    return (values * factor).astype(jnp.bfloat16)

def reference(initial_field, source_term, cell_class, class_shift, surface_cell, live_count, panel_geometry):
    shift_field = class_shift[cell_class]
    factor = 1.0 / math.sqrt(PANELS)
    slot_index = jnp.arange(PANELS, dtype=jnp.int32)
    owner = (slot_index // SLOTS).astype(jnp.int32)
    live = (slot_index % SLOTS < live_count[owner]).astype(jnp.float32)
    brick_row = owner // (N_COL * N_GZ)
    brick_col = owner // N_GZ % N_COL
    brick_depth = owner % N_GZ
    global_x = brick_row * CX + surface_cell // (CY * CZ)
    global_y = brick_col * CY + surface_cell // CZ % CY
    global_z = brick_depth * CZ + surface_cell % CZ
    cell_of = ((global_x * NY + global_y) * NZ + global_z).astype(jnp.int32)
    width = math.gcd(PANELS, 512)
    blocks = panel_geometry.reshape(4, PANELS // width, width).transpose(1, 0, 2)
    state = initial_field
    load = jnp.zeros_like(source_term)
    potential = jnp.zeros((EXC, PANELS), jnp.float32)
    for round_index in range(ROUNDS):
        forcing = source_term + load
        for sweep_index in range(SWEEPS):
            padded = jnp.pad(state, ((0, 0), (1, 1), (1, 1), (1, 1)))
            state = relax(state, padded, forcing, shift_field)
        density = (state.reshape(EXC, -1)[:, cell_of] * live).astype(jnp.bfloat16)
        density = lax.optimization_barrier(density).astype(jnp.float32)

        def target_block(targets):
            tile = lax.optimization_barrier(kernel_tile(panel_geometry, targets, factor)).astype(jnp.float32)
            return jnp.dot(density, tile, precision=lax.Precision.HIGHEST)
        potential = lax.map(target_block, blocks)
        potential = potential.transpose(1, 0, 2).reshape(EXC, PANELS) * live
        if round_index + 1 < ROUNDS:
            spread = jnp.zeros((EXC, NX * NY * NZ), jnp.float32).at[:, cell_of].add(coupling * potential)
            load = spread.reshape(source_term.shape)
    return (state, potential)
```

```python
import math

import jax
import jax.numpy as jnp
from jax import lax
from jax.experimental import pallas as pl
from jax.experimental.pallas import tpu as pltpu
from jax.sharding import PartitionSpec as P

SWEEPS = 3
ROUNDS = 2

relax_weight = 0.8
wave_number = 25.0
soften = 0.05
coupling = 0.5

SINE = (6.2831851600894435, -41.34165503141112, 81.60100407296788, -76.54978228730859, 39.53670602126459)
TURNS = wave_number / (2.0 * math.pi)
ROUNDER = 12582912.0


def tile_kernel(source_ref, target_ref, out_ref, columns):
    bricks, slots = target_ref.shape[0], target_ref.shape[2]
    live = jnp.max(source_ref[0, 4:5, :]).astype(jnp.int32)
    columns[...] = jnp.transpose(source_ref[0])
    steps = (live + 15) // 16

    def fill(step, carry):
        rows = pl.ds(pl.multiple_of(step * 16, 16), 16)
        here = columns[rows, :]
        spread = [jnp.broadcast_to(here[:, d : d + 1], (16, slots)) for d in range(4)]
        for brick in range(bricks):
            square = 1e-30
            for d in range(3):
                delta = target_ref[brick, d : d + 1, :] - spread[d]
                square = square + delta * delta
            turns = square * lax.rsqrt(square)
            whole = (turns + ROUNDER) - ROUNDER
            angle = 0.25 - jnp.abs(turns - whole)
            angle2 = angle * angle
            wave = SINE[4]
            for c in SINE[3::-1]:
                wave = wave * angle2 + c
            below = turns + soften * TURNS
            guess = pl.reciprocal(below, approx=True)
            value = (angle * spread[3]) * (guess * (2.0 - below * guess)) * wave
            out_ref[rows, brick * slots : (brick + 1) * slots] = value.astype(jnp.bfloat16)
        return carry

    lax.fori_loop(0, steps, fill, 0)

    def clear(step, carry):
        rows = pl.ds(pl.multiple_of(step * 16, 16), 16)
        out_ref[rows, :] = jnp.zeros((16, out_ref.shape[1]), jnp.bfloat16)
        return carry

    lax.fori_loop(steps, slots // 16, clear, 0)


def make_tile(sources, targets):
    bricks, rows, slots = sources.shape
    width = targets.shape[0] * slots
    return pl.pallas_call(
        tile_kernel,
        grid=(bricks,),
        in_specs=[
            pl.BlockSpec((1, rows, slots), lambda b: (b, 0, 0)),
            pl.BlockSpec(targets.shape, lambda b: (0, 0, 0)),
        ],
        out_specs=pl.BlockSpec((slots, width), lambda b: (b, 0)),
        out_shape=jax.ShapeDtypeStruct((bricks * slots, width), jnp.bfloat16),
        scratch_shapes=[pltpu.VMEM((slots, rows), jnp.float32)],
        name="tile",
    )(sources, targets)


def product_kernel(density_ref, tile_ref, out_ref, total):
    step = pl.program_id(0)

    @pl.when(step == 0)
    def _():
        total[...] = jnp.zeros_like(total)

    values = jnp.concatenate([density_ref[0], density_ref[1]], axis=1)
    total[...] += jnp.dot(values, tile_ref[...], preferred_element_type=jnp.float32)

    @pl.when(step == pl.num_programs(0) - 1)
    def _():
        slots = out_ref.shape[2]
        for brick in range(out_ref.shape[0]):
            out_ref[brick] = total[:, brick * slots : (brick + 1) * slots]


def products(densities, tile):
    bricks, channels, slots = densities.shape
    width = tile.shape[1]
    return pl.pallas_call(
        product_kernel,
        grid=(bricks // 2,),
        in_specs=[
            pl.BlockSpec((2, channels, slots), lambda b: (b, 0, 0)),
            pl.BlockSpec((2 * slots, width), lambda b: (b, 0)),
        ],
        out_specs=pl.BlockSpec((width // slots, channels, slots), lambda b: (0, 0, 0)),
        out_shape=jax.ShapeDtypeStruct((width // slots, channels, slots), jnp.float32),
        scratch_shapes=[pltpu.VMEM((channels, width), jnp.float32)],
        name="product",
    )(densities, tile)


def from_everyone(x, axis):
    copies = jnp.broadcast_to(x, (lax.axis_size(axis), *x.shape))
    return lax.all_to_all(copies, axis, split_axis=0, concat_axis=0, tiled=True)


def padded_2(x, sides, width):
    edges = {}
    for axis, dim in sides:
        devices, length = (lax.axis_size(axis), x.shape[dim])
        up = [(i, (i + 1) % devices) for i in range(devices - 1)]
        last = lax.slice_in_dim(x, length - width, length, axis=dim)
        initial = lax.slice_in_dim(x, 0, width, axis=dim)
        edges[dim] = (
            lax.ppermute(last, axis, up),
            lax.ppermute(initial, axis, [(b, a) for a, b in up]),
        )
    done = []
    for _, dim in sides:
        low, high = edges[dim]
        around = [(width, width) if d in done else (0, 0) for d in range(x.ndim)]
        x = jnp.concatenate([jnp.pad(low, around), x, jnp.pad(high, around)], axis=dim)
        done.append(dim)
    return x


def neighbours(padded):
    total = padded[:, 2:, 1:-1, 1:-1] + padded[:, :-2, 1:-1, 1:-1]
    total = total + padded[:, 1:-1, 2:, 1:-1] + padded[:, 1:-1, :-2, 1:-1]
    total = total + padded[:, 1:-1, 1:-1, 2:] + padded[:, 1:-1, 1:-1, :-2]
    return total


def relax(state, padded, forcing, shift_field):
    diagonal = 6.0 + shift_field
    residual = forcing - (diagonal * state - neighbours(padded))
    return state + relax_weight * residual / diagonal


def shift_lookup(cell_class, class_shift):
    shift_field = jnp.zeros(cell_class.shape, jnp.float32)
    for level in range(class_shift.shape[0]):
        shift_field = shift_field + jnp.where(cell_class == level, class_shift[level], 0.0)
    return shift_field


def local(
    initial_field, source_term, cell_class, class_shift, surface_cell, live_count, panel_geometry
):
    channels, size_x, size_y, size_z = initial_field.shape
    slots = surface_cell.shape[0]
    panels = slots * lax.axis_size("row") * lax.axis_size("col") * lax.axis_size("gz")
    factor = 1.0 / math.sqrt(panels)
    live_row = jnp.broadcast_to(live_count.astype(jnp.float32)[:, None], (1, slots))
    message = jnp.concatenate(
        [panel_geometry[:3] * TURNS, panel_geometry[3:] * (factor * TURNS), live_row, jnp.zeros((3, slots), jnp.float32)]
    )
    sources = from_everyone(message, "row")
    targets = from_everyone(message, ("col", "gz"))
    tile = make_tile(sources, targets)
    shift_field = shift_lookup(cell_class, class_shift)
    live = (jnp.arange(slots, dtype=jnp.int32) < live_count[0]).astype(jnp.float32)
    state = initial_field
    load = jnp.zeros_like(source_term)
    for round_index in range(ROUNDS):
        forcing = source_term + load
        for sweep_index in range(SWEEPS):
            padded = padded_2(state, (("row", 1), ("col", 2), ("gz", 3)), 1)
            state = relax(state, padded, forcing, shift_field)
        density = (jnp.take(state.reshape(channels, -1), surface_cell, axis=1) * live).astype(
            jnp.bfloat16
        )
        shares = products(from_everyone(density, "row"), tile)
        parts = lax.all_to_all(shares, ("col", "gz"), 0, 0, tiled=True)
        potential = jnp.sum(parts, axis=0) * live
        if round_index + 1 < ROUNDS:
            spread = (
                jnp.zeros((channels, size_x * size_y * size_z), jnp.float32)
                .at[:, surface_cell]
                .add(coupling * potential)
            )
            load = spread.reshape(source_term.shape)
    return (state, potential)


def solution(mesh):
    placed = (
        P(None, "row", "col", "gz"),
        P(None, "row", "col", "gz"),
        P("row", "col", "gz"),
        P(),
        P(("row", "col", "gz")),
        P(("row", "col", "gz")),
        P(None, ("row", "col", "gz")),
    )
    return jax.shard_map(
        local,
        mesh=mesh,
        in_specs=placed,
        out_specs=(P(None, "row", "col", "gz"), P(None, ("row", "col", "gz"))),
        check_vma=False,
    )
```

```python
import functools
import math

import jax
import jax.numpy as jnp
from jax import lax
from jax.experimental import pallas as pl
from jax.experimental.pallas import tpu as pltpu
from jax.sharding import PartitionSpec as P

SIZE_Y = 16

relax_weight = 0.8
wave_number = 25.0
soften = 0.05
coupling = 0.5

SINE = (6.2831851600894435, -41.34165503141112, 81.60100407296788, -76.54978228730859, 39.53670602126459)
TURNS = wave_number / (2.0 * math.pi)
ROUNDER = 12582912.0


def tile_kernel(source_ref, target_ref, out_ref, columns):
    bricks, slots = target_ref.shape[0], target_ref.shape[2]
    live = jnp.max(source_ref[0, 4:5, :]).astype(jnp.int32)
    columns[...] = jnp.transpose(source_ref[0])
    steps = (live + 15) // 16

    def fill(step, carry):
        rows = pl.ds(pl.multiple_of(step * 16, 16), 16)
        here = columns[rows, :]
        spread = [jnp.broadcast_to(here[:, d : d + 1], (16, slots)) for d in range(4)]
        for brick in range(bricks):
            square = 1e-30
            for d in range(3):
                delta = target_ref[brick, d : d + 1, :] - spread[d]
                square = square + delta * delta
            turns = square * lax.rsqrt(square)
            whole = (turns + ROUNDER) - ROUNDER
            angle = 0.25 - jnp.abs(turns - whole)
            angle2 = angle * angle
            wave = SINE[4]
            for c in SINE[3::-1]:
                wave = wave * angle2 + c
            below = turns + soften * TURNS
            guess = pl.reciprocal(below, approx=True)
            value = (angle * spread[3]) * (guess * (2.0 - below * guess)) * wave
            out_ref[rows, brick * slots : (brick + 1) * slots] = value.astype(jnp.bfloat16)
        return carry

    lax.fori_loop(0, steps, fill, 0)

    def clear(step, carry):
        rows = pl.ds(pl.multiple_of(step * 16, 16), 16)
        out_ref[rows, :] = jnp.zeros((16, out_ref.shape[1]), jnp.bfloat16)
        return carry

    lax.fori_loop(steps, slots // 16, clear, 0)


def make_tile(sources, targets):
    bricks, rows, slots = sources.shape
    width = targets.shape[0] * slots
    return pl.pallas_call(
        tile_kernel,
        grid=(bricks,),
        in_specs=[
            pl.BlockSpec((1, rows, slots), lambda b: (b, 0, 0)),
            pl.BlockSpec(targets.shape, lambda b: (0, 0, 0)),
        ],
        out_specs=pl.BlockSpec((slots, width), lambda b: (b, 0)),
        out_shape=jax.ShapeDtypeStruct((bricks * slots, width), jnp.bfloat16),
        scratch_shapes=[pltpu.VMEM((slots, rows), jnp.float32)],
        name="tile",
    )(sources, targets)


def product_kernel(near, density_ref, tile_ref, out_ref, total):
    step = pl.program_id(0)

    @pl.when(step == 0)
    def _():
        total[...] = jnp.zeros_like(total)

    values = jnp.concatenate([density_ref[0], density_ref[1]], axis=1)
    total[...] += jnp.dot(values, tile_ref[...], preferred_element_type=jnp.float32)

    @pl.when(step == pl.num_programs(0) - 1)
    def _():
        bricks, slots = out_ref.shape[0], out_ref.shape[-1]
        for brick in range(bricks):
            if not near:
                out_ref[brick] = total[:, brick * slots : (brick + 1) * slots]
                continue
            for n in range(6):
                side, half = brick // 2 + n % 3 - 1, (brick + n // 3) % 2
                other = side * 2 + half
                if 0 <= side < bricks // 2:
                    out_ref[brick, n] = total[:, other * slots : (other + 1) * slots]
                else:
                    out_ref[brick, n] = jnp.zeros((total.shape[0], slots), jnp.float32)


def products(densities, tile, near):
    bricks, channels, slots = densities.shape
    width = tile.shape[1]
    shape = (width // slots, 6, channels, slots) if near else (width // slots, channels, slots)
    return pl.pallas_call(
        functools.partial(product_kernel, near),
        grid=(bricks // 2,),
        in_specs=[
            pl.BlockSpec((2, channels, slots), lambda b: (b, 0, 0)),
            pl.BlockSpec((2 * slots, width), lambda b: (b, 0)),
        ],
        out_specs=pl.BlockSpec(shape, lambda b: (0,) * len(shape)),
        out_shape=jax.ShapeDtypeStruct(shape, jnp.float32),
        scratch_shapes=[pltpu.VMEM((channels, width), jnp.float32)],
        name="product",
    )(densities, tile)


def from_everyone(x, axis):
    copies = jnp.broadcast_to(x, (lax.axis_size(axis), *x.shape))
    return lax.all_to_all(copies, axis, split_axis=0, concat_axis=0, tiled=True)


REACH = 3
XO, YO = 3, 4
SEND = 5


def lanes(shape):
    return lax.broadcasted_iota(jnp.int32, shape, len(shape) - 1)


def turned(x, shift):
    return pltpu.roll(x, shift % x.shape[-1], x.ndim - 1)


def params(megabytes=24):
    return pltpu.CompilerParams(vmem_limit_bytes=megabytes << 20)


def whole_call(kernel, out_shape, scratch, name, scalars, *operands):
    smem = pl.BlockSpec(memory_space=pltpu.SMEM)
    vmem = pl.BlockSpec(memory_space=pltpu.VMEM)
    return pl.pallas_call(
        kernel,
        in_specs=[smem] * len(scalars) + [vmem] * len(operands),
        out_specs=jax.tree.map(lambda _: vmem, out_shape),
        out_shape=out_shape,
        scratch_shapes=scratch,
        compiler_params=params(),
        name=name,
    )(*scalars, *operands)


def f32(*shape):
    return jax.ShapeDtypeStruct(shape, jnp.float32)


def bf16(*shape):
    return jax.ShapeDtypeStruct(shape, jnp.bfloat16)


def put_planes(up_ref, down_ref, base, field_ref, depth, offset=0):
    size_x, size_y = field_ref.shape[-3], field_ref.shape[-2]
    for e in range(field_ref.shape[0]):
        for i in range(depth):
            rows = pl.ds(base + (e * depth + i) * size_y, size_y)
            high = field_ref[e, size_x - depth + i] + offset
            low = field_ref[e, i] + offset
            up_ref[rows, :] = high.astype(jnp.bfloat16)
            down_ref[rows, :] = low.astype(jnp.bfloat16)
    return base + field_ref.shape[0] * depth * size_y


def planes_kernel(state_ref, source_ref, class_ref, up_ref, down_ref):
    base = put_planes(up_ref, down_ref, 0, state_ref, 3)
    base = put_planes(up_ref, down_ref, base, source_ref, 2)
    put_planes(up_ref, down_ref, base, class_ref, 2, 1.0)


def framed(frame_ref, field_ref, low_ref, high_ref, base, depth, offset=0):
    channels, size_x, size_y = field_ref.shape[:3]
    planes, rows = size_x + 2 * XO, size_y + 2 * YO
    frame_ref[...] = jnp.zeros_like(frame_ref)
    for e in range(channels):
        for x in range(size_x):
            at = (e * planes + XO + x) * rows + YO
            frame_ref[at : at + size_y, :] = field_ref[e, x].astype(jnp.float32) + offset
        for i in range(depth):
            here = pl.ds(base + (e * depth + i) * size_y, size_y)
            at = (e * planes + XO - depth + i) * rows + YO
            frame_ref[at : at + size_y, :] = low_ref[here, :].astype(jnp.float32)
            at = (e * planes + XO + size_x + i) * rows + YO
            frame_ref[at : at + size_y, :] = high_ref[here, :].astype(jnp.float32)
    return base + channels * depth * size_y


def depth_rows(frames, gz, x, size_y, rows, planes, channels):
    lane = lanes((size_y, 128))
    out = jnp.zeros((size_y, 128), jnp.float32)
    for e in range(channels):
        for index, frame_ref in enumerate(frames):
            own = frame_ref.shape[0] == planes * rows
            at = ((0 if own else e) * planes + x) * rows + YO
            start = e * 16 + index * SEND + 1
            moved = turned(frame_ref[at : at + size_y, :], start + 3 - 3 * gz)
            out = jnp.where((lane >= start) & (lane < start + 3), moved, out)
    return out


def frame_kernel(full, place_ref, *refs):
    if full:
        state_ref, source_ref, class_ref, low_ref, high_ref, frame_ref, forcing_ref, code_ref, depth_ref = refs
    else:
        state_ref, low_ref, high_ref, frame_ref, depth_ref = refs
    channels, size_x, size_y = state_ref.shape[:3]
    planes, rows = size_x + 2 * XO, size_y + 2 * YO
    base = framed(frame_ref, state_ref, low_ref, high_ref, 0, 3)
    frames = [frame_ref]
    if full:
        base = framed(forcing_ref, source_ref, low_ref, high_ref, base, 2)
        framed(code_ref, class_ref, low_ref, high_ref, base, 2, 1.0)
        frames = [frame_ref, forcing_ref, code_ref]
    gz = place_ref[1]
    for x in range(planes):
        out = depth_rows(frames, gz, x, size_y, rows, planes, channels)
        depth_ref[x * size_y : (x + 1) * size_y, :] = out.astype(jnp.bfloat16)


def edge_kernel(full, *refs):
    if full:
        frame_ref, forcing_ref, code_ref, other_ref, depth_ref, up_ref, down_ref = refs
    else:
        frame_ref, other_ref, depth_ref, up_ref, down_ref = refs
    rows = SIZE_Y + 2 * YO
    planes = depth_ref.shape[0] // rows
    depth_ref[...] = jnp.zeros_like(depth_ref)
    for x in range(planes):
        here = other_ref[x * SIZE_Y : (x + 1) * SIZE_Y, :].astype(jnp.float32)
        depth_ref[x * rows + YO : x * rows + YO + SIZE_Y, :] = here

    def put(base, ref, depth, step):
        count = ref.shape[0] // rows
        for j in range(depth):
            high = ref[pl.ds(YO + SIZE_Y - depth + j, count, stride=rows), :]
            low = ref[pl.ds(YO + j, count, stride=rows), :]
            up_ref[base + j * step : base + j * step + count, :] = high.astype(jnp.bfloat16)
            down_ref[base + j * step : base + j * step + count, :] = low.astype(jnp.bfloat16)
        return base + depth * step

    if full:
        up_ref[edge_tail(full) :, :] = jnp.zeros((80, 128), jnp.bfloat16)
        down_ref[edge_tail(full) :, :] = jnp.zeros((80, 128), jnp.bfloat16)
    else:
        up_ref[edge_tail(full) :, :] = jnp.zeros((48, 128), jnp.bfloat16)
        down_ref[edge_tail(full) :, :] = jnp.zeros((48, 128), jnp.bfloat16)
    base = put(0, frame_ref, 3, 80)
    if full:
        base = put(base, forcing_ref, 2, 80)
        base = put(base, code_ref, 2, 16)
    put(base, depth_ref, 3, 16)


def edge_tail(full):
    return 400 if full else 240


def take_edges(frame_ref, low_ref, high_ref, base, depth, step):
    rows = SIZE_Y + 2 * YO
    count = frame_ref.shape[0] // rows
    for j in range(depth):
        low = low_ref[base + j * step : base + j * step + count, :].astype(jnp.float32)
        high = high_ref[base + j * step : base + j * step + count, :].astype(jnp.float32)
        frame_ref[pl.ds(YO - depth + j, count, stride=rows), :] = low
        frame_ref[pl.ds(YO + SIZE_Y + j, count, stride=rows), :] = high
    return base + depth * step


def faces(get, e_range, gz, shape):
    lane = lanes(shape)
    out = jnp.zeros(shape, jnp.float32)
    for e in e_range:
        out = jnp.where(lane == e * 16 + 4 * gz, turned(get(e), e * 16 + 1 + 3 * gz), out)
    return out


def sweep(src, dst, zsrc, zdst, forcing, coef, zforcing, zcoef, gz, x_low, x_high, channels, planes, finish=None):
    rows = SIZE_Y + 2 * YO
    shape = (rows, 128)
    lane = lanes(shape)
    keep = 1.0 - relax_weight
    inner_low = (lane > 0).astype(jnp.float32)
    inner_high = (lane < 127).astype(jnp.float32)
    border = (lane == 127 - 127 * gz).astype(jnp.float32)
    face_lane = (lane & 15) == 4 * gz

    def one_plane(x, carry):
        at = pl.multiple_of(x * rows, 8)
        other = zsrc[pl.ds(at, rows), :]
        weight = coef[pl.ds(at, rows), :]
        fresh = []
        for e in range(channels):
            row = pl.multiple_of((e * planes + x) * rows, 8)
            own = src[pl.ds(row, rows), :]
            total = src[pl.ds(row + rows, rows), :] + src[pl.ds(row - rows, rows), :]
            total = total + pltpu.roll(own, rows - 1, 0) + pltpu.roll(own, 1, 0)
            total = total + pltpu.roll(own, 127, 1) * inner_high + pltpu.roll(own, 1, 1) * inner_low
            total = total + turned(other, 126 - gz - 16 * e + 256) * border
            new = keep * own + weight * (forcing[pl.ds(row, rows), :] + total)
            if finish is None:
                dst[pl.ds(row, rows), :] = new
            else:
                finish(e, x, new)
            fresh.append(new)
        if finish is None:
            total = zsrc[pl.ds(at + rows, rows), :] + zsrc[pl.ds(at - rows, rows), :]
            total = total + pltpu.roll(other, rows - 1, 0) + pltpu.roll(other, 1, 0)
            total = total + pltpu.roll(other, 127, 1) + pltpu.roll(other, 1, 1)
            new = keep * other + zcoef[pl.ds(at, rows), :] * (zforcing[pl.ds(at, rows), :] + total)
            face = faces(lambda e: fresh[e], range(channels), gz, shape)
            zdst[pl.ds(at, rows), :] = jnp.where(face_lane, face, new)
        return carry

    lax.fori_loop(x_low, x_high, one_plane, 0)


def sweeps(frame, second, zframe, zsecond, forcing, coef, zforcing, zcoef, gz, out_ref, planes):
    channels = out_ref.shape[0]
    rows = SIZE_Y + 2 * YO
    face_lane = (lanes((rows, 128)) & 15) == 4 * gz
    for x in range(planes):
        face = faces(lambda e: frame[(e * planes + x) * rows : (e * planes + x + 1) * rows, :], range(channels), gz, (rows, 128))
        here = zframe[x * rows : (x + 1) * rows, :]
        zframe[x * rows : (x + 1) * rows, :] = jnp.where(face_lane, face, here)
    sweep(frame, second, zframe, zsecond, forcing, coef, zforcing, zcoef, gz, 1, planes - 1, channels, planes)
    sweep(second, frame, zsecond, zframe, forcing, coef, zforcing, zcoef, gz, 2, planes - 2, channels, planes)

    def finish(e, x, new):
        out_ref[e, x - XO] = new[YO : YO + SIZE_Y, :]

    sweep(frame, None, zframe, None, forcing, coef, zforcing, zcoef, gz, XO, planes - XO, channels, planes, finish)


def put_density(out_ref, density_ref, cell_ref, live):
    channels, size_x, size_y, size_z = out_ref.shape
    slots = cell_ref.shape[1]
    cell = cell_ref[...]
    pick = (lax.broadcasted_iota(jnp.int32, (size_z, slots), 0) == (cell & (size_z - 1))).astype(jnp.bfloat16)
    count = size_x * size_y
    layers = out_ref[...].reshape(channels * count, size_z).astype(jnp.bfloat16)
    lines = jnp.dot(layers, pick, preferred_element_type=jnp.float32)
    used = lanes((count, slots)) < live
    mask = used & (lax.broadcasted_iota(jnp.int32, (count, slots), 0) == (cell >> 7))
    found = [
        jnp.sum(jnp.where(mask, lines[e * count : (e + 1) * count, :], 0.0), axis=0, keepdims=True)
        for e in range(channels)
    ]
    density = jnp.concatenate(found, axis=0).astype(jnp.bfloat16)
    for brick in range(density_ref.shape[0]):
        density_ref[brick] = density


def first_kernel(
    place_ref, coef_table_ref, frame_ref, forcing_ref, code_ref, depth_ref, low_ref, high_ref, cell_ref,
    out_ref, forcing_out, coef_out, zforcing_out, zcoef_out, density_ref, up_ref, down_ref,
    first, second, zfirst, zsecond, code, zcode,
):
    gz = place_ref[1]
    rows = SIZE_Y + 2 * YO
    planes = code_ref.shape[0] // rows
    first[...] = frame_ref[...]
    forcing_out[...] = forcing_ref[...]
    code[...] = code_ref[...]
    zcode[...] = depth_ref[...]
    base = take_edges(first, low_ref, high_ref, 0, 3, 80)
    base = take_edges(forcing_out, low_ref, high_ref, base, 2, 80)
    base = take_edges(code, low_ref, high_ref, base, 2, 16)
    take_edges(zcode, low_ref, high_ref, base, 3, 16)
    lane = lanes((rows, 128)) & 15
    outer = (lane >= 1) & (lane <= 3)
    for x in range(planes):
        here = pl.ds(x * rows, rows)
        packed = zcode[here, :]
        zfirst[here, :] = jnp.where(outer, packed, 0.0)
        zforcing_out[here, :] = jnp.where(outer, turned(packed, 128 - SEND), 0.0)
        level = jnp.where(outer, turned(packed, 128 - 2 * SEND), 0.0)
        own_level = code[here, :]
        zweight = jnp.zeros((rows, 128), jnp.float32)
        weight = jnp.zeros((rows, 128), jnp.float32)
        for index in range(coef_table_ref.shape[0]):
            value = coef_table_ref[index]
            zweight = jnp.where(level == index + 1.0, value, zweight)
            weight = jnp.where(own_level == index + 1.0, value, weight)
        zcoef_out[here, :] = zweight
        coef_out[here, :] = weight
    sweeps(first, second, zfirst, zsecond, forcing_out, coef_out, zforcing_out, zcoef_out, gz, out_ref, planes)
    put_density(out_ref, density_ref, cell_ref, place_ref[2])
    put_planes(up_ref, down_ref, 0, out_ref, 3)


def split(x):
    high = x.astype(jnp.bfloat16)
    return high, (x - high.astype(jnp.float32)).astype(jnp.bfloat16)


def across(a, b):
    return lax.dot_general(a, b, (((1,), (1,)), ((), ())), preferred_element_type=jnp.float32)


def add_load(forcing, zforcing, near_ref, side, gz, channels, planes):
    rows = SIZE_Y + 2 * YO
    size_x = planes - 2 * XO
    cells = near_ref[6].astype(jnp.int32)
    slots = cells.shape[1]
    wide = 3 * slots

    def row_of(first):
        cell = jnp.concatenate([cells[first + n : first + n + 1, :] for n in range(3)], axis=1)
        shift = jnp.concatenate([jnp.full((1, slots), YO + SIZE_Y * (n - 1), jnp.int32) for n in range(3)], axis=1)
        value = coupling * jnp.concatenate([near_ref[first + n] for n in range(3)], axis=1)
        return cell & 127, ((cell >> 7) & (SIZE_Y - 1)) + shift, cell >> 11, value

    span = {-1: range(size_x - 2, size_x), 0: range(size_x), 1: range(2)}[side]
    level = lax.broadcasted_iota(jnp.int32, (rows, wide), 0)
    z, y, x, value = row_of(0)
    pick = (lax.broadcasted_iota(jnp.int32, (128, wide), 0) == z).astype(jnp.bfloat16)
    for plane in span:
        mask = (level == y) & (x == plane)
        spread = jnp.concatenate([jnp.where(mask, value[e : e + 1, :], 0.0) for e in range(channels)], axis=0)
        high, low = split(spread)
        load = across(high, pick) + across(low, pick)
        at = plane + XO + size_x * side
        for e in range(channels):
            row = (e * planes + at) * rows
            forcing[row : row + rows, :] += load[e * rows : (e + 1) * rows, :]
    z, y, x, value = row_of(3)
    lane = z - 125 * gz + 1
    step = lax.broadcasted_iota(jnp.int32, (16, wide), 0)
    ok = (step == lane) & (step >= 1) & (step <= 3)
    spread = jnp.concatenate([jnp.where(ok, value[e : e + 1, :], 0.0) for e in range(channels)], axis=0)
    high, low = split(spread)
    for plane in span:
        mask = ((level == y) & (x == plane)).astype(jnp.bfloat16)
        row = (plane + XO + size_x * side) * rows
        zforcing[row : row + rows, :] += across(mask, high) + across(mask, low)


def second_kernel(
    place_ref, frame_ref, forcing_ref, coef_ref, zforcing_ref, zcoef_ref, depth_ref, low_ref, high_ref, cell_ref,
    near_low, near_own, near_high, out_ref, density_ref, first, second, zfirst, zsecond, forcing, zforcing,
):
    gz = place_ref[1]
    rows = SIZE_Y + 2 * YO
    planes = coef_ref.shape[0] // rows
    channels = out_ref.shape[0]
    first[...] = frame_ref[...]
    zfirst[...] = depth_ref[...]
    forcing[...] = forcing_ref[...]
    zforcing[...] = zforcing_ref[...]
    base = take_edges(first, low_ref, high_ref, 0, 3, 80)
    take_edges(zfirst, low_ref, high_ref, base, 3, 16)
    for side, near in ((-1, near_low), (0, near_own), (1, near_high)):
        add_load(forcing, zforcing, near, side, gz, channels, planes)
    sweeps(first, second, zfirst, zsecond, forcing, coef_ref, zforcing, zcoef_ref, gz, out_ref, planes)
    put_density(out_ref, density_ref, cell_ref, place_ref[2])


def near_kernel(place_ref, parts_ref, targets_ref, near_ref, own_ref):
    col, gz = place_ref[0], place_ref[1]
    cols = targets_ref.shape[0] // 2
    slots = targets_ref.shape[2]
    lane = lanes((8, slots))
    near_ref[6] = jnp.zeros((8, slots), jnp.float32)
    for n in range(6):
        side = jnp.clip(col + n % 3 - 1, 0, cols - 1)
        half = gz if n < 3 else 1 - gz
        about = targets_ref[side * 2 + half]
        total = parts_ref[0, n]
        for sender in range(1, parts_ref.shape[0]):
            total = total + parts_ref[sender, n]
        total = jnp.where(lane < about[4:5, :].astype(jnp.int32), total, 0.0)
        near_ref[n] = total
        near_ref[6, n : n + 1, :] = about[5:6, :]
        if n == 1:
            own_ref[...] = total


def last_kernel(place_ref, parts_ref, own_ref):
    total = parts_ref[0]
    for sender in range(1, parts_ref.shape[0]):
        total = total + parts_ref[sender]
    own_ref[...] = jnp.where(lanes(total.shape) < place_ref[2], total, 0.0)


def both_ways(up, down, axis):
    devices = lax.axis_size(axis)
    pairs = [(i, i + 1) for i in range(devices - 1)]
    return lax.ppermute(up, axis, pairs), lax.ppermute(down, axis, [(b, a) for a, b in pairs])


def local(
    initial_field, source_term, cell_class, class_shift, surface_cell, live_count, panel_geometry
):
    channels, size_x, size_y, size_z = initial_field.shape
    slots = surface_cell.shape[0]
    bricks = lax.axis_size("row")
    panels = slots * lax.axis_size("row") * lax.axis_size("col") * lax.axis_size("gz")
    factor = 1.0 / math.sqrt(panels)
    planes, rows = size_x + 2 * XO, size_y + 2 * YO
    frame, flat = (channels * planes * rows, 128), (planes * rows, 128)
    place = jnp.stack([lax.axis_index("col"), lax.axis_index("gz"), live_count[0]]).astype(jnp.int32)
    coefs = relax_weight / (6.0 + class_shift)
    classes = cell_class[None]
    cells = surface_cell[None]

    send_x = channels * 5 * size_y + 2 * size_y
    up, down = whole_call(
        planes_kernel, (bf16(send_x, 128), bf16(send_x, 128)), [], "planes", (),
        initial_field, source_term, classes,
    )
    low, high = both_ways(up, down, "row")
    start, forcing, code, depth = whole_call(
        functools.partial(frame_kernel, True),
        (f32(*frame), f32(*frame), f32(*flat), bf16(planes * size_y, 128)), [], "frame", (place,),
        initial_field, source_term, classes, low, high,
    )
    other = lax.ppermute(depth, "gz", [(0, 1), (1, 0)])

    live_row = jnp.broadcast_to(live_count.astype(jnp.float32)[:, None], (1, slots))
    message = jnp.concatenate(
        [panel_geometry[:3] * TURNS, panel_geometry[3:] * (factor * TURNS), live_row,
         cells.astype(jnp.float32), jnp.zeros((2, slots), jnp.float32)]
    )
    sources = from_everyone(message, "row")
    targets = from_everyone(message, ("col", "gz"))
    tile = make_tile(sources, targets)

    zframe, up, down = whole_call(
        functools.partial(edge_kernel, True), (f32(*flat), bf16(480, 128), bf16(480, 128)), [], "edges", (),
        start, forcing, code, other,
    )
    low, high = both_ways(up, down, "col")
    vm = lambda shape: pltpu.VMEM(shape, jnp.float32)
    state, forcing, coef, zforcing, zcoef, density, up, down = whole_call(
        first_kernel,
        (f32(*initial_field.shape), f32(*frame), f32(*flat), f32(*flat), f32(*flat), bf16(bricks, channels, slots),
         bf16(channels * 3 * size_y, 128), bf16(channels * 3 * size_y, 128)),
        [vm(frame), vm(frame), vm(flat), vm(flat), vm(flat), vm(flat)], "first", (place, coefs),
        start, forcing, code, zframe, low, high, cells,
    )
    densities = lax.all_to_all(density, "row", 0, 0, tiled=True)
    shares = products(densities, tile, True)
    parts = lax.all_to_all(shares, ("col", "gz"), 0, 0, tiled=True)
    near, _ = whole_call(near_kernel, (f32(7, channels, slots), f32(channels, slots)), [], "near", (place,), parts, targets)
    near_low, near_high = both_ways(near, near, "row")

    low, high = both_ways(up, down, "row")
    start, depth = whole_call(
        functools.partial(frame_kernel, False), (f32(*frame), bf16(planes * size_y, 128)), [], "frame", (place,),
        state, low, high,
    )
    other = lax.ppermute(depth, "gz", [(0, 1), (1, 0)])
    zframe, up, down = whole_call(
        functools.partial(edge_kernel, False), (f32(*flat), bf16(288, 128), bf16(288, 128)), [], "edges", (),
        start, other,
    )
    low, high = both_ways(up, down, "col")
    state, density = whole_call(
        second_kernel, (f32(*initial_field.shape), bf16(bricks, channels, slots)),
        [vm(frame), vm(frame), vm(flat), vm(flat), vm(frame), vm(flat)], "second", (place,),
        start, forcing, coef, zforcing, zcoef, zframe, low, high, cells, near_low, near, near_high,
    )
    densities = lax.all_to_all(density, "row", 0, 0, tiled=True)
    shares = products(densities, tile, False)
    parts = lax.all_to_all(shares, ("col", "gz"), 0, 0, tiled=True)
    potential = whole_call(last_kernel, f32(channels, slots), [], "last", (place,), parts)
    return (state, potential)


def solution(mesh):
    placed = (
        P(None, "row", "col", "gz"),
        P(None, "row", "col", "gz"),
        P("row", "col", "gz"),
        P(),
        P(("row", "col", "gz")),
        P(("row", "col", "gz")),
        P(None, ("row", "col", "gz")),
    )
    return jax.shard_map(
        local,
        mesh=mesh,
        in_specs=placed,
        out_specs=(P(None, "row", "col", "gz"), P(None, ("row", "col", "gz"))),
        check_vma=False,
    )
```

```python
import functools
import math

import jax
import jax.numpy as jnp
from jax import lax
from jax.experimental import pallas as pl
from jax.experimental.pallas import tpu as pltpu
from jax.sharding import PartitionSpec as P

SIZE_Y = 16
ROOM = 8

relax_weight = 0.8
wave_number = 25.0
soften = 0.05
coupling = 0.5

SINE = (6.2831851600894435, -41.34165503141112, 81.60100407296788, -76.54978228730859, 39.53670602126459)
TURNS = wave_number / (2.0 * math.pi)
ROUNDER = 12582912.0


def from_everyone(x, axis):
    copies = jnp.broadcast_to(x, (lax.axis_size(axis), *x.shape))
    return lax.all_to_all(copies, axis, split_axis=0, concat_axis=0, tiled=True)


REACH = 3
XO, YO = 3, 4
SEND = 5


def lanes(shape):
    return lax.broadcasted_iota(jnp.int32, shape, len(shape) - 1)


def turned(x, shift):
    return pltpu.roll(x, shift % x.shape[-1], x.ndim - 1)


def params(megabytes):
    return pltpu.CompilerParams(vmem_limit_bytes=megabytes << 20)


def whole_call(kernel, out_shape, scratch, name, scalars, *operands, megabytes=4, away=(), aliases={}):
    smem = pl.BlockSpec(memory_space=pltpu.SMEM)
    vmem = pl.BlockSpec(memory_space=pltpu.VMEM)
    far = pl.BlockSpec(memory_space=pltpu.HBM)
    return pl.pallas_call(
        kernel,
        in_specs=[smem] * len(scalars) + [far if n in away else vmem for n in range(len(operands))],
        out_specs=jax.tree.map(lambda _: vmem, out_shape),
        out_shape=out_shape,
        scratch_shapes=scratch,
        compiler_params=params(megabytes),
        input_output_aliases={len(scalars) + k: v for k, v in aliases.items()},
        name=name,
    )(*scalars, *operands)


def f32(*shape):
    return jax.ShapeDtypeStruct(shape, jnp.float32)


def bf16(*shape):
    return jax.ShapeDtypeStruct(shape, jnp.bfloat16)


def split(x):
    high = x.astype(jnp.bfloat16)
    return high, (x - high.astype(jnp.float32)).astype(jnp.bfloat16)


def across(a, b):
    return lax.dot_general(a, b, (((1,), (1,)), ((), ())), preferred_element_type=jnp.float32)


def compact_kernel(message_ref, target_ref, source_out, target_out, table_ref, counts, table, arrived):
    bricks, depth, slots = message_ref.shape
    channels = depth // 2
    lane = lanes((8, slots))
    first = jnp.zeros((8, slots), jnp.float32)
    for brick in range(bricks):
        first = jnp.where(lane == brick, message_ref[brick, channels + 4 : channels + 5, :], first)
        first = jnp.where(lane == bricks + brick, target_ref[brick, 4:5, :], first)
    counts[...] = first.astype(jnp.int32)
    copy = pltpu.make_async_copy(counts, table, arrived)
    copy.start()
    source_out[...] = jnp.zeros_like(source_out)
    target_out[...] = jnp.zeros_like(target_out)
    copy.wait()
    begin = [jnp.int32(0), jnp.int32(0)]
    for brick in range(bricks):
        for which, ref, out in ((0, message_ref, source_out), (1, target_ref, target_out)):
            count = table[0, which * bricks + brick]
            append(out, ref[brick], begin[which], count)
            table_ref[which, brick] = begin[which]
            begin[which] = begin[which] + count
    table_ref[0, bricks] = begin[0]
    table_ref[1, bricks] = begin[1]


def append(out, rows, begin, count):
    group, shift = begin >> 7, begin & 127
    lane = lanes(rows.shape)
    moved = pltpu.roll(rows, shift, 1)
    out[group] = jnp.where((lane >= shift) & (lane < shift + count), moved, out[group])
    out[group + 1] = jnp.where(lane < shift + count - rows.shape[1], moved, out[group + 1])


def tile_kernel(half, table_ref, source_ref, target_ref, *refs):
    tile_ref, share_ref, columns, density = refs[-4:]
    bricks, slots = source_ref.shape[0] - 1, source_ref.shape[2]
    channels = share_ref.shape[1]
    step = pl.program_id(0)
    pairs = (table_ref[0, bricks] + (2 * slots - 1)) >> 8

    @pl.when(step == 0)
    def _():
        for group in range(bricks):
            density[:, group * slots : (group + 1) * slots] = source_ref[group, :channels].astype(jnp.bfloat16)

    @pl.when((2 * step + half) * slots < table_ref[1, bricks])
    def _():
        columns[...] = jnp.transpose(target_ref[0])
        spread = [jnp.broadcast_to(columns[:, d : d + 1], (slots, slots)) for d in range(3)]

        def one_pair(pair, total):
            both = []
            for index in range(2):
                here = source_ref.at[2 * pair + index]
                square = 1e-30
                for d in range(3):
                    delta = spread[d] - here[channels + d : channels + d + 1, :]
                    square = square + delta * delta
                turns = square * lax.rsqrt(square)
                whole = (turns + ROUNDER) - ROUNDER
                angle = 0.25 - jnp.abs(turns - whole)
                angle2 = angle * angle
                wave = SINE[4]
                for c in SINE[3::-1]:
                    wave = wave * angle2 + c
                weight = here[channels + 3 : channels + 4, :]
                value = (angle * weight) * wave / (turns + soften * TURNS)
                both.append(value.astype(jnp.bfloat16))
            values = jnp.concatenate(both, axis=1)
            at = pl.ds(pl.multiple_of(pair * 2 * slots, 2 * slots), 2 * slots)
            tile_ref[:, at] = values
            return total + across(density[:, at], values)

        share_ref[0] = lax.fori_loop(0, pairs, one_pair, jnp.zeros((channels, slots), jnp.float32))

        def clear(pair, carry):
            at = pl.ds(pl.multiple_of(pair * 2 * slots, 2 * slots), 2 * slots)
            tile_ref[:, at] = jnp.zeros((slots, 2 * slots), jnp.bfloat16)
            return carry

        lax.fori_loop(pairs, bricks // 2, clear, 0)


def make_tile(half, table, sources, targets, channels, before=()):
    bricks, slots = sources.shape[0] - 1, sources.shape[2]
    far = pl.BlockSpec(memory_space=pl.ANY)
    return pl.pallas_call(
        functools.partial(tile_kernel, half),
        grid=(bricks // 2,),
        in_specs=[
            pl.BlockSpec(memory_space=pltpu.SMEM),
            pl.BlockSpec(sources.shape, lambda b: (0, 0, 0)),
            pl.BlockSpec((1, targets.shape[1], slots), lambda b: (2 * b + half, 0, 0)),
        ]
        + [far] * len(before),
        out_specs=[
            pl.BlockSpec((slots, bricks * slots), lambda b: (2 * b + half, 0)),
            pl.BlockSpec((1, channels, slots), lambda b: (2 * b + half, 0, 0)),
        ],
        out_shape=[
            jax.ShapeDtypeStruct((ROOM * bricks * slots, bricks * slots), jnp.bfloat16),
            jax.ShapeDtypeStruct((bricks, channels, slots), jnp.float32),
        ],
        scratch_shapes=[
            pltpu.VMEM((slots, targets.shape[1]), jnp.float32),
            pltpu.VMEM((channels, bricks * slots), jnp.bfloat16),
        ],
        input_output_aliases={3 + n: n for n in range(len(before))},
        compiler_params=params(8),
        name="tile",
    )(table, sources, targets, *before)


def taken(share_ref, table_ref, brick, bricks):
    begin = table_ref[1, brick]
    count = table_ref[1, brick + 1] - begin
    group, shift = begin >> 7, begin & 127
    lane = lanes(share_ref.shape[1:])
    slots = share_ref.shape[2]
    this = pltpu.roll(share_ref[group], (slots - shift) & 127, 1)
    following = pltpu.roll(share_ref[jnp.minimum(group + 1, bricks - 1)], (slots - shift) & 127, 1)
    return jnp.where(lane < count, jnp.where(lane < slots - shift, this, following), 0.0)


def arrange_kernel(table_ref, share_ref, out_ref):
    bricks = out_ref.shape[0]
    for index in range(bricks):
        value = taken(share_ref, table_ref, index, bricks)
        for n in range(6):
            side, other = index // 2 - (n % 3 - 1), (index + n // 3) % 2
            if 0 <= side < bricks // 2:
                out_ref[side * 2 + other, n] = value
    for brick in range(bricks):
        for n in range(6):
            if not 0 <= brick // 2 + n % 3 - 1 < bricks // 2:
                out_ref[brick, n] = jnp.zeros(out_ref.shape[2:], jnp.float32)


def product_kernel(table_ref, density_ref, tile_ref, out_ref, sources, density, shares):
    bricks, channels, slots = density_ref.shape
    step = pl.program_id(0)
    count = tile_ref.shape[0] // slots

    @pl.when(step == 0)
    def _():
        sources[...] = jnp.zeros_like(sources)
        for brick in range(bricks):
            begin = table_ref[0, brick]
            append(sources, density_ref[brick].astype(jnp.float32), begin, table_ref[0, brick + 1] - begin)
        for group in range(bricks):
            density[:, group * slots : (group + 1) * slots] = sources[group].astype(jnp.bfloat16)

    @pl.when(step * count * slots < table_ref[1, bricks])
    def _():
        total = across(density[...], tile_ref[...])
        for index in range(count):
            shares[step * count + index] = total[:, index * slots : (index + 1) * slots]

    @pl.when(step == pl.num_programs(0) - 1)
    def _():
        for brick in range(bricks):
            out_ref[brick] = taken(shares, table_ref, brick, bricks)


def products(table, density, tile, rows):
    bricks, channels, slots = density.shape
    width = tile.shape[1]
    steps = bricks * slots // rows

    def block(b, table_ref):
        last = (table_ref[1, bricks] + rows - 1) // rows - 1
        return jnp.minimum(b, last), 0

    return pl.pallas_call(
        product_kernel,
        grid_spec=pltpu.PrefetchScalarGridSpec(
            num_scalar_prefetch=1,
            grid=(steps,),
            in_specs=[pl.BlockSpec(density.shape, lambda b, t: (0, 0, 0)), pl.BlockSpec((rows, width), block)],
            out_specs=pl.BlockSpec((bricks, channels, slots), lambda b, t: (0, 0, 0)),
            scratch_shapes=[
                pltpu.VMEM((bricks + 1, channels, slots), jnp.float32),
                pltpu.VMEM((channels, width), jnp.bfloat16),
                pltpu.VMEM((bricks, channels, slots), jnp.float32),
            ],
        ),
        out_shape=jax.ShapeDtypeStruct((bricks, channels, slots), jnp.float32),
        compiler_params=params(12),
        name="product",
    )(table, density, tile)


def put_planes(up_ref, down_ref, base, field_ref, depth, offset=0):
    size_x, size_y = field_ref.shape[-3], field_ref.shape[-2]
    for e in range(field_ref.shape[0]):
        for i in range(depth):
            rows = pl.ds(base + (e * depth + i) * size_y, size_y)
            high = field_ref[e, size_x - depth + i] + offset
            low = field_ref[e, i] + offset
            up_ref[rows, :] = high.astype(jnp.bfloat16)
            down_ref[rows, :] = low.astype(jnp.bfloat16)
    return base + field_ref.shape[0] * depth * size_y


def own_cells(frame_ref, field_ref, offset=0):
    channels, size_x, size_y = field_ref.shape[:3]
    planes, rows = size_x + 2 * XO, size_y + 2 * YO
    frame_ref[...] = jnp.zeros_like(frame_ref)
    for e in range(channels):
        for x in range(size_x):
            at = (e * planes + XO + x) * rows + YO
            frame_ref[at : at + size_y, :] = field_ref[e, x].astype(jnp.float32) + offset


def planes_kernel(
    factor, live_ref, state_hbm, source_hbm, class_hbm, geometry_ref, cell_ref,
    up_ref, down_ref, frame_ref, forcing_ref, code_ref, message_ref, state_ref, source_ref, class_ref, arrived,
):
    copies = [
        pltpu.make_async_copy(state_hbm, state_ref, arrived.at[0]),
        pltpu.make_async_copy(source_hbm, source_ref, arrived.at[1]),
        pltpu.make_async_copy(class_hbm, class_ref, arrived.at[2]),
    ]
    for copy in copies:
        copy.start()
    slots = cell_ref.shape[1]
    message = jnp.concatenate(
        [
            geometry_ref[:3] * TURNS,
            geometry_ref[3:] * (factor * TURNS),
            jnp.full((1, slots), live_ref[0], jnp.int32).astype(jnp.float32),
            cell_ref[...].astype(jnp.float32),
            jnp.zeros((2, slots), jnp.float32),
        ],
        axis=0,
    )
    for brick in range(message_ref.shape[0]):
        message_ref[brick] = message
    for copy in copies:
        copy.wait()
    base = put_planes(up_ref, down_ref, 0, state_ref, 3)
    base = put_planes(up_ref, down_ref, base, source_ref, 2)
    put_planes(up_ref, down_ref, base, class_ref, 2, 1.0)
    own_cells(frame_ref, state_ref)
    own_cells(forcing_ref, source_ref)
    own_cells(code_ref, class_ref, 1.0)


def beside(frame_ref, channels, low_ref, high_ref, base, depth):
    rows = SIZE_Y + 2 * YO
    planes = frame_ref.shape[0] // (channels * rows)
    size_x = planes - 2 * XO
    for e in range(channels):
        for i in range(depth):
            here = pl.ds(base + (e * depth + i) * SIZE_Y, SIZE_Y)
            at = (e * planes + XO - depth + i) * rows + YO
            frame_ref[at : at + SIZE_Y, :] = low_ref[here, :].astype(jnp.float32)
            at = (e * planes + XO + size_x + i) * rows + YO
            frame_ref[at : at + SIZE_Y, :] = high_ref[here, :].astype(jnp.float32)
    return base + channels * depth * SIZE_Y


def depth_rows(frames, gz, x, size_y, rows, planes, channels):
    lane = lanes((size_y, 128))
    out = jnp.zeros((size_y, 128), jnp.float32)
    for e in range(channels):
        for index, frame_ref in enumerate(frames):
            own = frame_ref.shape[0] == planes * rows
            at = ((0 if own else e) * planes + x) * rows + YO
            start = e * 16 + index * SEND + 1
            moved = turned(frame_ref[at : at + size_y, :], start + 3 - 3 * gz)
            out = jnp.where((lane >= start) & (lane < start + 3), moved, out)
    return out


def frame_kernel(full, channels, place_ref, *refs):
    if full:
        _, _, _, low_ref, high_ref, frame_ref, forcing_ref, code_ref, depth_ref = refs
    else:
        state_ref, low_ref, high_ref, frame_ref, depth_ref = refs
        own_cells(frame_ref, state_ref)
    rows = SIZE_Y + 2 * YO
    planes = frame_ref.shape[0] // (channels * rows)
    base = beside(frame_ref, channels, low_ref, high_ref, 0, 3)
    frames = [frame_ref]
    if full:
        base = beside(forcing_ref, channels, low_ref, high_ref, base, 2)
        beside(code_ref, 1, low_ref, high_ref, base, 2)
        frames = [frame_ref, forcing_ref, code_ref]
    gz = place_ref[1]
    for x in range(planes):
        out = depth_rows(frames, gz, x, SIZE_Y, rows, planes, channels)
        depth_ref[x * SIZE_Y : (x + 1) * SIZE_Y, :] = out.astype(jnp.bfloat16)


def edge_kernel(full, *refs):
    if full:
        frame_ref, forcing_ref, code_ref, other_ref, depth_ref, up_ref, down_ref = refs
    else:
        frame_ref, other_ref, depth_ref, up_ref, down_ref = refs
    rows = SIZE_Y + 2 * YO
    planes = depth_ref.shape[0] // rows
    depth_ref[...] = jnp.zeros_like(depth_ref)
    for x in range(planes):
        here = other_ref[x * SIZE_Y : (x + 1) * SIZE_Y, :].astype(jnp.float32)
        depth_ref[x * rows + YO : x * rows + YO + SIZE_Y, :] = here

    def put(base, ref, depth, step):
        count = ref.shape[0] // rows
        for j in range(depth):
            high = ref[pl.ds(YO + SIZE_Y - depth + j, count, stride=rows), :]
            low = ref[pl.ds(YO + j, count, stride=rows), :]
            up_ref[base + j * step : base + j * step + count, :] = high.astype(jnp.bfloat16)
            down_ref[base + j * step : base + j * step + count, :] = low.astype(jnp.bfloat16)
        return base + depth * step

    if full:
        up_ref[edge_tail(full) :, :] = jnp.zeros((80, 128), jnp.bfloat16)
        down_ref[edge_tail(full) :, :] = jnp.zeros((80, 128), jnp.bfloat16)
    else:
        up_ref[edge_tail(full) :, :] = jnp.zeros((48, 128), jnp.bfloat16)
        down_ref[edge_tail(full) :, :] = jnp.zeros((48, 128), jnp.bfloat16)
    base = put(0, frame_ref, 3, 80)
    if full:
        base = put(base, forcing_ref, 2, 80)
        base = put(base, code_ref, 2, 16)
    put(base, depth_ref, 3, 16)


def edge_tail(full):
    return 400 if full else 240


def take_edges(frame_ref, low_ref, high_ref, base, depth, step):
    rows = SIZE_Y + 2 * YO
    count = frame_ref.shape[0] // rows
    for j in range(depth):
        low = low_ref[base + j * step : base + j * step + count, :].astype(jnp.float32)
        high = high_ref[base + j * step : base + j * step + count, :].astype(jnp.float32)
        frame_ref[pl.ds(YO - depth + j, count, stride=rows), :] = low
        frame_ref[pl.ds(YO + SIZE_Y + j, count, stride=rows), :] = high
    return base + depth * step


def faces(get, e_range, gz, shape):
    lane = lanes(shape)
    out = jnp.zeros(shape, jnp.float32)
    for e in e_range:
        out = jnp.where(lane == e * 16 + 4 * gz, turned(get(e), e * 16 + 1 + 3 * gz), out)
    return out


def sweep(src, dst, zsrc, zdst, forcing, coef, zforcing, zcoef, gz, x_low, x_high, channels, planes, finish=None):
    rows = SIZE_Y + 2 * YO
    shape = (rows, 128)
    lane = lanes(shape)
    keep = 1.0 - relax_weight
    inner_low = (lane > 0).astype(jnp.float32)
    inner_high = (lane < 127).astype(jnp.float32)
    border = (lane == 127 - 127 * gz).astype(jnp.float32)
    face_lane = (lane & 15) == 4 * gz

    def one_plane(x, carry):
        at = pl.multiple_of(x * rows, 8)
        other = zsrc[pl.ds(at, rows), :]
        weight = coef[pl.ds(at, rows), :]
        fresh = []
        for e in range(channels):
            row = pl.multiple_of((e * planes + x) * rows, 8)
            own = src[pl.ds(row, rows), :]
            total = src[pl.ds(row + rows, rows), :] + src[pl.ds(row - rows, rows), :]
            total = total + pltpu.roll(own, rows - 1, 0) + pltpu.roll(own, 1, 0)
            total = total + pltpu.roll(own, 127, 1) * inner_high + pltpu.roll(own, 1, 1) * inner_low
            total = total + turned(other, 126 - gz - 16 * e + 256) * border
            new = keep * own + weight * (forcing[pl.ds(row, rows), :] + total)
            if finish is None:
                dst[pl.ds(row, rows), :] = new
            else:
                finish(e, x, new)
            fresh.append(new)
        if finish is None:
            total = zsrc[pl.ds(at + rows, rows), :] + zsrc[pl.ds(at - rows, rows), :]
            total = total + pltpu.roll(other, rows - 1, 0) + pltpu.roll(other, 1, 0)
            total = total + pltpu.roll(other, 127, 1) + pltpu.roll(other, 1, 1)
            new = keep * other + zcoef[pl.ds(at, rows), :] * (zforcing[pl.ds(at, rows), :] + total)
            face = faces(lambda e: fresh[e], range(channels), gz, shape)
            zdst[pl.ds(at, rows), :] = jnp.where(face_lane, face, new)
        return carry

    lax.fori_loop(x_low, x_high, one_plane, 0)


def sweeps(frame, second, zframe, zsecond, forcing, coef, zforcing, zcoef, gz, out_ref, planes):
    channels = out_ref.shape[0]
    rows = SIZE_Y + 2 * YO
    face_lane = (lanes((rows, 128)) & 15) == 4 * gz
    for x in range(planes):
        face = faces(lambda e: frame[(e * planes + x) * rows : (e * planes + x + 1) * rows, :], range(channels), gz, (rows, 128))
        here = zframe[x * rows : (x + 1) * rows, :]
        zframe[x * rows : (x + 1) * rows, :] = jnp.where(face_lane, face, here)
    sweep(frame, second, zframe, zsecond, forcing, coef, zforcing, zcoef, gz, 1, planes - 1, channels, planes)
    sweep(second, frame, zsecond, zframe, forcing, coef, zforcing, zcoef, gz, 2, planes - 2, channels, planes)

    def finish(e, x, new):
        out_ref[e, x - XO] = new[YO : YO + SIZE_Y, :]

    sweep(frame, None, zframe, None, forcing, coef, zforcing, zcoef, gz, XO, planes - XO, channels, planes, finish)


def put_density(out_ref, density_ref, cell_ref, live, message_ref=None):
    channels, size_x, size_y, size_z = out_ref.shape
    slots = cell_ref.shape[1]
    cell = cell_ref[...]
    pick = (lax.broadcasted_iota(jnp.int32, (size_z, slots), 0) == (cell & (size_z - 1))).astype(jnp.bfloat16)
    count = size_x * size_y
    layers = out_ref[...].reshape(channels * count, size_z).astype(jnp.bfloat16)
    lines = jnp.dot(layers, pick, preferred_element_type=jnp.float32)
    used = lanes((count, slots)) < live
    mask = used & (lax.broadcasted_iota(jnp.int32, (count, slots), 0) == (cell >> 7))
    found = [
        jnp.sum(jnp.where(mask, lines[e * count : (e + 1) * count, :], 0.0), axis=0, keepdims=True)
        for e in range(channels)
    ]
    density = jnp.concatenate(found, axis=0).astype(jnp.bfloat16)
    if message_ref is None:
        for brick in range(density_ref.shape[0]):
            density_ref[brick] = density
    else:
        message = jnp.concatenate([density.astype(jnp.float32), message_ref[0]], axis=0)
        for brick in range(density_ref.shape[0]):
            density_ref[brick] = message


def first_kernel(
    place_ref, shift_ref, frame_ref, forcing_ref, code_ref, depth_ref, low_ref, high_ref, cell_ref, message_ref,
    out_ref, forcing_out, coef_out, zforcing_out, zcoef_out, density_ref, up_ref, down_ref,
    first, second, zfirst, zsecond, code, zcode,
):
    gz = place_ref[1]
    rows = SIZE_Y + 2 * YO
    planes = code_ref.shape[0] // rows
    first[...] = frame_ref[...]
    forcing_out[...] = forcing_ref[...]
    code[...] = code_ref[...]
    zcode[...] = depth_ref[...]
    base = take_edges(first, low_ref, high_ref, 0, 3, 80)
    base = take_edges(forcing_out, low_ref, high_ref, base, 2, 80)
    base = take_edges(code, low_ref, high_ref, base, 2, 16)
    take_edges(zcode, low_ref, high_ref, base, 3, 16)
    lane = lanes((rows, 128)) & 15
    outer = (lane >= 1) & (lane <= 3)
    for x in range(planes):
        here = pl.ds(x * rows, rows)
        packed = zcode[here, :]
        zfirst[here, :] = jnp.where(outer, packed, 0.0)
        zforcing_out[here, :] = jnp.where(outer, turned(packed, 128 - SEND), 0.0)
        level = jnp.where(outer, turned(packed, 128 - 2 * SEND), 0.0)
        own_level = code[here, :]
        zweight = jnp.zeros((rows, 128), jnp.float32)
        weight = jnp.zeros((rows, 128), jnp.float32)
        for index in range(shift_ref.shape[0]):
            value = shift_ref[index]
            zweight = jnp.where(level == index + 1.0, value, zweight)
            weight = jnp.where(own_level == index + 1.0, value, weight)
        zcoef_out[here, :] = jnp.where(level > 0.0, relax_weight / (6.0 + zweight), 0.0)
        coef_out[here, :] = jnp.where(own_level > 0.0, relax_weight / (6.0 + weight), 0.0)
    sweeps(first, second, zfirst, zsecond, forcing_out, coef_out, zforcing_out, zcoef_out, gz, out_ref, planes)
    put_planes(up_ref, down_ref, 0, out_ref, 3)
    put_density(out_ref, density_ref, cell_ref, place_ref[2], message_ref)


def add_load(forcing, zforcing, near_ref, side, gz, channels, planes):
    rows = SIZE_Y + 2 * YO
    size_x = planes - 2 * XO
    cells = near_ref[6].astype(jnp.int32)
    slots = cells.shape[1]
    wide = 3 * slots

    def row_of(first):
        cell = jnp.concatenate([cells[first + n : first + n + 1, :] for n in range(3)], axis=1)
        shift = jnp.concatenate([jnp.full((1, slots), YO + SIZE_Y * (n - 1), jnp.int32) for n in range(3)], axis=1)
        value = coupling * jnp.concatenate([near_ref[first + n] for n in range(3)], axis=1)
        return cell & 127, ((cell >> 7) & (SIZE_Y - 1)) + shift, cell >> 11, value

    span = {-1: range(size_x - 2, size_x), 0: range(size_x), 1: range(2)}[side]
    level = lax.broadcasted_iota(jnp.int32, (rows, wide), 0)
    z, y, x, value = row_of(0)
    pick = (lax.broadcasted_iota(jnp.int32, (128, wide), 0) == z).astype(jnp.bfloat16)
    for plane in span:
        mask = (level == y) & (x == plane)
        spread = jnp.concatenate([jnp.where(mask, value[e : e + 1, :], 0.0) for e in range(channels)], axis=0)
        high, low = split(spread)
        load = across(high, pick) + across(low, pick)
        at = plane + XO + size_x * side
        for e in range(channels):
            row = (e * planes + at) * rows
            forcing[row : row + rows, :] += load[e * rows : (e + 1) * rows, :]
    z, y, x, value = row_of(3)
    lane = z - 125 * gz + 1
    step = lax.broadcasted_iota(jnp.int32, (16, wide), 0)
    ok = (step == lane) & (step >= 1) & (step <= 3)
    spread = jnp.concatenate([jnp.where(ok, value[e : e + 1, :], 0.0) for e in range(channels)], axis=0)
    high, low = split(spread)
    for plane in span:
        mask = ((level == y) & (x == plane)).astype(jnp.bfloat16)
        row = (plane + XO + size_x * side) * rows
        zforcing[row : row + rows, :] += across(mask, high) + across(mask, low)


def second_kernel(
    place_ref, frame_ref, forcing_ref, coef_ref, zforcing_ref, zcoef_ref, depth_ref, low_ref, high_ref, cell_ref,
    near_low, near_own, near_high, out_ref, density_ref, first, second, zfirst, zsecond, forcing, zforcing,
):
    gz = place_ref[1]
    rows = SIZE_Y + 2 * YO
    planes = coef_ref.shape[0] // rows
    channels = out_ref.shape[0]
    first[...] = frame_ref[...]
    zfirst[...] = depth_ref[...]
    forcing[...] = forcing_ref[...]
    zforcing[...] = zforcing_ref[...]
    base = take_edges(first, low_ref, high_ref, 0, 3, 80)
    take_edges(zfirst, low_ref, high_ref, base, 3, 16)
    for side, near in ((-1, near_low), (0, near_own), (1, near_high)):
        add_load(forcing, zforcing, near, side, gz, channels, planes)
    sweeps(first, second, zfirst, zsecond, forcing, coef_ref, zforcing, zcoef_ref, gz, out_ref, planes)
    put_density(out_ref, density_ref, cell_ref, place_ref[2])


def near_kernel(place_ref, parts_ref, targets_ref, near_ref, own_ref):
    col, gz = place_ref[0], place_ref[1]
    cols = targets_ref.shape[0] // 2
    slots = targets_ref.shape[2]
    lane = lanes((8, slots))
    near_ref[6] = jnp.zeros((8, slots), jnp.float32)
    for n in range(6):
        side = jnp.clip(col + n % 3 - 1, 0, cols - 1)
        half = gz if n < 3 else 1 - gz
        about = targets_ref[side * 2 + half]
        total = parts_ref[0, n]
        for sender in range(1, parts_ref.shape[0]):
            total = total + parts_ref[sender, n]
        total = jnp.where(lane < about[4:5, :].astype(jnp.int32), total, 0.0)
        near_ref[n] = total
        near_ref[6, n : n + 1, :] = about[5:6, :]
        if n == 1:
            own_ref[...] = total


def last_kernel(place_ref, parts_ref, own_ref):
    total = parts_ref[0]
    for sender in range(1, parts_ref.shape[0]):
        total = total + parts_ref[sender]
    own_ref[...] = jnp.where(lanes(total.shape) < place_ref[2], total, 0.0)


def both_ways(up, down, axis):
    devices = lax.axis_size(axis)
    pairs = [(i, i + 1) for i in range(devices - 1)]
    return lax.ppermute(up, axis, pairs), lax.ppermute(down, axis, [(b, a) for a, b in pairs])


def local(
    initial_field, source_term, cell_class, class_shift, surface_cell, live_count, panel_geometry
):
    channels, size_x, size_y, size_z = initial_field.shape
    slots = surface_cell.shape[0]
    bricks = lax.axis_size("row")
    panels = slots * lax.axis_size("row") * lax.axis_size("col") * lax.axis_size("gz")
    factor = 1.0 / math.sqrt(panels)
    planes, rows = size_x + 2 * XO, size_y + 2 * YO
    frame, flat = (channels * planes * rows, 128), (planes * rows, 128)
    place = jnp.stack([lax.axis_index("col"), lax.axis_index("gz"), live_count[0]]).astype(jnp.int32)
    cells = surface_cell[None]
    vm = lambda shape, dtype=jnp.float32: pltpu.VMEM(shape, dtype)

    send_x = channels * 5 * size_y + 2 * size_y
    up, down, start, forcing, code, message = whole_call(
        functools.partial(planes_kernel, factor),
        (bf16(send_x, 128), bf16(send_x, 128), f32(*frame), f32(*frame), f32(*flat), f32(bricks, 8, slots)),
        [vm(initial_field.shape), vm(initial_field.shape), vm((1, *cell_class.shape), jnp.int32),
         pltpu.SemaphoreType.DMA((3,))],
        "planes", (live_count,), initial_field, source_term, cell_class[None], panel_geometry, cells,
        away=(0, 1, 2),
    )
    low, high = both_ways(up, down, "row")
    targets = lax.all_to_all(message, ("col", "gz"), 0, 0, tiled=True)
    low, high, targets = lax.optimization_barrier((low, high, targets))
    start, forcing, code, depth = whole_call(
        functools.partial(frame_kernel, True, channels),
        (f32(*frame), f32(*frame), f32(*flat), bf16(planes * size_y, 128)), [], "frame", (place,),
        start, forcing, code, low, high, aliases={0: 0, 1: 1, 2: 2},
    )
    other = lax.ppermute(depth, "gz", [(0, 1), (1, 0)])
    zframe, up, down = whole_call(
        functools.partial(edge_kernel, True), (f32(*flat), bf16(480, 128), bf16(480, 128)), [], "edges", (),
        start, forcing, code, other,
    )
    low, high = both_ways(up, down, "col")
    state, forcing, coef, zforcing, zcoef, density, up, down = whole_call(
        first_kernel,
        (f32(*initial_field.shape), f32(*frame), f32(*flat), f32(*flat), f32(*flat), f32(bricks, 2 * channels, slots),
         bf16(channels * 3 * size_y, 128), bf16(channels * 3 * size_y, 128)),
        [vm(frame), vm(frame), vm(flat), vm(flat), vm(flat), vm(flat)], "first", (place, class_shift),
        start, forcing, code, zframe, low, high, cells, message, megabytes=8,
    )
    low, high = both_ways(up, down, "row")
    densities = lax.all_to_all(density, "row", 0, 0, tiled=True)
    start, depth = whole_call(
        functools.partial(frame_kernel, False, channels), (f32(*frame), bf16(planes * size_y, 128)), [], "frame", (place,),
        state, low, high,
    )
    other = lax.ppermute(depth, "gz", [(0, 1), (1, 0)])
    densities, depth = lax.optimization_barrier((densities, depth))
    smem = pl.BlockSpec(memory_space=pltpu.SMEM)
    vmem = pl.BlockSpec(memory_space=pltpu.VMEM)
    packed, aims, table = pl.pallas_call(
        compact_kernel,
        in_specs=[vmem, vmem],
        out_specs=(vmem, vmem, smem),
        out_shape=(f32(bricks + 1, 2 * channels, slots), f32(bricks + 1, 8, slots),
                   jax.ShapeDtypeStruct((2, bricks + 1), jnp.int32)),
        scratch_shapes=[vm((8, slots), jnp.int32), pltpu.SMEM((8, slots), jnp.int32), pltpu.SemaphoreType.DMA],
        compiler_params=params(4),
        name="compact",
    )(densities, targets)
    tile, shares = make_tile(0, table, packed, aims, channels)
    other, shares = lax.optimization_barrier((other, shares))
    zframe, up, down = whole_call(
        functools.partial(edge_kernel, False), (f32(*flat), bf16(288, 128), bf16(288, 128)), [], "edges", (),
        start, other,
    )
    low, high = both_ways(up, down, "col")
    packed, up = lax.optimization_barrier((packed, up))
    tile, shares = make_tile(1, table, packed, aims, channels, (tile, shares))
    shares = whole_call(arrange_kernel, f32(bricks, 6, channels, slots), [], "arrange", (table,), shares)
    parts = lax.all_to_all(shares, ("col", "gz"), 0, 0, tiled=True)
    near, _ = whole_call(near_kernel, (f32(7, channels, slots), f32(channels, slots)), [], "near", (place,), parts, targets)
    near_low, near_high = both_ways(near, near, "row")
    state, density = whole_call(
        second_kernel, (f32(*initial_field.shape), bf16(bricks, channels, slots)),
        [vm(frame), vm(frame), vm(flat), vm(flat), vm(frame), vm(flat)], "second", (place,),
        start, forcing, coef, zforcing, zcoef, zframe, low, high, cells, near_low, near, near_high, megabytes=8,
    )
    densities = lax.all_to_all(density, "row", 0, 0, tiled=True)
    shares = products(table, densities, tile, 512)
    parts = lax.all_to_all(shares, ("col", "gz"), 0, 0, tiled=True)
    potential = whole_call(last_kernel, f32(channels, slots), [], "last", (place,), parts)
    return (state, potential)


def solution(mesh):
    placed = (
        P(None, "row", "col", "gz"),
        P(None, "row", "col", "gz"),
        P("row", "col", "gz"),
        P(),
        P(("row", "col", "gz")),
        P(("row", "col", "gz")),
        P(None, ("row", "col", "gz")),
    )
    return jax.shard_map(
        local,
        mesh=mesh,
        in_specs=placed,
        out_specs=(P(None, "row", "col", "gz"), P(None, ("row", "col", "gz"))),
        check_vma=False,
    )
```

```python
import functools
import math

import jax
import jax.numpy as jnp
from jax import lax
from jax.experimental import pallas as pl
from jax.experimental.pallas import tpu as pltpu
from jax.sharding import PartitionSpec as P

SIZE_Y = 16
CLASSES = 16
KEPT = 11
ROOM = 8

relax_weight = 0.8
wave_number = 25.0
soften = 0.05
coupling = 0.5

SINE = (6.283164044297846, -41.33714237050646, 81.34076886863805, -70.99343309793157)
TURNS = wave_number / (2.0 * math.pi)
ROUNDER = 12582912.0


def from_everyone(x, axis):
    copies = jnp.broadcast_to(x, (lax.axis_size(axis), *x.shape))
    return lax.all_to_all(copies, axis, split_axis=0, concat_axis=0, tiled=True)


REACH = 3
XO, YO = 3, 4
SEND = 5


def lanes(shape):
    return lax.broadcasted_iota(jnp.int32, shape, len(shape) - 1)


def turned(x, shift):
    return pltpu.roll(x, shift % x.shape[-1], x.ndim - 1)


def params(megabytes):
    return pltpu.CompilerParams(vmem_limit_bytes=megabytes << 20)


def whole_call(kernel, out_shape, scratch, name, scalars, *operands, megabytes=4, away=(), aliases={}):
    smem = pl.BlockSpec(memory_space=pltpu.SMEM)
    vmem = pl.BlockSpec(memory_space=pltpu.VMEM)
    far = pl.BlockSpec(memory_space=pltpu.HBM)
    return pl.pallas_call(
        kernel,
        in_specs=[smem] * len(scalars) + [far if n in away else vmem for n in range(len(operands))],
        out_specs=jax.tree.map(lambda _: vmem, out_shape),
        out_shape=out_shape,
        scratch_shapes=scratch,
        compiler_params=params(megabytes),
        input_output_aliases={len(scalars) + k: v for k, v in aliases.items()},
        name=name,
    )(*scalars, *operands)


def f32(*shape):
    return jax.ShapeDtypeStruct(shape, jnp.float32)


def bf16(*shape):
    return jax.ShapeDtypeStruct(shape, jnp.bfloat16)


def split(x):
    high = x.astype(jnp.bfloat16)
    return high, (x - high.astype(jnp.float32)).astype(jnp.bfloat16)


def across(a, b):
    return lax.dot_general(a, b, (((1,), (1,)), ((), ())), preferred_element_type=jnp.float32)


def compact_kernel(target_ref, target_out, table_ref, counts, table, arrived):
    bricks, depth, slots = target_ref.shape
    lane = lanes((depth, slots))
    first = jnp.zeros((depth, slots), jnp.float32)
    for brick in range(bricks):
        first = jnp.where(lane == brick, target_ref[brick, 4:5, :], first)
    counts[...] = first.astype(jnp.int32)
    copy = pltpu.make_async_copy(counts, table, arrived)
    copy.start()
    target_out[...] = jnp.zeros_like(target_out)
    copy.wait()
    begin = jnp.int32(0)
    for brick in range(bricks):
        append(target_out, target_ref[brick], begin, table[0, brick])
        table_ref[brick] = begin
        begin = begin + table[0, brick]
    table_ref[bricks] = begin


def append(out, rows, begin, count):
    group, shift = begin >> 7, begin & 127
    lane = lanes(rows.shape)
    moved = pltpu.roll(rows, shift, 1)
    out[group] = jnp.where((lane >= shift) & (lane < shift + count), moved, out[group])
    out[group + 1] = jnp.where(lane < shift + count - rows.shape[1], moved, out[group + 1])


def tile_kernel(half, table_ref, source_ref, target_ref, *refs):
    tile_ref, share_ref, columns, density = refs[-4:]
    bricks, slots = source_ref.shape[0], source_ref.shape[2]
    channels = share_ref.shape[1]
    step = pl.program_id(0)

    @pl.when(step == 0)
    def _():
        for brick in range(bricks):
            density[:, brick * slots : (brick + 1) * slots] = source_ref[brick, :channels].astype(jnp.bfloat16)

    @pl.when((2 * step + half) * slots < table_ref[bricks])
    def _():
        columns[...] = jnp.transpose(target_ref[0])
        spread = [jnp.broadcast_to(columns[:, d : d + 1], (slots, slots)) for d in range(3)]
        total = jnp.zeros((channels, slots), jnp.float32)
        for pair in range(0, bricks, 2):
            both = []
            for brick in (pair, pair + 1):
                square = 1e-30
                for d in range(3):
                    delta = spread[d] - source_ref[brick, channels + d : channels + d + 1, :]
                    square = square + delta * delta
                turns = square * lax.rsqrt(square)
                whole = (turns + ROUNDER) - ROUNDER
                angle = 0.25 - jnp.abs(turns - whole)
                angle2 = angle * angle
                wave = SINE[-1]
                for c in SINE[-2::-1]:
                    wave = wave * angle2 + c
                weight = source_ref[brick, channels + 3 : channels + 4, :]
                value = (angle * weight) * wave / (turns + soften * TURNS)
                both.append(value.astype(jnp.bfloat16))
                tile_ref[:, brick * slots : (brick + 1) * slots] = both[-1]
            at = slice(pair * slots, (pair + 2) * slots)
            total = total + across(density[:, at], jnp.concatenate(both, axis=1))
        share_ref[0] = total


def make_tile(half, table, sources, targets, channels, before=()):
    bricks, slots = sources.shape[0], sources.shape[2]
    far = pl.BlockSpec(memory_space=pl.ANY)
    return pl.pallas_call(
        functools.partial(tile_kernel, half),
        grid=(bricks // 2,),
        in_specs=[
            pl.BlockSpec(memory_space=pltpu.SMEM),
            pl.BlockSpec(sources.shape, lambda b: (0, 0, 0)),
            pl.BlockSpec((1, targets.shape[1], slots), lambda b: (2 * b + half, 0, 0)),
        ]
        + [far] * len(before),
        out_specs=[
            pl.BlockSpec((slots, bricks * slots), lambda b: (2 * b + half, 0)),
            pl.BlockSpec((1, channels, slots), lambda b: (2 * b + half, 0, 0)),
        ],
        out_shape=[
            jax.ShapeDtypeStruct((ROOM * bricks * slots, bricks * slots), jnp.bfloat16),
            jax.ShapeDtypeStruct((bricks, channels, slots), jnp.float32),
        ],
        scratch_shapes=[
            pltpu.VMEM((slots, targets.shape[1]), jnp.float32),
            pltpu.VMEM((channels, bricks * slots), jnp.bfloat16),
        ],
        input_output_aliases={3 + n: n for n in range(len(before))},
        compiler_params=params(8),
        name="tile",
    )(table, sources, targets, *before)


def taken(share_ref, table_ref, brick, bricks):
    begin = table_ref[brick]
    count = table_ref[brick + 1] - begin
    group, shift = begin >> 7, begin & 127
    lane = lanes(share_ref.shape[1:])
    slots = share_ref.shape[2]
    this = pltpu.roll(share_ref[group], (slots - shift) & 127, 1)
    following = pltpu.roll(share_ref[jnp.minimum(group + 1, bricks - 1)], (slots - shift) & 127, 1)
    return jnp.where(lane < count, jnp.where(lane < slots - shift, this, following), 0.0)


def arrange_kernel(table_ref, share_ref, out_ref):
    bricks = out_ref.shape[0]
    for index in range(bricks):
        value = taken(share_ref, table_ref, index, bricks)
        for n in range(6):
            side, other = index // 2 - (n % 3 - 1), (index + n // 3) % 2
            if 0 <= side < bricks // 2:
                out_ref[side * 2 + other, n] = value
    for brick in range(bricks):
        for n in range(6):
            if not 0 <= brick // 2 + n % 3 - 1 < bricks // 2:
                out_ref[brick, n] = jnp.zeros(out_ref.shape[2:], jnp.float32)


def product_kernel(table_ref, density_ref, tile_ref, out_ref, density, shares):
    bricks, channels, slots = density_ref.shape
    step = pl.program_id(0)
    count = tile_ref.shape[0] // slots

    @pl.when(step == 0)
    def _():
        for brick in range(bricks):
            density[:, brick * slots : (brick + 1) * slots] = density_ref[brick]

    @pl.when(step * count * slots < table_ref[bricks])
    def _():
        total = across(density[...], tile_ref[...])
        for index in range(count):
            shares[step * count + index] = total[:, index * slots : (index + 1) * slots]

    @pl.when(step == pl.num_programs(0) - 1)
    def _():
        for brick in range(bricks):
            out_ref[brick] = taken(shares, table_ref, brick, bricks)


def products(table, density, tile, rows):
    bricks, channels, slots = density.shape
    width = tile.shape[1]
    steps = bricks * slots // rows

    def block(b, table_ref):
        last = (table_ref[bricks] + rows - 1) // rows - 1
        return jnp.minimum(b, last), 0

    return pl.pallas_call(
        product_kernel,
        grid_spec=pltpu.PrefetchScalarGridSpec(
            num_scalar_prefetch=1,
            grid=(steps,),
            in_specs=[pl.BlockSpec(density.shape, lambda b, t: (0, 0, 0)), pl.BlockSpec((rows, width), block)],
            out_specs=pl.BlockSpec((bricks, channels, slots), lambda b, t: (0, 0, 0)),
            scratch_shapes=[
                pltpu.VMEM((channels, width), jnp.bfloat16),
                pltpu.VMEM((bricks, channels, slots), jnp.float32),
            ],
        ),
        out_shape=jax.ShapeDtypeStruct((bricks, channels, slots), jnp.float32),
        compiler_params=params(12),
        name="product",
    )(table, density, tile)


def put_planes(up_ref, down_ref, base, field_ref, depth, offset=0):
    size_x, size_y = field_ref.shape[-3], field_ref.shape[-2]
    for e in range(field_ref.shape[0]):
        for i in range(depth):
            rows = pl.ds(base + (e * depth + i) * size_y, size_y)
            high = field_ref[e, size_x - depth + i] + offset
            low = field_ref[e, i] + offset
            up_ref[rows, :] = high.astype(jnp.bfloat16)
            down_ref[rows, :] = low.astype(jnp.bfloat16)
    return base + field_ref.shape[0] * depth * size_y


def own_cells(frame_ref, field_ref, offset=0):
    channels, size_x, size_y = field_ref.shape[:3]
    planes, rows = size_x + 2 * XO, size_y + 2 * YO
    frame_ref[...] = jnp.zeros_like(frame_ref)
    for e in range(channels):
        for x in range(size_x):
            at = (e * planes + XO + x) * rows + YO
            frame_ref[at : at + size_y, :] = field_ref[e, x].astype(jnp.float32) + offset


def planes_kernel(
    factor, live_ref, shift_ref, state_hbm, source_hbm, class_hbm, geometry_ref, cell_ref,
    up_ref, down_ref, frame_ref, forcing_ref, code_ref, message_ref, state_ref, source_ref, class_ref, arrived,
):
    copies = [
        pltpu.make_async_copy(state_hbm, state_ref, arrived.at[0]),
        pltpu.make_async_copy(source_hbm, source_ref, arrived.at[1]),
        pltpu.make_async_copy(class_hbm, class_ref, arrived.at[2]),
    ]
    for copy in copies:
        copy.start()
    slots = cell_ref.shape[1]
    shifts = jnp.zeros((1, slots), jnp.float32)
    for index in range(CLASSES):
        shifts = jnp.where(lanes((1, slots)) == index, shift_ref[index], shifts)
    message = jnp.concatenate(
        [
            geometry_ref[:3] * TURNS,
            geometry_ref[3:] * (factor * TURNS),
            jnp.full((1, slots), live_ref[0], jnp.int32).astype(jnp.float32),
            cell_ref[...].astype(jnp.float32),
            shifts,
            jnp.zeros((1, slots), jnp.float32),
        ],
        axis=0,
    )
    for brick in range(message_ref.shape[0]):
        message_ref[brick] = message
    for copy in copies:
        copy.wait()
    base = put_planes(up_ref, down_ref, 0, state_ref, 3)
    base = put_planes(up_ref, down_ref, base, source_ref, 2)
    put_planes(up_ref, down_ref, base, class_ref, 2, 1.0)
    own_cells(frame_ref, state_ref)
    own_cells(forcing_ref, source_ref)
    own_cells(code_ref, class_ref, 1.0)


def beside(frame_ref, channels, low_ref, high_ref, base, depth):
    rows = SIZE_Y + 2 * YO
    planes = frame_ref.shape[0] // (channels * rows)
    size_x = planes - 2 * XO
    for e in range(channels):
        for i in range(depth):
            here = pl.ds(base + (e * depth + i) * SIZE_Y, SIZE_Y)
            at = (e * planes + XO - depth + i) * rows + YO
            frame_ref[at : at + SIZE_Y, :] = low_ref[here, :].astype(jnp.float32)
            at = (e * planes + XO + size_x + i) * rows + YO
            frame_ref[at : at + SIZE_Y, :] = high_ref[here, :].astype(jnp.float32)
    return base + channels * depth * SIZE_Y


def depth_rows(frames, gz, x, size_y, rows, planes, channels):
    lane = lanes((size_y, 128))
    out = jnp.zeros((size_y, 128), jnp.float32)
    for e in range(channels):
        for index, frame_ref in enumerate(frames):
            own = frame_ref.shape[0] == planes * rows
            at = ((0 if own else e) * planes + x) * rows + YO
            start = e * 16 + index * SEND + 1
            moved = turned(frame_ref[at : at + size_y, :], start + 3 - 3 * gz)
            out = jnp.where((lane >= start) & (lane < start + 3), moved, out)
    return out


def frame_kernel(full, channels, place_ref, *refs):
    if full:
        _, _, _, low_ref, high_ref, frame_ref, forcing_ref, code_ref, depth_ref = refs
    else:
        state_ref, low_ref, high_ref, frame_ref, depth_ref = refs
        own_cells(frame_ref, state_ref)
    rows = SIZE_Y + 2 * YO
    planes = frame_ref.shape[0] // (channels * rows)
    base = beside(frame_ref, channels, low_ref, high_ref, 0, 3)
    frames = [frame_ref]
    if full:
        base = beside(forcing_ref, channels, low_ref, high_ref, base, 2)
        beside(code_ref, 1, low_ref, high_ref, base, 2)
        frames = [frame_ref, forcing_ref, code_ref]
    gz = place_ref[1]
    for x in range(planes):
        out = depth_rows(frames, gz, x, SIZE_Y, rows, planes, channels)
        depth_ref[x * SIZE_Y : (x + 1) * SIZE_Y, :] = out.astype(jnp.bfloat16)


def edge_kernel(full, *refs):
    if full:
        frame_ref, forcing_ref, code_ref, other_ref, depth_ref, up_ref, down_ref = refs
    else:
        frame_ref, other_ref, depth_ref, up_ref, down_ref = refs
    rows = SIZE_Y + 2 * YO
    planes = depth_ref.shape[0] // rows
    depth_ref[...] = jnp.zeros_like(depth_ref)
    for x in range(planes):
        here = other_ref[x * SIZE_Y : (x + 1) * SIZE_Y, :].astype(jnp.float32)
        depth_ref[x * rows + YO : x * rows + YO + SIZE_Y, :] = here

    def put(base, ref, depth, step):
        count = ref.shape[0] // rows
        for j in range(depth):
            high = ref[pl.ds(YO + SIZE_Y - depth + j, count, stride=rows), :]
            low = ref[pl.ds(YO + j, count, stride=rows), :]
            up_ref[base + j * step : base + j * step + count, :] = high.astype(jnp.bfloat16)
            down_ref[base + j * step : base + j * step + count, :] = low.astype(jnp.bfloat16)
        return base + depth * step

    if full:
        up_ref[edge_tail(full) :, :] = jnp.zeros((80, 128), jnp.bfloat16)
        down_ref[edge_tail(full) :, :] = jnp.zeros((80, 128), jnp.bfloat16)
    else:
        up_ref[edge_tail(full) :, :] = jnp.zeros((48, 128), jnp.bfloat16)
        down_ref[edge_tail(full) :, :] = jnp.zeros((48, 128), jnp.bfloat16)
    base = put(0, frame_ref, 3, 80)
    if full:
        base = put(base, forcing_ref, 2, 80)
        base = put(base, code_ref, 2, 16)
    put(base, depth_ref, 3, 16)


def edge_tail(full):
    return 400 if full else 240


def take_edges(frame_ref, low_ref, high_ref, base, depth, step):
    rows = SIZE_Y + 2 * YO
    count = frame_ref.shape[0] // rows
    for j in range(depth):
        low = low_ref[base + j * step : base + j * step + count, :].astype(jnp.float32)
        high = high_ref[base + j * step : base + j * step + count, :].astype(jnp.float32)
        frame_ref[pl.ds(YO - depth + j, count, stride=rows), :] = low
        frame_ref[pl.ds(YO + SIZE_Y + j, count, stride=rows), :] = high
    return base + depth * step


def faces(get, e_range, gz, shape):
    lane = lanes(shape)
    out = jnp.zeros(shape, jnp.float32)
    for e in e_range:
        out = jnp.where(lane == e * 16 + 4 * gz, turned(get(e), e * 16 + 1 + 3 * gz), out)
    return out


def sweep(src, dst, zsrc, zdst, forcing, coef, zforcing, zcoef, gz, x_low, x_high, channels, planes, finish=None):
    rows = SIZE_Y + 2 * YO
    shape = (rows, 128)
    lane = lanes(shape)
    keep = 1.0 - relax_weight
    inner_low = (lane > 0).astype(jnp.float32)
    inner_high = (lane < 127).astype(jnp.float32)
    border = (lane == 127 - 127 * gz).astype(jnp.float32)
    face_lane = (lane & 15) == 4 * gz

    def one_plane(x, carry):
        at = pl.multiple_of(x * rows, 8)
        other = zsrc[pl.ds(at, rows), :]
        weight = coef[pl.ds(at, rows), :]
        fresh = []
        for e in range(channels):
            row = pl.multiple_of((e * planes + x) * rows, 8)
            own = src[pl.ds(row, rows), :]
            total = src[pl.ds(row + rows, rows), :] + src[pl.ds(row - rows, rows), :]
            total = total + pltpu.roll(own, rows - 1, 0) + pltpu.roll(own, 1, 0)
            total = total + pltpu.roll(own, 127, 1) * inner_high + pltpu.roll(own, 1, 1) * inner_low
            total = total + turned(other, 126 - gz - 16 * e + 256) * border
            new = keep * own + weight * (forcing[pl.ds(row, rows), :] + total)
            if finish is None:
                dst[pl.ds(row, rows), :] = new
            else:
                finish(e, x, new)
            fresh.append(new)
        if finish is None:
            total = zsrc[pl.ds(at + rows, rows), :] + zsrc[pl.ds(at - rows, rows), :]
            total = total + pltpu.roll(other, rows - 1, 0) + pltpu.roll(other, 1, 0)
            total = total + pltpu.roll(other, 127, 1) + pltpu.roll(other, 1, 1)
            new = keep * other + zcoef[pl.ds(at, rows), :] * (zforcing[pl.ds(at, rows), :] + total)
            face = faces(lambda e: fresh[e], range(channels), gz, shape)
            zdst[pl.ds(at, rows), :] = jnp.where(face_lane, face, new)
        return carry

    lax.fori_loop(x_low, x_high, one_plane, 0, unroll=True)


def sweeps(frame, second, zframe, zsecond, forcing, coef, zforcing, zcoef, gz, out_ref, planes):
    channels = out_ref.shape[0]
    rows = SIZE_Y + 2 * YO
    face_lane = (lanes((rows, 128)) & 15) == 4 * gz
    for x in range(planes):
        face = faces(lambda e: frame[(e * planes + x) * rows : (e * planes + x + 1) * rows, :], range(channels), gz, (rows, 128))
        here = zframe[x * rows : (x + 1) * rows, :]
        zframe[x * rows : (x + 1) * rows, :] = jnp.where(face_lane, face, here)
    sweep(frame, second, zframe, zsecond, forcing, coef, zforcing, zcoef, gz, 1, planes - 1, channels, planes)
    sweep(second, frame, zsecond, zframe, forcing, coef, zforcing, zcoef, gz, 2, planes - 2, channels, planes)

    def finish(e, x, new):
        out_ref[e, x - XO] = new[YO : YO + SIZE_Y, :]

    sweep(frame, None, zframe, None, forcing, coef, zforcing, zcoef, gz, XO, planes - XO, channels, planes, finish)


def put_density(out_ref, density_ref, cell, live, message_ref=None):
    channels, size_x, size_y, size_z = out_ref.shape
    slots = cell.shape[1]
    pick = (lax.broadcasted_iota(jnp.int32, (size_z, slots), 0) == (cell & (size_z - 1))).astype(jnp.bfloat16)
    count = size_x * size_y
    layers = out_ref[...].reshape(channels * count, size_z).astype(jnp.bfloat16)
    lines = jnp.dot(layers, pick, preferred_element_type=jnp.float32)
    used = lanes((count, slots)) < live
    mask = used & (lax.broadcasted_iota(jnp.int32, (count, slots), 0) == (cell >> 7))
    found = [
        jnp.sum(jnp.where(mask, lines[e * count : (e + 1) * count, :], 0.0), axis=0, keepdims=True)
        for e in range(channels)
    ]
    density = jnp.concatenate(found, axis=0).astype(jnp.bfloat16)
    if message_ref is None:
        for brick in range(density_ref.shape[0]):
            density_ref[brick] = density
    else:
        message = jnp.concatenate([density.astype(jnp.float32), message_ref[0]], axis=0)
        for brick in range(density_ref.shape[0]):
            density_ref[brick] = message


def parted(kept_ref):
    flat = SIZE_Y + 2 * YO
    flat = flat * (kept_ref.shape[0] // flat // KEPT)
    ends = [kept_ref.shape[0] - 3 * flat + n * flat for n in range(4)]
    return [kept_ref.at[0 : ends[0]]] + [kept_ref.at[ends[n] : ends[n + 1]] for n in range(3)]


def first_kernel(
    place_ref, frame_ref, forcing_ref, code_ref, depth_ref, low_ref, high_ref, message_ref,
    out_ref, kept_ref, density_ref, up_ref, down_ref, first, second, zfirst, zsecond, code, zcode,
):
    gz = place_ref[1]
    rows = SIZE_Y + 2 * YO
    planes = code_ref.shape[0] // rows
    forcing, coef, zforcing, zcoef = parted(kept_ref)
    first[...] = frame_ref[...]
    forcing[...] = forcing_ref[...]
    code[...] = code_ref[...]
    zcode[...] = depth_ref[...]
    base = take_edges(first, low_ref, high_ref, 0, 3, 80)
    base = take_edges(forcing, low_ref, high_ref, base, 2, 80)
    base = take_edges(code, low_ref, high_ref, base, 2, 16)
    take_edges(zcode, low_ref, high_ref, base, 3, 16)
    lane = lanes((rows, 128)) & 15
    outer = (lane >= 1) & (lane <= 3)
    shifts = [jnp.broadcast_to(message_ref[0, 6:7, n : n + 1], (rows, 128)) for n in range(CLASSES)]
    for x in range(planes):
        here = pl.ds(x * rows, rows)
        packed = zcode[here, :]
        zfirst[here, :] = jnp.where(outer, packed, 0.0)
        zforcing[here, :] = jnp.where(outer, turned(packed, 128 - SEND), 0.0)
        level = jnp.where(outer, turned(packed, 128 - 2 * SEND), 0.0)
        own_level = code[here, :]
        zshift = jnp.zeros((rows, 128), jnp.float32)
        shift = jnp.zeros((rows, 128), jnp.float32)
        for index in range(CLASSES):
            zshift = jnp.where(level == index + 1.0, shifts[index], zshift)
            shift = jnp.where(own_level == index + 1.0, shifts[index], shift)
        zcoef[here, :] = jnp.where(level > 0.0, relax_weight / (6.0 + zshift), 0.0)
        coef[here, :] = jnp.where(own_level > 0.0, relax_weight / (6.0 + shift), 0.0)
    sweeps(first, second, zfirst, zsecond, forcing, coef, zforcing, zcoef, gz, out_ref, planes)
    put_planes(up_ref, down_ref, 0, out_ref, 3)
    put_density(out_ref, density_ref, message_ref[0, 5:6, :].astype(jnp.int32), place_ref[2], message_ref)


def add_load(forcing, zforcing, near_ref, side, gz, channels, planes):
    rows = SIZE_Y + 2 * YO
    size_x = planes - 2 * XO
    cells = near_ref[6].astype(jnp.int32)
    slots = cells.shape[1]
    wide = 3 * slots

    def row_of(first):
        cell = jnp.concatenate([cells[first + n : first + n + 1, :] for n in range(3)], axis=1)
        shift = jnp.concatenate([jnp.full((1, slots), YO + SIZE_Y * (n - 1), jnp.int32) for n in range(3)], axis=1)
        value = coupling * jnp.concatenate([near_ref[first + n] for n in range(3)], axis=1)
        return cell & 127, ((cell >> 7) & (SIZE_Y - 1)) + shift, cell >> 11, value

    span = {-1: range(size_x - 2, size_x), 0: range(size_x), 1: range(2)}[side]
    level = lax.broadcasted_iota(jnp.int32, (rows, wide), 0)
    z, y, x, value = row_of(0)
    pick = (lax.broadcasted_iota(jnp.int32, (128, wide), 0) == z).astype(jnp.bfloat16)
    for plane in span:
        mask = (level == y) & (x == plane)
        spread = jnp.concatenate([jnp.where(mask, value[e : e + 1, :], 0.0) for e in range(channels)], axis=0)
        high, low = split(spread)
        load = across(high, pick) + across(low, pick)
        at = plane + XO + size_x * side
        for e in range(channels):
            row = (e * planes + at) * rows
            forcing[row : row + rows, :] += load[e * rows : (e + 1) * rows, :]
    z, y, x, value = row_of(3)
    lane = z - 125 * gz + 1
    step = lax.broadcasted_iota(jnp.int32, (16, wide), 0)
    ok = (step == lane) & (step >= 1) & (step <= 3)
    spread = jnp.concatenate([jnp.where(ok, value[e : e + 1, :], 0.0) for e in range(channels)], axis=0)
    high, low = split(spread)
    for plane in span:
        mask = ((level == y) & (x == plane)).astype(jnp.bfloat16)
        row = (plane + XO + size_x * side) * rows
        zforcing[row : row + rows, :] += across(mask, high) + across(mask, low)


def second_kernel(
    place_ref, frame_ref, kept_ref, depth_ref, low_ref, high_ref, near_low, near_own, near_high,
    out_ref, density_ref, first, second, zfirst, zsecond, forcing, zforcing,
):
    gz = place_ref[1]
    rows = SIZE_Y + 2 * YO
    planes = depth_ref.shape[0] // rows
    channels = out_ref.shape[0]
    old, coef, zold, zcoef = parted(kept_ref)
    first[...] = frame_ref[...]
    zfirst[...] = depth_ref[...]
    forcing[...] = old[...]
    zforcing[...] = zold[...]
    base = take_edges(first, low_ref, high_ref, 0, 3, 80)
    take_edges(zfirst, low_ref, high_ref, base, 3, 16)
    for side, near in ((-1, near_low), (0, near_own), (1, near_high)):
        add_load(forcing, zforcing, near, side, gz, channels, planes)
    sweeps(first, second, zfirst, zsecond, forcing, coef, zforcing, zcoef, gz, out_ref, planes)
    put_density(out_ref, density_ref, near_own[6, 1:2, :].astype(jnp.int32), place_ref[2])


def near_kernel(place_ref, parts_ref, targets_ref, near_ref, own_ref):
    col, gz = place_ref[0], place_ref[1]
    cols = targets_ref.shape[0] // 2
    slots = targets_ref.shape[2]
    lane = lanes((8, slots))
    near_ref[6] = jnp.zeros((8, slots), jnp.float32)
    for n in range(6):
        side = jnp.clip(col + n % 3 - 1, 0, cols - 1)
        half = gz if n < 3 else 1 - gz
        about = targets_ref[side * 2 + half]
        total = parts_ref[0, n]
        for sender in range(1, parts_ref.shape[0]):
            total = total + parts_ref[sender, n]
        total = jnp.where(lane < about[4:5, :].astype(jnp.int32), total, 0.0)
        near_ref[n] = total
        near_ref[6, n : n + 1, :] = about[5:6, :]
        if n == 1:
            own_ref[...] = total


def last_kernel(place_ref, parts_ref, own_ref):
    total = parts_ref[0]
    for sender in range(1, parts_ref.shape[0]):
        total = total + parts_ref[sender]
    own_ref[...] = jnp.where(lanes(total.shape) < place_ref[2], total, 0.0)


def both_ways(up, down, axis):
    devices = lax.axis_size(axis)
    pairs = [(i, i + 1) for i in range(devices - 1)]
    return lax.ppermute(up, axis, pairs), lax.ppermute(down, axis, [(b, a) for a, b in pairs])


def local(
    initial_field, source_term, cell_class, class_shift, surface_cell, live_count, panel_geometry
):
    channels, size_x, size_y, size_z = initial_field.shape
    slots = surface_cell.shape[0]
    bricks = lax.axis_size("row")
    panels = slots * lax.axis_size("row") * lax.axis_size("col") * lax.axis_size("gz")
    factor = 1.0 / math.sqrt(panels)
    planes, rows = size_x + 2 * XO, size_y + 2 * YO
    frame, flat = (channels * planes * rows, 128), (planes * rows, 128)
    place = jnp.stack([lax.axis_index("col"), lax.axis_index("gz"), live_count[0]]).astype(jnp.int32)
    cells = surface_cell[None]
    vm = lambda shape, dtype=jnp.float32: pltpu.VMEM(shape, dtype)

    send_x = channels * 5 * size_y + 2 * size_y
    up, down, start, forcing, code, message = whole_call(
        functools.partial(planes_kernel, factor),
        (bf16(send_x, 128), bf16(send_x, 128), f32(*frame), f32(*frame), f32(*flat), f32(bricks, 8, slots)),
        [vm(initial_field.shape), vm(initial_field.shape), vm((1, *cell_class.shape), jnp.int32),
         pltpu.SemaphoreType.DMA((3,))],
        "planes", (live_count, class_shift), initial_field, source_term, cell_class[None], panel_geometry, cells,
        away=(0, 1, 2),
    )
    low, high = both_ways(up, down, "row")
    targets = lax.all_to_all(message, ("col", "gz"), 0, 0, tiled=True)
    start, forcing, code, depth = whole_call(
        functools.partial(frame_kernel, True, channels),
        (f32(*frame), f32(*frame), f32(*flat), bf16(planes * size_y, 128)), [], "frame", (place,),
        start, forcing, code, low, high, aliases={0: 0, 1: 1, 2: 2},
    )
    other = lax.ppermute(depth, "gz", [(0, 1), (1, 0)])
    other, targets = lax.optimization_barrier((other, targets))
    zframe, up, down = whole_call(
        functools.partial(edge_kernel, True), (f32(*flat), bf16(480, 128), bf16(480, 128)), [], "edges", (),
        start, forcing, code, other,
    )
    low, high = both_ways(up, down, "col")
    smem = pl.BlockSpec(memory_space=pltpu.SMEM)
    vmem = pl.BlockSpec(memory_space=pltpu.VMEM)
    aims, table = pl.pallas_call(
        compact_kernel,
        in_specs=[vmem],
        out_specs=(vmem, smem),
        out_shape=(f32(bricks + 1, 8, slots), jax.ShapeDtypeStruct((bricks + 1,), jnp.int32)),
        scratch_shapes=[vm((8, slots), jnp.int32), pltpu.SMEM((8, slots), jnp.int32), pltpu.SemaphoreType.DMA],
        compiler_params=params(4),
        name="compact",
    )(targets)
    low, high, aims, table = lax.optimization_barrier((low, high, aims, table))
    state, kept, density, up, down = whole_call(
        first_kernel,
        (f32(*initial_field.shape), f32(frame[0] + 3 * flat[0], 128), f32(bricks, 2 * channels, slots),
         bf16(channels * 3 * size_y, 128), bf16(channels * 3 * size_y, 128)),
        [vm(frame), vm(frame), vm(flat), vm(flat), vm(flat), vm(flat)], "first", (place,),
        start, forcing, code, zframe, low, high, message, megabytes=8,
    )
    low, high = both_ways(up, down, "row")
    densities = lax.all_to_all(density, "row", 0, 0, tiled=True)
    start, depth = whole_call(
        functools.partial(frame_kernel, False, channels), (f32(*frame), bf16(planes * size_y, 128)), [], "frame", (place,),
        state, low, high,
    )
    other = lax.ppermute(depth, "gz", [(0, 1), (1, 0)])
    densities, depth = lax.optimization_barrier((densities, depth))
    tile, shares = make_tile(0, table, densities, aims, channels)
    other, shares = lax.optimization_barrier((other, shares))
    zframe, up, down = whole_call(
        functools.partial(edge_kernel, False), (f32(*flat), bf16(288, 128), bf16(288, 128)), [], "edges", (),
        start, other,
    )
    low, high = both_ways(up, down, "col")
    densities, up = lax.optimization_barrier((densities, up))
    tile, shares = make_tile(1, table, densities, aims, channels, (tile, shares))
    shares = whole_call(arrange_kernel, f32(bricks, 6, channels, slots), [], "arrange", (table,), shares)
    parts = lax.all_to_all(shares, ("col", "gz"), 0, 0, tiled=True)
    near, _ = whole_call(near_kernel, (f32(7, channels, slots), f32(channels, slots)), [], "near", (place,), parts, targets)
    near_low, near_high = both_ways(near, near, "row")
    state, density = whole_call(
        second_kernel, (f32(*initial_field.shape), bf16(bricks, channels, slots)),
        [vm(frame), vm(frame), vm(flat), vm(flat), vm(frame), vm(flat)], "second", (place,),
        start, kept, zframe, low, high, near_low, near, near_high, megabytes=8,
    )
    densities = lax.all_to_all(density, "row", 0, 0, tiled=True)
    shares = products(table, densities, tile, 512)
    parts = lax.all_to_all(shares, ("col", "gz"), 0, 0, tiled=True)
    potential = whole_call(last_kernel, f32(channels, slots), [], "last", (place,), parts)
    return (state, potential)


def solution(mesh):
    placed = (
        P(None, "row", "col", "gz"),
        P(None, "row", "col", "gz"),
        P("row", "col", "gz"),
        P(),
        P(("row", "col", "gz")),
        P(("row", "col", "gz")),
        P(None, ("row", "col", "gz")),
    )
    return jax.shard_map(
        local,
        mesh=mesh,
        in_specs=placed,
        out_specs=(P(None, "row", "col", "gz"), P(None, ("row", "col", "gz"))),
        check_vma=False,
    )
```

```python
import functools
import math

import jax
import jax.numpy as jnp
from jax import lax
from jax.experimental import pallas as pl
from jax.experimental.pallas import tpu as pltpu
from jax.sharding import PartitionSpec as P

SIZE_Y = 16
CLASSES = 16
KEPT = 19
TILES = 3
ROOM = 8

relax_weight = 0.8
wave_number = 25.0
soften = 0.05
coupling = 0.5

SINE = (6.283164044297846, -41.33714237050646, 81.34076886863805, -70.99343309793157)
TURNS = wave_number / (2.0 * math.pi)


def from_everyone(x, axis):
    copies = jnp.broadcast_to(x, (lax.axis_size(axis), *x.shape))
    return lax.all_to_all(copies, axis, split_axis=0, concat_axis=0, tiled=True)


REACH = 3
XO, YO = 3, 4
SEND = 5


def lanes(shape):
    return lax.broadcasted_iota(jnp.int32, shape, len(shape) - 1)


def turned(x, shift):
    return pltpu.roll(x, shift % x.shape[-1], x.ndim - 1)


def params(megabytes):
    return pltpu.CompilerParams(vmem_limit_bytes=megabytes << 20)


def whole_call(kernel, out_shape, scratch, name, scalars, *operands, megabytes=4, away=(), aliases={}):
    smem = pl.BlockSpec(memory_space=pltpu.SMEM)
    vmem = pl.BlockSpec(memory_space=pltpu.VMEM)
    far = pl.BlockSpec(memory_space=pltpu.HBM)
    return pl.pallas_call(
        kernel,
        in_specs=[smem] * len(scalars) + [far if n in away else vmem for n in range(len(operands))],
        out_specs=jax.tree.map(lambda _: vmem, out_shape),
        out_shape=out_shape,
        scratch_shapes=scratch,
        compiler_params=params(megabytes),
        input_output_aliases={len(scalars) + k: v for k, v in aliases.items()},
        name=name,
    )(*scalars, *operands)


def f32(*shape):
    return jax.ShapeDtypeStruct(shape, jnp.float32)


def bf16(*shape):
    return jax.ShapeDtypeStruct(shape, jnp.bfloat16)


def split(x):
    high = x.astype(jnp.bfloat16)
    return high, (x - high.astype(jnp.float32)).astype(jnp.bfloat16)


def across(a, b):
    return lax.dot_general(a, b, (((1,), (1,)), ((), ())), preferred_element_type=jnp.float32)


def compact_kernel(place_ref, target_ref, target_out, note_ref, table_ref, counts, table, arrived):
    bricks, depth, slots = target_ref.shape
    lane = lanes((depth, slots))
    first = jnp.zeros((depth, slots), jnp.float32)
    for brick in range(bricks):
        first = jnp.where(lane == brick, target_ref[brick, 4:5, :], first)
    counts[...] = first.astype(jnp.int32)
    copy = pltpu.make_async_copy(counts, table, arrived)
    copy.start()
    target_out[...] = jnp.zeros_like(target_out)
    note_ref[...] = target_ref[place_ref[0] * 2 + place_ref[1]]
    copy.wait()
    begin = jnp.int32(0)
    for brick in range(bricks):
        append(target_out, target_ref[brick], begin, table[0, brick])
        table_ref[brick] = begin
        begin = begin + table[0, brick]
    table_ref[bricks] = begin


def append(out, rows, begin, count):
    group, shift = begin >> 7, begin & 127
    lane = lanes(rows.shape)
    moved = pltpu.roll(rows, shift, 1)
    out[group] = jnp.where((lane >= shift) & (lane < shift + count), moved, out[group])
    out[group + 1] = jnp.where(lane < shift + count - rows.shape[1], moved, out[group + 1])


def tile_kernel(part, table_ref, source_ref, target_ref, *refs):
    tile_ref, share_ref, columns, density = refs[-4:]
    bricks, slots = source_ref.shape[0], source_ref.shape[2]
    channels = share_ref.shape[1]
    step = pl.program_id(0)

    @pl.when(step == 0)
    def _():
        for brick in range(bricks):
            density[:, brick * slots : (brick + 1) * slots] = source_ref[brick, :channels].astype(jnp.bfloat16)

    @pl.when((TILES * step + part) * slots < table_ref[bricks])
    def _():
        columns[...] = jnp.transpose(target_ref[0])
        spread = [jnp.broadcast_to(columns[:, d : d + 1], (slots, slots)) for d in range(3)]
        total = jnp.zeros((channels, slots), jnp.float32)
        for pair in range(0, bricks, 2):
            both = []
            for brick in (pair, pair + 1):
                delta = [spread[d] - source_ref[brick, channels + d : channels + d + 1, :] for d in range(3)]
                square = delta[0] * delta[0] + (delta[1] * delta[1] + (delta[2] * delta[2] + 1e-30))
                turns = square * lax.rsqrt(square)
                angle = 0.25 - jnp.abs(turns - jnp.round(turns))
                angle2 = angle * angle
                wave = SINE[-1]
                for c in SINE[-2::-1]:
                    wave = wave * angle2 + c
                weight = source_ref[brick, channels + 3 : channels + 4, :]
                value = (angle * weight) * wave / (turns + soften * TURNS)
                both.append(value.astype(jnp.bfloat16))
                tile_ref[:, brick * slots : (brick + 1) * slots] = both[-1]
            at = slice(pair * slots, (pair + 2) * slots)
            total = total + across(density[:, at], jnp.concatenate(both, axis=1))
        share_ref[0] = total


def make_tile(part, table, sources, targets, channels, before=()):
    bricks, slots = sources.shape[0], sources.shape[2]
    far = pl.BlockSpec(memory_space=pl.ANY)
    return pl.pallas_call(
        functools.partial(tile_kernel, part),
        grid=(-(-bricks // TILES),),
        in_specs=[
            pl.BlockSpec(memory_space=pltpu.SMEM),
            pl.BlockSpec(sources.shape, lambda b: (0, 0, 0)),
            pl.BlockSpec((1, targets.shape[1], slots), lambda b: (TILES * b + part, 0, 0)),
        ]
        + [far] * len(before),
        out_specs=[
            pl.BlockSpec((slots, bricks * slots), lambda b: (TILES * b + part, 0)),
            pl.BlockSpec((1, channels, slots), lambda b: (TILES * b + part, 0, 0)),
        ],
        out_shape=[
            jax.ShapeDtypeStruct((ROOM * bricks * slots, bricks * slots), jnp.bfloat16),
            jax.ShapeDtypeStruct((bricks + 2, channels, slots), jnp.float32),
        ],
        scratch_shapes=[
            pltpu.VMEM((slots, targets.shape[1]), jnp.float32),
            pltpu.VMEM((channels, bricks * slots), jnp.bfloat16),
        ],
        input_output_aliases={3 + n: n for n in range(len(before))},
        compiler_params=params(8),
        name="tile",
    )(table, sources, targets, *before)


def taken(share_ref, table_ref, brick, bricks):
    begin = table_ref[brick]
    count = table_ref[brick + 1] - begin
    group, shift = begin >> 7, begin & 127
    lane = lanes(share_ref.shape[1:])
    slots = share_ref.shape[2]
    this = pltpu.roll(share_ref[group], (slots - shift) & 127, 1)
    following = pltpu.roll(share_ref[jnp.minimum(group + 1, bricks - 1)], (slots - shift) & 127, 1)
    return jnp.where(lane < count, jnp.where(lane < slots - shift, this, following), 0.0)


def arrange_kernel(table_ref, share_ref, out_ref):
    bricks = out_ref.shape[0]
    for index in range(bricks):
        value = taken(share_ref, table_ref, index, bricks)
        for n in range(6):
            side, other = index // 2 - (n % 3 - 1), (index + n // 3) % 2
            if 0 <= side < bricks // 2:
                out_ref[side * 2 + other, n] = value
    for brick in range(bricks):
        for n in range(6):
            if not 0 <= brick // 2 + n % 3 - 1 < bricks // 2:
                out_ref[brick, n] = jnp.zeros(out_ref.shape[2:], jnp.float32)


def product_kernel(table_ref, density_ref, tile_ref, out_ref, density, shares):
    bricks, channels, slots = density_ref.shape
    step = pl.program_id(0)
    count = tile_ref.shape[0] // slots

    @pl.when(step == 0)
    def _():
        for brick in range(bricks):
            density[:, brick * slots : (brick + 1) * slots] = density_ref[brick]

    @pl.when(step * count * slots < table_ref[bricks])
    def _():
        total = across(density[...], tile_ref[...])
        for index in range(count):
            shares[step * count + index] = total[:, index * slots : (index + 1) * slots]

    @pl.when(step == pl.num_programs(0) - 1)
    def _():
        for brick in range(bricks):
            out_ref[brick] = taken(shares, table_ref, brick, bricks)


def products(table, density, tile, rows):
    bricks, channels, slots = density.shape
    width = tile.shape[1]
    steps = bricks * slots // rows

    def block(b, table_ref):
        last = (table_ref[bricks] + rows - 1) // rows - 1
        return jnp.minimum(b, last), 0

    return pl.pallas_call(
        product_kernel,
        grid_spec=pltpu.PrefetchScalarGridSpec(
            num_scalar_prefetch=1,
            grid=(steps,),
            in_specs=[pl.BlockSpec(density.shape, lambda b, t: (0, 0, 0)), pl.BlockSpec((rows, width), block)],
            out_specs=pl.BlockSpec((bricks, channels, slots), lambda b, t: (0, 0, 0)),
            scratch_shapes=[
                pltpu.VMEM((channels, width), jnp.bfloat16),
                pltpu.VMEM((bricks, channels, slots), jnp.float32),
            ],
        ),
        out_shape=jax.ShapeDtypeStruct((bricks, channels, slots), jnp.float32),
        compiler_params=params(12),
        name="product",
    )(table, density, tile)


def put_planes(up_ref, down_ref, base, field_ref, depth, offset=0):
    size_x, size_y = field_ref.shape[-3], field_ref.shape[-2]
    for e in range(field_ref.shape[0]):
        for i in range(depth):
            rows = pl.ds(base + (e * depth + i) * size_y, size_y)
            high = field_ref[e, size_x - depth + i] + offset
            low = field_ref[e, i] + offset
            up_ref[rows, :] = high.astype(jnp.bfloat16)
            down_ref[rows, :] = low.astype(jnp.bfloat16)
    return base + field_ref.shape[0] * depth * size_y


def own_cells(frame_ref, field_ref, offset=0):
    channels, size_x, size_y = field_ref.shape[:3]
    planes, rows = size_x + 2 * XO, size_y + 2 * YO
    frame_ref[...] = jnp.zeros_like(frame_ref)
    for e in range(channels):
        for x in range(size_x):
            at = (e * planes + XO + x) * rows + YO
            frame_ref[at : at + size_y, :] = field_ref[e, x].astype(jnp.float32) + offset


def put_framed_planes(up_ref, down_ref, frame_ref, channels, depth):
    rows = SIZE_Y + 2 * YO
    planes = frame_ref.shape[0] // (channels * rows)
    for e in range(channels):
        for i in range(depth):
            here = pl.ds((e * depth + i) * SIZE_Y, SIZE_Y)
            high = (e * planes + planes - XO - depth + i) * rows + YO
            low = (e * planes + XO + i) * rows + YO
            up_ref[here, :] = frame_ref[high : high + SIZE_Y, :].astype(jnp.bfloat16)
            down_ref[here, :] = frame_ref[low : low + SIZE_Y, :].astype(jnp.bfloat16)


def planes_kernel(
    factor, live_ref, shift_ref, state_hbm, source_hbm, class_hbm, geometry_hbm, cell_hbm,
    up_ref, down_ref, message_ref, state_ref, source_ref, class_ref, geometry_ref, cell_ref, arrived,
):
    pairs = (
        (geometry_hbm, geometry_ref), (cell_hbm, cell_ref),
        (state_hbm, state_ref), (source_hbm, source_ref), (class_hbm, class_ref),
    )
    copies = [pltpu.make_async_copy(a, b, arrived.at[n]) for n, (a, b) in enumerate(pairs)]
    for copy in copies:
        copy.start()
    slots = cell_ref.shape[1]
    shifts = jnp.zeros((1, slots), jnp.float32)
    for index in range(CLASSES):
        shifts = jnp.where(lanes((1, slots)) == index, shift_ref[index], shifts)
    copies[0].wait()
    copies[1].wait()
    message = jnp.concatenate(
        [
            geometry_ref[:3] * TURNS,
            geometry_ref[3:] * (factor * TURNS),
            jnp.full((1, slots), live_ref[0], jnp.int32).astype(jnp.float32),
            cell_ref[...].astype(jnp.float32),
            shifts,
            jnp.zeros((1, slots), jnp.float32),
        ],
        axis=0,
    )
    for brick in range(message_ref.shape[0]):
        message_ref[brick] = message
    for copy in copies[2:]:
        copy.wait()
    base = put_planes(up_ref, down_ref, 0, state_ref, 3)
    base = put_planes(up_ref, down_ref, base, source_ref, 2)
    put_planes(up_ref, down_ref, base, class_ref, 2, 1.0)


def own_kernel(state_ref, source_ref, class_ref, kept_ref):
    frame_ref, forcing_ref, code_ref, _, _ = parted(kept_ref)
    own_cells(frame_ref, state_ref)
    own_cells(forcing_ref, source_ref)
    own_cells(code_ref, class_ref, 1.0)


def beside(frame_ref, channels, low_ref, high_ref, base, depth):
    rows = SIZE_Y + 2 * YO
    planes = frame_ref.shape[0] // (channels * rows)
    size_x = planes - 2 * XO
    for e in range(channels):
        for i in range(depth):
            here = pl.ds(base + (e * depth + i) * SIZE_Y, SIZE_Y)
            at = (e * planes + XO - depth + i) * rows + YO
            frame_ref[at : at + SIZE_Y, :] = low_ref[here, :].astype(jnp.float32)
            at = (e * planes + XO + size_x + i) * rows + YO
            frame_ref[at : at + SIZE_Y, :] = high_ref[here, :].astype(jnp.float32)
    return base + channels * depth * SIZE_Y


def depth_rows(frames, gz, x, size_y, rows, planes, channels):
    lane = lanes((size_y, 128))
    out = jnp.zeros((size_y, 128), jnp.float32)
    for e in range(channels):
        for index, frame_ref in enumerate(frames):
            own = frame_ref.shape[0] == planes * rows
            at = ((0 if own else e) * planes + x) * rows + YO
            start = e * 16 + index * SEND + 1
            moved = turned(frame_ref[at : at + size_y, :], start + 3 - 3 * gz)
            out = jnp.where((lane >= start) & (lane < start + 3), moved, out)
    return out


def frame_kernel(full, channels, place_ref, _, low_ref, high_ref, kept_ref, depth_ref):
    frame_ref, forcing_ref, code_ref, _, _ = parted(kept_ref)
    rows = SIZE_Y + 2 * YO
    planes = frame_ref.shape[0] // (channels * rows)
    base = beside(frame_ref, channels, low_ref, high_ref, 0, 3)
    frames = [frame_ref]
    if full:
        base = beside(forcing_ref, channels, low_ref, high_ref, base, 2)
        beside(code_ref, 1, low_ref, high_ref, base, 2)
        frames = [frame_ref, forcing_ref, code_ref]
    gz = place_ref[1]
    for x in range(planes):
        out = depth_rows(frames, gz, x, SIZE_Y, rows, planes, channels)
        depth_ref[x * SIZE_Y : (x + 1) * SIZE_Y, :] = out.astype(jnp.bfloat16)


def edge_kernel(full, kept_ref, other_ref, depth_ref, up_ref, down_ref):
    frame_ref, forcing_ref, code_ref, _, _ = parted(kept_ref)
    rows = SIZE_Y + 2 * YO
    planes = depth_ref.shape[0] // rows
    depth_ref[...] = jnp.zeros_like(depth_ref)
    for x in range(planes):
        here = other_ref[x * SIZE_Y : (x + 1) * SIZE_Y, :].astype(jnp.float32)
        depth_ref[x * rows + YO : x * rows + YO + SIZE_Y, :] = here

    def put(base, ref, depth, step):
        count = ref.shape[0] // rows
        for j in range(depth):
            high = ref[pl.ds(YO + SIZE_Y - depth + j, count, stride=rows), :]
            low = ref[pl.ds(YO + j, count, stride=rows), :]
            up_ref[base + j * step : base + j * step + count, :] = high.astype(jnp.bfloat16)
            down_ref[base + j * step : base + j * step + count, :] = low.astype(jnp.bfloat16)
        return base + depth * step

    if full:
        up_ref[edge_tail(full) :, :] = jnp.zeros((80, 128), jnp.bfloat16)
        down_ref[edge_tail(full) :, :] = jnp.zeros((80, 128), jnp.bfloat16)
    else:
        up_ref[edge_tail(full) :, :] = jnp.zeros((48, 128), jnp.bfloat16)
        down_ref[edge_tail(full) :, :] = jnp.zeros((48, 128), jnp.bfloat16)
    base = put(0, frame_ref, 3, 80)
    if full:
        base = put(base, forcing_ref, 2, 80)
        base = put(base, code_ref, 2, 16)
    put(base, depth_ref, 3, 16)


def edge_tail(full):
    return 400 if full else 240


def take_edges(frame_ref, low_ref, high_ref, base, depth, step):
    rows = SIZE_Y + 2 * YO
    count = frame_ref.shape[0] // rows
    for j in range(depth):
        low = low_ref[base + j * step : base + j * step + count, :].astype(jnp.float32)
        high = high_ref[base + j * step : base + j * step + count, :].astype(jnp.float32)
        frame_ref[pl.ds(YO - depth + j, count, stride=rows), :] = low
        frame_ref[pl.ds(YO + SIZE_Y + j, count, stride=rows), :] = high
    return base + depth * step


def faces(get, e_range, gz, shape):
    lane = lanes(shape)
    out = jnp.zeros(shape, jnp.float32)
    for e in e_range:
        out = jnp.where(lane == e * 16 + 4 * gz, turned(get(e), e * 16 + 1 + 3 * gz), out)
    return out


def sweep(src, dst, zsrc, zdst, forcing, coef, zforcing, zcoef, gz, x_low, x_high, channels, planes, finish=None):
    rows = SIZE_Y + 2 * YO
    shape = (rows, 128)
    lane = lanes(shape)
    keep = 1.0 - relax_weight
    inner_low = (lane > 0).astype(jnp.float32)
    inner_high = (lane < 127).astype(jnp.float32)
    border = (lane == 127 - 127 * gz).astype(jnp.float32)
    face_lane = (lane & 15) == 4 * gz

    def one_plane(x, carry):
        at = pl.multiple_of(x * rows, 8)
        other = zsrc[pl.ds(at, rows), :]
        weight = coef[pl.ds(at, rows), :]
        fresh = []
        for e in range(channels):
            row = pl.multiple_of((e * planes + x) * rows, 8)
            own = src[pl.ds(row, rows), :]
            total = src[pl.ds(row + rows, rows), :] + src[pl.ds(row - rows, rows), :]
            total = total + pltpu.roll(own, rows - 1, 0) + pltpu.roll(own, 1, 0)
            total = total + pltpu.roll(own, 127, 1) * inner_high + pltpu.roll(own, 1, 1) * inner_low
            total = total + turned(other, 126 - gz - 16 * e + 256) * border
            new = keep * own + weight * (forcing[pl.ds(row, rows), :] + total)
            if finish is None:
                dst[pl.ds(row, rows), :] = new
            else:
                finish(e, x, new)
            fresh.append(new)
        if finish is None:
            total = zsrc[pl.ds(at + rows, rows), :] + zsrc[pl.ds(at - rows, rows), :]
            total = total + pltpu.roll(other, rows - 1, 0) + pltpu.roll(other, 1, 0)
            total = total + pltpu.roll(other, 127, 1) + pltpu.roll(other, 1, 1)
            new = keep * other + zcoef[pl.ds(at, rows), :] * (zforcing[pl.ds(at, rows), :] + total)
            face = faces(lambda e: fresh[e], range(channels), gz, shape)
            zdst[pl.ds(at, rows), :] = jnp.where(face_lane, face, new)
        return carry

    lax.fori_loop(x_low, x_high, one_plane, 0, unroll=True)


def sweeps(frame, second, zframe, zsecond, forcing, coef, zforcing, zcoef, gz, channels, planes, finish):
    rows = SIZE_Y + 2 * YO
    face_lane = (lanes((rows, 128)) & 15) == 4 * gz
    for x in range(planes):
        face = faces(lambda e: frame[(e * planes + x) * rows : (e * planes + x + 1) * rows, :], range(channels), gz, (rows, 128))
        here = zframe[x * rows : (x + 1) * rows, :]
        zframe[x * rows : (x + 1) * rows, :] = jnp.where(face_lane, face, here)
    sweep(frame, second, zframe, zsecond, forcing, coef, zforcing, zcoef, gz, 1, planes - 1, channels, planes)
    sweep(second, frame, zsecond, zframe, forcing, coef, zforcing, zcoef, gz, 2, planes - 2, channels, planes)

    sweep(frame, None, zframe, None, forcing, coef, zforcing, zcoef, gz, XO, planes - XO, channels, planes, finish)


def density_of(layers, cell, live, channels):
    slots, size_z = cell.shape[1], layers.shape[1]
    pick = (lax.broadcasted_iota(jnp.int32, (size_z, slots), 0) == (cell & (size_z - 1))).astype(jnp.bfloat16)
    count = layers.shape[0] // channels
    lines = jnp.dot(layers.astype(jnp.bfloat16), pick, preferred_element_type=jnp.float32)
    used = lanes((count, slots)) < live
    mask = used & (lax.broadcasted_iota(jnp.int32, (count, slots), 0) == (cell >> 7))
    found = [
        jnp.sum(jnp.where(mask, lines[e * count : (e + 1) * count, :], 0.0), axis=0, keepdims=True)
        for e in range(channels)
    ]
    return jnp.concatenate(found, axis=0).astype(jnp.bfloat16)


def parted(kept_ref):
    rows = kept_ref.shape[0] // KEPT
    frame = (KEPT - 3) // 2 * rows
    ends = [0, frame, 2 * frame] + [2 * frame + n * rows for n in range(1, 4)]
    return [kept_ref.at[ends[n] : ends[n + 1]] for n in range(5)]


def first_kernel(
    place_ref, _, depth_ref, low_ref, high_ref, note_ref,
    kept_ref, up_ref, down_ref, first, second, zfirst, zsecond, code, zcode,
):
    gz = place_ref[1]
    rows = SIZE_Y + 2 * YO
    planes = depth_ref.shape[0] // rows
    state, forcing, coef, zforcing, zcoef = parted(kept_ref)
    channels = first.shape[0] // (planes * rows)
    first[...] = state[...]
    code[...] = coef[...]
    zcode[...] = depth_ref[...]
    base = take_edges(first, low_ref, high_ref, 0, 3, 80)
    base = take_edges(forcing, low_ref, high_ref, base, 2, 80)
    base = take_edges(code, low_ref, high_ref, base, 2, 16)
    take_edges(zcode, low_ref, high_ref, base, 3, 16)
    lane = lanes((rows, 128)) & 15
    outer = (lane >= 1) & (lane <= 3)
    shifts = [jnp.broadcast_to(note_ref[6:7, n : n + 1], (rows, 128)) for n in range(CLASSES)]
    for x in range(planes):
        here = pl.ds(x * rows, rows)
        packed = zcode[here, :]
        zfirst[here, :] = jnp.where(outer, packed, 0.0)
        zforcing[here, :] = jnp.where(outer, turned(packed, 128 - SEND), 0.0)
        level = jnp.where(outer, turned(packed, 128 - 2 * SEND), 0.0)
        own_level = code[here, :]
        zshift = jnp.zeros((rows, 128), jnp.float32)
        shift = jnp.zeros((rows, 128), jnp.float32)
        for index in range(CLASSES):
            zshift = jnp.where(level == index + 1.0, shifts[index], zshift)
            shift = jnp.where(own_level == index + 1.0, shifts[index], shift)
        zcoef[here, :] = jnp.where(level > 0.0, relax_weight / (6.0 + zshift), 0.0)
        coef[here, :] = jnp.where(own_level > 0.0, relax_weight / (6.0 + shift), 0.0)

    def finish(e, x, new):
        state[pl.ds((e * planes + x) * rows + YO, SIZE_Y), :] = new[YO : YO + SIZE_Y, :]

    sweeps(first, second, zfirst, zsecond, forcing, coef, zforcing, zcoef, gz, channels, planes, finish)
    put_framed_planes(up_ref, down_ref, state, channels, 3)


def density_kernel(channels, place_ref, kept_ref, note_ref, density_ref, layers):
    state = parted(kept_ref)[0]
    rows = SIZE_Y + 2 * YO
    planes = state.shape[0] // (channels * rows)
    inner = planes - 2 * XO
    for e in range(channels):
        for x in range(inner):
            at = (e * planes + XO + x) * rows + YO
            layers[(e * inner + x) * SIZE_Y : (e * inner + x + 1) * SIZE_Y, :] = state[at : at + SIZE_Y, :]
    density = density_of(layers[...], note_ref[5:6, :].astype(jnp.int32), place_ref[2], channels)
    message = jnp.concatenate([density.astype(jnp.float32), note_ref[...]], axis=0)
    for brick in range(density_ref.shape[0]):
        density_ref[brick] = message


def add_load(forcing, zforcing, near_ref, side, gz, channels, planes):
    rows = SIZE_Y + 2 * YO
    size_x = planes - 2 * XO
    cells = near_ref[6].astype(jnp.int32)
    slots = cells.shape[1]
    wide = 3 * slots

    def row_of(first):
        cell = jnp.concatenate([cells[first + n : first + n + 1, :] for n in range(3)], axis=1)
        shift = jnp.concatenate([jnp.full((1, slots), YO + SIZE_Y * (n - 1), jnp.int32) for n in range(3)], axis=1)
        value = coupling * jnp.concatenate([near_ref[first + n] for n in range(3)], axis=1)
        return cell & 127, ((cell >> 7) & (SIZE_Y - 1)) + shift, cell >> 11, value

    span = {-1: range(size_x - 2, size_x), 0: range(size_x), 1: range(2)}[side]
    level = lax.broadcasted_iota(jnp.int32, (rows, wide), 0)
    z, y, x, value = row_of(0)
    pick = (lax.broadcasted_iota(jnp.int32, (128, wide), 0) == z).astype(jnp.bfloat16)
    for plane in span:
        mask = (level == y) & (x == plane)
        spread = jnp.concatenate([jnp.where(mask, value[e : e + 1, :], 0.0) for e in range(channels)], axis=0)
        high, low = split(spread)
        load = across(high, pick) + across(low, pick)
        at = plane + XO + size_x * side
        for e in range(channels):
            row = (e * planes + at) * rows
            forcing[row : row + rows, :] += load[e * rows : (e + 1) * rows, :]
    z, y, x, value = row_of(3)
    lane = z - 125 * gz + 1
    step = lax.broadcasted_iota(jnp.int32, (16, wide), 0)
    ok = (step == lane) & (step >= 1) & (step <= 3)
    spread = jnp.concatenate([jnp.where(ok, value[e : e + 1, :], 0.0) for e in range(channels)], axis=0)
    high, low = split(spread)
    for plane in span:
        mask = ((level == y) & (x == plane)).astype(jnp.bfloat16)
        row = (plane + XO + size_x * side) * rows
        zforcing[row : row + rows, :] += across(mask, high) + across(mask, low)


def second_kernel(
    place_ref, kept_ref, depth_ref, low_ref, high_ref, near_low, near_own, near_high,
    out_ref, density_ref, first, second, zfirst, zsecond, forcing, zforcing,
):
    gz = place_ref[1]
    rows = SIZE_Y + 2 * YO
    planes = depth_ref.shape[0] // rows
    channels = out_ref.shape[0]
    state, old, coef, zold, zcoef = parted(kept_ref)
    first[...] = state[...]
    zfirst[...] = depth_ref[...]
    forcing[...] = old[...]
    zforcing[...] = zold[...]
    base = take_edges(first, low_ref, high_ref, 0, 3, 80)
    take_edges(zfirst, low_ref, high_ref, base, 3, 16)
    for side, near in ((-1, near_low), (0, near_own), (1, near_high)):
        add_load(forcing, zforcing, near, side, gz, channels, planes)

    def finish(e, x, new):
        out_ref[e, x - XO] = new[YO : YO + SIZE_Y, :]

    sweeps(first, second, zfirst, zsecond, forcing, coef, zforcing, zcoef, gz, channels, planes, finish)
    layers = out_ref[...].reshape(-1, out_ref.shape[3])
    density = density_of(layers, near_own[6, 1:2, :].astype(jnp.int32), place_ref[2], channels)
    for brick in range(density_ref.shape[0]):
        density_ref[brick] = density


def near_kernel(place_ref, parts_ref, targets_ref, near_ref, own_ref):
    col, gz = place_ref[0], place_ref[1]
    cols = targets_ref.shape[0] // 2
    slots = targets_ref.shape[2]
    lane = lanes((8, slots))
    near_ref[6] = jnp.zeros((8, slots), jnp.float32)
    for n in range(6):
        side = jnp.clip(col + n % 3 - 1, 0, cols - 1)
        half = gz if n < 3 else 1 - gz
        about = targets_ref[side * 2 + half]
        total = parts_ref[0, n]
        for sender in range(1, parts_ref.shape[0]):
            total = total + parts_ref[sender, n]
        total = jnp.where(lane < about[4:5, :].astype(jnp.int32), total, 0.0)
        near_ref[n] = total
        near_ref[6, n : n + 1, :] = about[5:6, :]
        if n == 1:
            own_ref[...] = total


def last_kernel(place_ref, parts_ref, own_ref):
    total = parts_ref[0]
    for sender in range(1, parts_ref.shape[0]):
        total = total + parts_ref[sender]
    own_ref[...] = jnp.where(lanes(total.shape) < place_ref[2], total, 0.0)


def both_ways(up, down, axis):
    devices = lax.axis_size(axis)
    pairs = [(i, i + 1) for i in range(devices - 1)]
    return lax.ppermute(up, axis, pairs), lax.ppermute(down, axis, [(b, a) for a, b in pairs])


def local(
    initial_field, source_term, cell_class, class_shift, surface_cell, live_count, panel_geometry
):
    channels, size_x, size_y, size_z = initial_field.shape
    slots = surface_cell.shape[0]
    bricks = lax.axis_size("row")
    panels = slots * lax.axis_size("row") * lax.axis_size("col") * lax.axis_size("gz")
    factor = 1.0 / math.sqrt(panels)
    planes, rows = size_x + 2 * XO, size_y + 2 * YO
    frame, flat = (channels * planes * rows, 128), (planes * rows, 128)
    place = jnp.stack([lax.axis_index("col"), lax.axis_index("gz"), live_count[0]]).astype(jnp.int32)
    cells = surface_cell[None]
    vm = lambda shape, dtype=jnp.float32: pltpu.VMEM(shape, dtype)

    send_x = channels * 5 * size_y + 2 * size_y
    up, down, message = whole_call(
        functools.partial(planes_kernel, factor),
        (bf16(send_x, 128), bf16(send_x, 128), f32(bricks, 8, slots)),
        [vm(initial_field.shape), vm(initial_field.shape), vm((1, *cell_class.shape), jnp.int32),
         vm(panel_geometry.shape), vm(cells.shape, jnp.int32), pltpu.SemaphoreType.DMA((5,))],
        "planes", (live_count, class_shift), initial_field, source_term, cell_class[None], panel_geometry, cells,
        away=(0, 1, 2, 3, 4), megabytes=62,
    )
    kept = whole_call(
        own_kernel, f32(2 * frame[0] + 3 * flat[0], 128), [], "own", (),
        initial_field, source_term, cell_class[None],
    )
    low, high = both_ways(up, down, "row")
    kept, depth = whole_call(
        functools.partial(frame_kernel, True, channels),
        (f32(*kept.shape), bf16(planes * size_y, 128)), [], "frame", (place,),
        kept, low, high, aliases={0: 0},
    )
    other = lax.ppermute(depth, "gz", [(0, 1), (1, 0)])
    targets = lax.all_to_all(message, ("col", "gz"), 0, 0, tiled=True)
    other, targets = lax.optimization_barrier((other, targets))
    zframe, up, down = whole_call(
        functools.partial(edge_kernel, True), (f32(*flat), bf16(480, 128), bf16(480, 128)), [], "edges", (),
        kept, other,
    )
    low, high = both_ways(up, down, "col")
    smem = pl.BlockSpec(memory_space=pltpu.SMEM)
    vmem = pl.BlockSpec(memory_space=pltpu.VMEM)
    aims, note, table = pl.pallas_call(
        compact_kernel,
        in_specs=[smem, vmem],
        out_specs=(vmem, vmem, smem),
        out_shape=(f32(bricks + 2, 8, slots), f32(8, slots), jax.ShapeDtypeStruct((bricks + 1,), jnp.int32)),
        scratch_shapes=[vm((8, slots), jnp.int32), pltpu.SMEM((8, slots), jnp.int32), pltpu.SemaphoreType.DMA],
        compiler_params=params(4),
        name="compact",
    )(place, targets)
    low, high, aims, table = lax.optimization_barrier((low, high, aims, table))
    kept, up, down = whole_call(
        first_kernel,
        (f32(*kept.shape), bf16(channels * 3 * size_y, 128), bf16(channels * 3 * size_y, 128)),
        [vm(frame), vm(frame), vm(flat), vm(flat), vm(flat), vm(flat)], "first", (place,),
        kept, zframe, low, high, note, aliases={0: 0}, megabytes=8,
    )
    density = whole_call(
        functools.partial(density_kernel, channels), f32(bricks, 2 * channels, slots),
        [vm((channels * size_x * size_y, size_z))], "density", (place,), kept, note,
    )
    low, high = both_ways(up, down, "row")
    densities = lax.all_to_all(density, "row", 0, 0, tiled=True)
    done = make_tile(0, table, densities, aims, channels)
    low, high, done = lax.optimization_barrier((low, high, done))
    kept, depth = whole_call(
        functools.partial(frame_kernel, False, channels),
        (f32(*kept.shape), bf16(planes * size_y, 128)), [], "frame", (place,),
        kept, low, high, aliases={0: 0},
    )
    other = lax.ppermute(depth, "gz", [(0, 1), (1, 0)])
    densities, depth = lax.optimization_barrier((densities, depth))
    done = make_tile(1, table, densities, aims, channels, done)
    other, done = lax.optimization_barrier((other, done))
    zframe, up, down = whole_call(
        functools.partial(edge_kernel, False), (f32(*flat), bf16(288, 128), bf16(288, 128)), [], "edges", (),
        kept, other,
    )
    low, high = both_ways(up, down, "col")
    densities, up = lax.optimization_barrier((densities, up))
    tile, shares = make_tile(2, table, densities, aims, channels, done)
    shares = whole_call(arrange_kernel, f32(bricks, 6, channels, slots), [], "arrange", (table,), shares)
    parts = lax.all_to_all(shares, ("col", "gz"), 0, 0, tiled=True)
    near, _ = whole_call(near_kernel, (f32(7, channels, slots), f32(channels, slots)), [], "near", (place,), parts, targets)
    near_low, near_high = both_ways(near, near, "row")
    state, density = whole_call(
        second_kernel, (f32(*initial_field.shape), bf16(bricks, channels, slots)),
        [vm(frame), vm(frame), vm(flat), vm(flat), vm(frame), vm(flat)], "second", (place,),
        kept, zframe, low, high, near_low, near, near_high, megabytes=8,
    )
    densities = lax.all_to_all(density, "row", 0, 0, tiled=True)
    shares = products(table, densities, tile, 512)
    parts = lax.all_to_all(shares, ("col", "gz"), 0, 0, tiled=True)
    potential = whole_call(last_kernel, f32(channels, slots), [], "last", (place,), parts)
    return (state, potential)


def solution(mesh):
    placed = (
        P(None, "row", "col", "gz"),
        P(None, "row", "col", "gz"),
        P("row", "col", "gz"),
        P(),
        P(("row", "col", "gz")),
        P(("row", "col", "gz")),
        P(None, ("row", "col", "gz")),
    )
    return jax.shard_map(
        local,
        mesh=mesh,
        in_specs=placed,
        out_specs=(P(None, "row", "col", "gz"), P(None, ("row", "col", "gz"))),
        check_vma=False,
    )
```

```python
import functools
import math

import jax
import jax.numpy as jnp
from jax import lax
from jax.experimental import pallas as pl
from jax.experimental.pallas import tpu as pltpu
from jax.sharding import PartitionSpec as P

SIZE_Y = 16
CLASSES = 16
KEPT = 19
TILES = 3
ROOM = 8

relax_weight = 0.8
wave_number = 25.0
soften = 0.05
coupling = 0.5

SINE = (6.283164044297846, -41.33714237050646, 81.34076886863805, -70.99343309793157)
TURNS = wave_number / (2.0 * math.pi)


def from_everyone(x, axis):
    copies = jnp.broadcast_to(x, (lax.axis_size(axis), *x.shape))
    return lax.all_to_all(copies, axis, split_axis=0, concat_axis=0, tiled=True)


REACH = 3
XO, YO = 3, 4
SEND = 5


def lanes(shape):
    return lax.broadcasted_iota(jnp.int32, shape, len(shape) - 1)


def turned(x, shift):
    return pltpu.roll(x, shift % x.shape[-1], x.ndim - 1)


def params(megabytes):
    return pltpu.CompilerParams(vmem_limit_bytes=megabytes << 20)


def whole_call(kernel, out_shape, scratch, name, scalars, *operands, megabytes=4, away=(), aliases={}):
    smem = pl.BlockSpec(memory_space=pltpu.SMEM)
    vmem = pl.BlockSpec(memory_space=pltpu.VMEM)
    far = pl.BlockSpec(memory_space=pltpu.HBM)
    return pl.pallas_call(
        kernel,
        in_specs=[smem] * len(scalars) + [far if n in away else vmem for n in range(len(operands))],
        out_specs=jax.tree.map(lambda _: vmem, out_shape),
        out_shape=out_shape,
        scratch_shapes=scratch,
        compiler_params=params(megabytes),
        input_output_aliases={len(scalars) + k: v for k, v in aliases.items()},
        name=name,
    )(*scalars, *operands)


def f32(*shape):
    return jax.ShapeDtypeStruct(shape, jnp.float32)


def bf16(*shape):
    return jax.ShapeDtypeStruct(shape, jnp.bfloat16)


def split(x):
    high = x.astype(jnp.bfloat16)
    return high, (x - high.astype(jnp.float32)).astype(jnp.bfloat16)


def across(a, b):
    return lax.dot_general(a, b, (((1,), (1,)), ((), ())), preferred_element_type=jnp.float32)


def compact_kernel(target_ref, target_out, note_ref, table_ref, counts, table, arrived):
    bricks, depth, slots = target_ref.shape
    lane = lanes((depth, slots))
    first = jnp.zeros((depth, slots), jnp.float32)
    for brick in range(bricks):
        first = jnp.where(lane == brick, target_ref[brick, 4:5, :], first)
    counts[...] = first.astype(jnp.int32)
    copy = pltpu.make_async_copy(counts, table, arrived)
    copy.start()
    target_out[...] = jnp.zeros_like(target_out)
    note_ref[...] = target_ref[lax.axis_index("col") * 2 + lax.axis_index("gz")]
    copy.wait()
    begin = jnp.int32(0)
    for brick in range(bricks):
        append(target_out, target_ref[brick], begin, table[0, brick])
        table_ref[brick] = begin
        begin = begin + table[0, brick]
    table_ref[bricks] = begin


def append(out, rows, begin, count):
    group, shift = begin >> 7, begin & 127
    lane = lanes(rows.shape)
    moved = pltpu.roll(rows, shift, 1)
    out[group] = jnp.where((lane >= shift) & (lane < shift + count), moved, out[group])
    out[group + 1] = jnp.where(lane < shift + count - rows.shape[1], moved, out[group + 1])


def tile_kernel(part, table_ref, source_ref, target_ref, *refs):
    tile_ref, share_ref, columns, density = refs[-4:]
    bricks, slots = source_ref.shape[0], source_ref.shape[2]
    channels = share_ref.shape[1]
    step = pl.program_id(0)

    @pl.when(step == 0)
    def _():
        for brick in range(bricks):
            density[:, brick * slots : (brick + 1) * slots] = source_ref[brick, :channels].astype(jnp.bfloat16)

    @pl.when((TILES * step + part) * slots < table_ref[bricks])
    def _():
        columns[...] = jnp.transpose(target_ref[0])
        spread = [jnp.broadcast_to(columns[:, d : d + 1], (slots, slots)) for d in range(3)]
        total = jnp.zeros((channels, slots), jnp.float32)
        for pair in range(0, bricks, 2):
            both = []
            for brick in (pair, pair + 1):
                delta = [spread[d] - source_ref[brick, channels + d : channels + d + 1, :] for d in range(3)]
                square = delta[0] * delta[0] + (delta[1] * delta[1] + (delta[2] * delta[2] + 1e-30))
                turns = square * lax.rsqrt(square)
                angle = 0.25 - jnp.abs(turns - jnp.round(turns))
                angle2 = angle * angle
                wave = SINE[-1]
                for c in SINE[-2::-1]:
                    wave = wave * angle2 + c
                weight = source_ref[brick, channels + 3 : channels + 4, :]
                value = (angle * weight) * wave / (turns + soften * TURNS)
                both.append(value.astype(jnp.bfloat16))
                tile_ref[:, brick * slots : (brick + 1) * slots] = both[-1]
            at = slice(pair * slots, (pair + 2) * slots)
            total = total + across(density[:, at], jnp.concatenate(both, axis=1))
        share_ref[0] = total


def make_tile(part, table, sources, targets, channels, before=()):
    bricks, slots = sources.shape[0], sources.shape[2]
    far = pl.BlockSpec(memory_space=pl.ANY)
    return pl.pallas_call(
        functools.partial(tile_kernel, part),
        grid=(-(-bricks // TILES),),
        in_specs=[
            pl.BlockSpec(memory_space=pltpu.SMEM),
            pl.BlockSpec(sources.shape, lambda b: (0, 0, 0)),
            pl.BlockSpec((1, targets.shape[1], slots), lambda b: (TILES * b + part, 0, 0)),
        ]
        + [far] * len(before),
        out_specs=[
            pl.BlockSpec((slots, bricks * slots), lambda b: (TILES * b + part, 0)),
            pl.BlockSpec((1, channels, slots), lambda b: (TILES * b + part, 0, 0)),
        ],
        out_shape=[
            jax.ShapeDtypeStruct((ROOM * bricks * slots, bricks * slots), jnp.bfloat16),
            jax.ShapeDtypeStruct((bricks + 2, channels, slots), jnp.float32),
        ],
        scratch_shapes=[
            pltpu.VMEM((slots, targets.shape[1]), jnp.float32),
            pltpu.VMEM((channels, bricks * slots), jnp.bfloat16),
        ],
        input_output_aliases={3 + n: n for n in range(len(before))},
        compiler_params=params(8),
        name="tile",
    )(table, sources, targets, *before)


def taken(share_ref, table_ref, brick, bricks):
    begin = table_ref[brick]
    count = table_ref[brick + 1] - begin
    group, shift = begin >> 7, begin & 127
    lane = lanes(share_ref.shape[1:])
    slots = share_ref.shape[2]
    this = pltpu.roll(share_ref[group], (slots - shift) & 127, 1)
    following = pltpu.roll(share_ref[jnp.minimum(group + 1, bricks - 1)], (slots - shift) & 127, 1)
    return jnp.where(lane < count, jnp.where(lane < slots - shift, this, following), 0.0)


def arrange_kernel(table_ref, share_ref, out_ref):
    bricks = out_ref.shape[0]
    for index in range(bricks):
        value = taken(share_ref, table_ref, index, bricks)
        for n in range(6):
            side, other = index // 2 - (n % 3 - 1), (index + n // 3) % 2
            if 0 <= side < bricks // 2:
                out_ref[side * 2 + other, n] = value
    for brick in range(bricks):
        for n in range(6):
            if not 0 <= brick // 2 + n % 3 - 1 < bricks // 2:
                out_ref[brick, n] = jnp.zeros(out_ref.shape[2:], jnp.float32)


def product_kernel(table_ref, density_ref, tile_ref, out_ref, density, shares):
    bricks, channels, slots = density_ref.shape
    step = pl.program_id(0)
    count = tile_ref.shape[0] // slots

    @pl.when(step == 0)
    def _():
        for brick in range(bricks):
            density[:, brick * slots : (brick + 1) * slots] = density_ref[brick]

    @pl.when(step * count * slots < table_ref[bricks])
    def _():
        total = across(density[...], tile_ref[...])
        for index in range(count):
            shares[step * count + index] = total[:, index * slots : (index + 1) * slots]

    @pl.when(step == pl.num_programs(0) - 1)
    def _():
        for brick in range(bricks):
            out_ref[brick] = taken(shares, table_ref, brick, bricks)


def products(table, density, tile, rows):
    bricks, channels, slots = density.shape
    width = tile.shape[1]
    steps = bricks * slots // rows

    def block(b, table_ref):
        last = (table_ref[bricks] + rows - 1) // rows - 1
        return jnp.minimum(b, last), 0

    return pl.pallas_call(
        product_kernel,
        grid_spec=pltpu.PrefetchScalarGridSpec(
            num_scalar_prefetch=1,
            grid=(steps,),
            in_specs=[pl.BlockSpec(density.shape, lambda b, t: (0, 0, 0)), pl.BlockSpec((rows, width), block)],
            out_specs=pl.BlockSpec((bricks, channels, slots), lambda b, t: (0, 0, 0)),
            scratch_shapes=[
                pltpu.VMEM((channels, width), jnp.bfloat16),
                pltpu.VMEM((bricks, channels, slots), jnp.float32),
            ],
        ),
        out_shape=jax.ShapeDtypeStruct((bricks, channels, slots), jnp.float32),
        compiler_params=params(12),
        name="product",
    )(table, density, tile)


def put_planes(up_ref, down_ref, base, field_ref, depth, offset=0):
    size_x, size_y = field_ref.shape[-3], field_ref.shape[-2]
    for e in range(field_ref.shape[0]):
        for i in range(depth):
            rows = pl.ds(base + (e * depth + i) * size_y, size_y)
            high = field_ref[e, size_x - depth + i] + offset
            low = field_ref[e, i] + offset
            up_ref[rows, :] = high.astype(jnp.bfloat16)
            down_ref[rows, :] = low.astype(jnp.bfloat16)
    return base + field_ref.shape[0] * depth * size_y


def own_cells(frame_ref, field_ref, offset=0):
    channels, size_x, size_y = field_ref.shape[:3]
    planes, rows = size_x + 2 * XO, size_y + 2 * YO
    frame_ref[...] = jnp.zeros_like(frame_ref)
    for e in range(channels):
        for x in range(size_x):
            at = (e * planes + XO + x) * rows + YO
            frame_ref[at : at + size_y, :] = field_ref[e, x].astype(jnp.float32) + offset


def put_framed_planes(up_ref, down_ref, frame_ref, channels, depth):
    rows = SIZE_Y + 2 * YO
    planes = frame_ref.shape[0] // (channels * rows)
    for e in range(channels):
        for i in range(depth):
            here = pl.ds((e * depth + i) * SIZE_Y, SIZE_Y)
            high = (e * planes + planes - XO - depth + i) * rows + YO
            low = (e * planes + XO + i) * rows + YO
            up_ref[here, :] = frame_ref[high : high + SIZE_Y, :].astype(jnp.bfloat16)
            down_ref[here, :] = frame_ref[low : low + SIZE_Y, :].astype(jnp.bfloat16)


def planes_kernel(
    factor, state_hbm, source_hbm, class_hbm, geometry_hbm, cell_hbm, live_hbm, shift_hbm,
    up_ref, down_ref, message_ref, state_ref, source_ref, class_ref, geometry_ref, cell_ref, live_ref, shift_ref, arrived,
):
    pairs = (
        (live_hbm, live_ref), (shift_hbm, shift_ref), (geometry_hbm, geometry_ref), (cell_hbm, cell_ref),
        (state_hbm, state_ref), (source_hbm, source_ref), (class_hbm, class_ref),
    )
    copies = [pltpu.make_async_copy(a, b, arrived.at[n]) for n, (a, b) in enumerate(pairs)]
    for copy in copies:
        copy.start()
    slots = cell_ref.shape[1]
    for copy in copies[:4]:
        copy.wait()
    shifts = jnp.zeros((1, slots), jnp.float32)
    for index in range(CLASSES):
        shifts = jnp.where(lanes((1, slots)) == index, shift_ref[index], shifts)
    message = jnp.concatenate(
        [
            geometry_ref[:3] * TURNS,
            geometry_ref[3:] * (factor * TURNS),
            jnp.full((1, slots), live_ref[0], jnp.int32).astype(jnp.float32),
            cell_ref[...].astype(jnp.float32),
            shifts,
            jnp.zeros((1, slots), jnp.float32),
        ],
        axis=0,
    )
    for brick in range(message_ref.shape[0]):
        message_ref[brick] = message
    for copy in copies[4:]:
        copy.wait()
    base = put_planes(up_ref, down_ref, 0, state_ref, 3)
    base = put_planes(up_ref, down_ref, base, source_ref, 2)
    put_planes(up_ref, down_ref, base, class_ref, 2, 1.0)


def own_kernel(state_ref, source_ref, class_ref, kept_ref):
    frame_ref, forcing_ref, code_ref, _, _ = parted(kept_ref)
    own_cells(frame_ref, state_ref)
    own_cells(forcing_ref, source_ref)
    own_cells(code_ref, class_ref, 1.0)


def beside(frame_ref, channels, low_ref, high_ref, base, depth):
    rows = SIZE_Y + 2 * YO
    planes = frame_ref.shape[0] // (channels * rows)
    size_x = planes - 2 * XO
    for e in range(channels):
        for i in range(depth):
            here = pl.ds(base + (e * depth + i) * SIZE_Y, SIZE_Y)
            at = (e * planes + XO - depth + i) * rows + YO
            frame_ref[at : at + SIZE_Y, :] = low_ref[here, :].astype(jnp.float32)
            at = (e * planes + XO + size_x + i) * rows + YO
            frame_ref[at : at + SIZE_Y, :] = high_ref[here, :].astype(jnp.float32)
    return base + channels * depth * SIZE_Y


def depth_rows(frames, gz, x, size_y, rows, planes, channels):
    lane = lanes((size_y, 128))
    out = jnp.zeros((size_y, 128), jnp.float32)
    for e in range(channels):
        for index, frame_ref in enumerate(frames):
            own = frame_ref.shape[0] == planes * rows
            at = ((0 if own else e) * planes + x) * rows + YO
            start = e * 16 + index * SEND + 1
            moved = turned(frame_ref[at : at + size_y, :], start + 3 - 3 * gz)
            out = jnp.where((lane >= start) & (lane < start + 3), moved, out)
    return out


def frame_kernel(full, channels, _, low_ref, high_ref, kept_ref, depth_ref):
    frame_ref, forcing_ref, code_ref, _, _ = parted(kept_ref)
    rows = SIZE_Y + 2 * YO
    planes = frame_ref.shape[0] // (channels * rows)
    base = beside(frame_ref, channels, low_ref, high_ref, 0, 3)
    frames = [frame_ref]
    if full:
        base = beside(forcing_ref, channels, low_ref, high_ref, base, 2)
        beside(code_ref, 1, low_ref, high_ref, base, 2)
        frames = [frame_ref, forcing_ref, code_ref]
    gz = lax.axis_index("gz")
    for x in range(planes):
        out = depth_rows(frames, gz, x, SIZE_Y, rows, planes, channels)
        depth_ref[x * SIZE_Y : (x + 1) * SIZE_Y, :] = out.astype(jnp.bfloat16)


def edge_kernel(full, kept_ref, other_ref, depth_ref, up_ref, down_ref):
    frame_ref, forcing_ref, code_ref, _, _ = parted(kept_ref)
    rows = SIZE_Y + 2 * YO
    planes = depth_ref.shape[0] // rows
    depth_ref[...] = jnp.zeros_like(depth_ref)
    for x in range(planes):
        here = other_ref[x * SIZE_Y : (x + 1) * SIZE_Y, :].astype(jnp.float32)
        depth_ref[x * rows + YO : x * rows + YO + SIZE_Y, :] = here

    def put(base, ref, depth, step):
        count = ref.shape[0] // rows
        for j in range(depth):
            high = ref[pl.ds(YO + SIZE_Y - depth + j, count, stride=rows), :]
            low = ref[pl.ds(YO + j, count, stride=rows), :]
            up_ref[base + j * step : base + j * step + count, :] = high.astype(jnp.bfloat16)
            down_ref[base + j * step : base + j * step + count, :] = low.astype(jnp.bfloat16)
        return base + depth * step

    if full:
        up_ref[edge_tail(full) :, :] = jnp.zeros((80, 128), jnp.bfloat16)
        down_ref[edge_tail(full) :, :] = jnp.zeros((80, 128), jnp.bfloat16)
    else:
        up_ref[edge_tail(full) :, :] = jnp.zeros((48, 128), jnp.bfloat16)
        down_ref[edge_tail(full) :, :] = jnp.zeros((48, 128), jnp.bfloat16)
    base = put(0, frame_ref, 3, 80)
    if full:
        base = put(base, forcing_ref, 2, 80)
        base = put(base, code_ref, 2, 16)
    put(base, depth_ref, 3, 16)


def edge_tail(full):
    return 400 if full else 240


def take_edges(frame_ref, low_ref, high_ref, base, depth, step):
    rows = SIZE_Y + 2 * YO
    count = frame_ref.shape[0] // rows
    for j in range(depth):
        low = low_ref[base + j * step : base + j * step + count, :].astype(jnp.float32)
        high = high_ref[base + j * step : base + j * step + count, :].astype(jnp.float32)
        frame_ref[pl.ds(YO - depth + j, count, stride=rows), :] = low
        frame_ref[pl.ds(YO + SIZE_Y + j, count, stride=rows), :] = high
    return base + depth * step


def faces(get, e_range, gz, shape):
    lane = lanes(shape)
    out = jnp.zeros(shape, jnp.float32)
    for e in e_range:
        out = jnp.where(lane == e * 16 + 4 * gz, turned(get(e), e * 16 + 1 + 3 * gz), out)
    return out


def sweep(src, dst, zsrc, zdst, forcing, coef, zforcing, zcoef, gz, x_low, x_high, channels, planes, finish=None):
    rows = SIZE_Y + 2 * YO
    shape = (rows, 128)
    lane = lanes(shape)
    keep = 1.0 - relax_weight
    inner_low = (lane > 0).astype(jnp.float32)
    inner_high = (lane < 127).astype(jnp.float32)
    border = (lane == 127 - 127 * gz).astype(jnp.float32)
    face_lane = (lane & 15) == 4 * gz

    def one_plane(x, carry):
        at = pl.multiple_of(x * rows, 8)
        other = zsrc[pl.ds(at, rows), :]
        weight = coef[pl.ds(at, rows), :]
        fresh = []
        for e in range(channels):
            row = pl.multiple_of((e * planes + x) * rows, 8)
            own = src[pl.ds(row, rows), :]
            total = src[pl.ds(row + rows, rows), :] + src[pl.ds(row - rows, rows), :]
            total = total + pltpu.roll(own, rows - 1, 0) + pltpu.roll(own, 1, 0)
            total = total + pltpu.roll(own, 127, 1) * inner_high + pltpu.roll(own, 1, 1) * inner_low
            total = total + turned(other, 126 - gz - 16 * e + 256) * border
            new = keep * own + weight * (forcing[pl.ds(row, rows), :] + total)
            if finish is None:
                dst[pl.ds(row, rows), :] = new
            else:
                finish(e, x, new)
            fresh.append(new)
        if finish is None:
            total = zsrc[pl.ds(at + rows, rows), :] + zsrc[pl.ds(at - rows, rows), :]
            total = total + pltpu.roll(other, rows - 1, 0) + pltpu.roll(other, 1, 0)
            total = total + pltpu.roll(other, 127, 1) + pltpu.roll(other, 1, 1)
            new = keep * other + zcoef[pl.ds(at, rows), :] * (zforcing[pl.ds(at, rows), :] + total)
            face = faces(lambda e: fresh[e], range(channels), gz, shape)
            zdst[pl.ds(at, rows), :] = jnp.where(face_lane, face, new)
        return carry

    lax.fori_loop(x_low, x_high, one_plane, 0, unroll=True)


def sweeps(frame, second, zframe, zsecond, forcing, coef, zforcing, zcoef, gz, channels, planes, finish):
    rows = SIZE_Y + 2 * YO
    face_lane = (lanes((rows, 128)) & 15) == 4 * gz
    for x in range(planes):
        face = faces(lambda e: frame[(e * planes + x) * rows : (e * planes + x + 1) * rows, :], range(channels), gz, (rows, 128))
        here = zframe[x * rows : (x + 1) * rows, :]
        zframe[x * rows : (x + 1) * rows, :] = jnp.where(face_lane, face, here)
    sweep(frame, second, zframe, zsecond, forcing, coef, zforcing, zcoef, gz, 1, planes - 1, channels, planes)
    sweep(second, frame, zsecond, zframe, forcing, coef, zforcing, zcoef, gz, 2, planes - 2, channels, planes)

    sweep(frame, None, zframe, None, forcing, coef, zforcing, zcoef, gz, XO, planes - XO, channels, planes, finish)


def density_of(layers, cell, live, channels):
    slots, size_z = cell.shape[1], layers.shape[1]
    pick = (lax.broadcasted_iota(jnp.int32, (size_z, slots), 0) == (cell & (size_z - 1))).astype(jnp.bfloat16)
    count = layers.shape[0] // channels
    lines = jnp.dot(layers.astype(jnp.bfloat16), pick, preferred_element_type=jnp.float32)
    used = lanes((count, slots)) < live.astype(jnp.int32)
    mask = used & (lax.broadcasted_iota(jnp.int32, (count, slots), 0) == (cell >> 7))
    found = [
        jnp.sum(jnp.where(mask, lines[e * count : (e + 1) * count, :], 0.0), axis=0, keepdims=True)
        for e in range(channels)
    ]
    return jnp.concatenate(found, axis=0).astype(jnp.bfloat16)


def parted(kept_ref):
    rows = kept_ref.shape[0] // KEPT
    frame = (KEPT - 3) // 2 * rows
    ends = [0, frame, 2 * frame] + [2 * frame + n * rows for n in range(1, 4)]
    return [kept_ref.at[ends[n] : ends[n + 1]] for n in range(5)]


def first_kernel(
    _, depth_ref, low_ref, high_ref, note_ref,
    kept_ref, density_ref, up_ref, down_ref, first, second, zfirst, zsecond, code, zcode, layers,
):
    gz = lax.axis_index("gz")
    rows = SIZE_Y + 2 * YO
    planes = depth_ref.shape[0] // rows
    state, forcing, coef, zforcing, zcoef = parted(kept_ref)
    channels = first.shape[0] // (planes * rows)
    first[...] = state[...]
    code[...] = coef[...]
    zcode[...] = depth_ref[...]
    base = take_edges(first, low_ref, high_ref, 0, 3, 80)
    base = take_edges(forcing, low_ref, high_ref, base, 2, 80)
    base = take_edges(code, low_ref, high_ref, base, 2, 16)
    take_edges(zcode, low_ref, high_ref, base, 3, 16)
    lane = lanes((rows, 128)) & 15
    outer = (lane >= 1) & (lane <= 3)
    shifts = [jnp.broadcast_to(note_ref[6:7, n : n + 1], (rows, 128)) for n in range(CLASSES)]
    for x in range(planes):
        here = pl.ds(x * rows, rows)
        packed = zcode[here, :]
        zfirst[here, :] = jnp.where(outer, packed, 0.0)
        zforcing[here, :] = jnp.where(outer, turned(packed, 128 - SEND), 0.0)
        level = jnp.where(outer, turned(packed, 128 - 2 * SEND), 0.0)
        own_level = code[here, :]
        zshift = jnp.zeros((rows, 128), jnp.float32)
        shift = jnp.zeros((rows, 128), jnp.float32)
        for index in range(CLASSES):
            zshift = jnp.where(level == index + 1.0, shifts[index], zshift)
            shift = jnp.where(own_level == index + 1.0, shifts[index], shift)
        zcoef[here, :] = jnp.where(level > 0.0, relax_weight / (6.0 + zshift), 0.0)
        coef[here, :] = jnp.where(own_level > 0.0, relax_weight / (6.0 + shift), 0.0)

    def finish(e, x, new):
        own = new[YO : YO + SIZE_Y, :]
        state[pl.ds((e * planes + x) * rows + YO, SIZE_Y), :] = own
        layers[pl.ds((e * (planes - 2 * XO) + x - XO) * SIZE_Y, SIZE_Y), :] = own

    sweeps(first, second, zfirst, zsecond, forcing, coef, zforcing, zcoef, gz, channels, planes, finish)
    put_framed_planes(up_ref, down_ref, state, channels, 3)
    density = density_of(layers[...], note_ref[5:6, :].astype(jnp.int32), note_ref[4:5, :], channels)
    message = jnp.concatenate([density.astype(jnp.float32), note_ref[...]], axis=0)
    for brick in range(density_ref.shape[0]):
        density_ref[brick] = message


def add_load(forcing, zforcing, near_ref, side, gz, channels, planes):
    rows = SIZE_Y + 2 * YO
    size_x = planes - 2 * XO
    cells = near_ref[6].astype(jnp.int32)
    slots = cells.shape[1]
    wide = 3 * slots

    def row_of(first):
        cell = jnp.concatenate([cells[first + n : first + n + 1, :] for n in range(3)], axis=1)
        shift = jnp.concatenate([jnp.full((1, slots), YO + SIZE_Y * (n - 1), jnp.int32) for n in range(3)], axis=1)
        value = coupling * jnp.concatenate([near_ref[first + n] for n in range(3)], axis=1)
        return cell & 127, ((cell >> 7) & (SIZE_Y - 1)) + shift, cell >> 11, value

    span = {-1: range(size_x - 2, size_x), 0: range(size_x), 1: range(2)}[side]
    level = lax.broadcasted_iota(jnp.int32, (rows, wide), 0)
    z, y, x, value = row_of(0)
    pick = (lax.broadcasted_iota(jnp.int32, (128, wide), 0) == z).astype(jnp.bfloat16)
    for plane in span:
        mask = (level == y) & (x == plane)
        spread = jnp.concatenate([jnp.where(mask, value[e : e + 1, :], 0.0) for e in range(channels)], axis=0)
        high, low = split(spread)
        load = across(high, pick) + across(low, pick)
        at = plane + XO + size_x * side
        for e in range(channels):
            row = (e * planes + at) * rows
            forcing[row : row + rows, :] += load[e * rows : (e + 1) * rows, :]
    z, y, x, value = row_of(3)
    lane = z - 125 * gz + 1
    step = lax.broadcasted_iota(jnp.int32, (16, wide), 0)
    ok = (step == lane) & (step >= 1) & (step <= 3)
    spread = jnp.concatenate([jnp.where(ok, value[e : e + 1, :], 0.0) for e in range(channels)], axis=0)
    high, low = split(spread)
    for plane in span:
        mask = ((level == y) & (x == plane)).astype(jnp.bfloat16)
        row = (plane + XO + size_x * side) * rows
        zforcing[row : row + rows, :] += across(mask, high) + across(mask, low)


def second_kernel(
    kept_ref, depth_ref, low_ref, high_ref, near_low, near_own, near_high,
    out_ref, density_ref, first, second, zfirst, zsecond, forcing, zforcing,
):
    gz = lax.axis_index("gz")
    rows = SIZE_Y + 2 * YO
    planes = depth_ref.shape[0] // rows
    channels = out_ref.shape[0]
    state, old, coef, zold, zcoef = parted(kept_ref)
    first[...] = state[...]
    zfirst[...] = depth_ref[...]
    forcing[...] = old[...]
    zforcing[...] = zold[...]
    base = take_edges(first, low_ref, high_ref, 0, 3, 80)
    take_edges(zfirst, low_ref, high_ref, base, 3, 16)
    for side, near in ((-1, near_low), (0, near_own), (1, near_high)):
        add_load(forcing, zforcing, near, side, gz, channels, planes)

    def finish(e, x, new):
        out_ref[e, x - XO] = new[YO : YO + SIZE_Y, :]

    sweeps(first, second, zfirst, zsecond, forcing, coef, zforcing, zcoef, gz, channels, planes, finish)
    layers = out_ref[...].reshape(-1, out_ref.shape[3])
    density = density_of(layers, near_own[6, 1:2, :].astype(jnp.int32), near_own[6, 7:8, :], channels)
    for brick in range(density_ref.shape[0]):
        density_ref[brick] = density


def near_kernel(parts_ref, targets_ref, near_ref):
    col, gz = lax.axis_index("col"), lax.axis_index("gz")
    cols = targets_ref.shape[0] // 2
    slots = targets_ref.shape[2]
    lane = lanes((8, slots))
    near_ref[6] = jnp.zeros((8, slots), jnp.float32)
    for n in range(6):
        side = jnp.clip(col + n % 3 - 1, 0, cols - 1)
        half = gz if n < 3 else 1 - gz
        about = targets_ref[side * 2 + half]
        total = parts_ref[0, n]
        for sender in range(1, parts_ref.shape[0]):
            total = total + parts_ref[sender, n]
        total = jnp.where(lane < about[4:5, :].astype(jnp.int32), total, 0.0)
        near_ref[n] = total
        near_ref[6, n : n + 1, :] = about[5:6, :]
        if n == 1:
            near_ref[6, 7:8, :] = about[4:5, :]


def last_kernel(parts_ref, own_ref):
    total = parts_ref[0]
    for sender in range(1, parts_ref.shape[0]):
        total = total + parts_ref[sender]
    own_ref[...] = total


def both_ways(up, down, axis):
    devices = lax.axis_size(axis)
    pairs = [(i, i + 1) for i in range(devices - 1)]
    return lax.ppermute(up, axis, pairs), lax.ppermute(down, axis, [(b, a) for a, b in pairs])


def local(
    initial_field, source_term, cell_class, class_shift, surface_cell, live_count, panel_geometry
):
    channels, size_x, size_y, size_z = initial_field.shape
    slots = surface_cell.shape[0]
    bricks = lax.axis_size("row")
    panels = slots * lax.axis_size("row") * lax.axis_size("col") * lax.axis_size("gz")
    factor = 1.0 / math.sqrt(panels)
    planes, rows = size_x + 2 * XO, size_y + 2 * YO
    frame, flat = (channels * planes * rows, 128), (planes * rows, 128)
    cells = surface_cell[None]
    vm = lambda shape, dtype=jnp.float32: pltpu.VMEM(shape, dtype)

    send_x = channels * 5 * size_y + 2 * size_y
    up, down, message = whole_call(
        functools.partial(planes_kernel, factor),
        (bf16(send_x, 128), bf16(send_x, 128), f32(bricks, 8, slots)),
        [vm(initial_field.shape), vm(initial_field.shape), vm((1, *cell_class.shape), jnp.int32),
         vm(panel_geometry.shape), vm(cells.shape, jnp.int32), pltpu.SMEM((1,), jnp.int32), pltpu.SMEM((CLASSES,), jnp.float32),
         pltpu.SemaphoreType.DMA((7,))],
        "planes", (), initial_field, source_term, cell_class[None], panel_geometry, cells, live_count, class_shift,
        away=(0, 1, 2, 3, 4, 5, 6), megabytes=62,
    )
    kept = whole_call(
        own_kernel, f32(2 * frame[0] + 3 * flat[0], 128), [], "own", (),
        initial_field, source_term, cell_class[None],
    )
    low, high = both_ways(up, down, "row")
    kept, depth = whole_call(
        functools.partial(frame_kernel, True, channels),
        (f32(*kept.shape), bf16(planes * size_y, 128)), [], "frame", (),
        kept, low, high, aliases={0: 0},
    )
    other = lax.ppermute(depth, "gz", [(0, 1), (1, 0)])
    targets = lax.all_to_all(message, ("col", "gz"), 0, 0, tiled=True)
    other, targets = lax.optimization_barrier((other, targets))
    zframe, up, down = whole_call(
        functools.partial(edge_kernel, True), (f32(*flat), bf16(480, 128), bf16(480, 128)), [], "edges", (),
        kept, other,
    )
    low, high = both_ways(up, down, "col")
    smem = pl.BlockSpec(memory_space=pltpu.SMEM)
    vmem = pl.BlockSpec(memory_space=pltpu.VMEM)
    aims, note, table = pl.pallas_call(
        compact_kernel,
        in_specs=[vmem],
        out_specs=(vmem, vmem, smem),
        out_shape=(f32(bricks + 2, 8, slots), f32(8, slots), jax.ShapeDtypeStruct((bricks + 1,), jnp.int32)),
        scratch_shapes=[vm((8, slots), jnp.int32), pltpu.SMEM((8, slots), jnp.int32), pltpu.SemaphoreType.DMA],
        compiler_params=params(4),
        name="compact",
    )(targets)
    low, high, aims, table = lax.optimization_barrier((low, high, aims, table))
    kept, density, up, down = whole_call(
        first_kernel,
        (f32(*kept.shape), f32(bricks, 2 * channels, slots),
         bf16(channels * 3 * size_y, 128), bf16(channels * 3 * size_y, 128)),
        [vm(frame), vm(frame), vm(flat), vm(flat), vm(flat), vm(flat),
         vm((channels * size_x * size_y, size_z))], "first", (),
        kept, zframe, low, high, note, aliases={0: 0}, megabytes=8,
    )
    low, high = both_ways(up, down, "row")
    densities = lax.all_to_all(density, "row", 0, 0, tiled=True)
    done = make_tile(0, table, densities, aims, channels)
    low, high, done = lax.optimization_barrier((low, high, done))
    kept, depth = whole_call(
        functools.partial(frame_kernel, False, channels),
        (f32(*kept.shape), bf16(planes * size_y, 128)), [], "frame", (),
        kept, low, high, aliases={0: 0},
    )
    other = lax.ppermute(depth, "gz", [(0, 1), (1, 0)])
    densities, depth = lax.optimization_barrier((densities, depth))
    done = make_tile(1, table, densities, aims, channels, done)
    other, done = lax.optimization_barrier((other, done))
    zframe, up, down = whole_call(
        functools.partial(edge_kernel, False), (f32(*flat), bf16(288, 128), bf16(288, 128)), [], "edges", (),
        kept, other,
    )
    low, high = both_ways(up, down, "col")
    densities, up = lax.optimization_barrier((densities, up))
    tile, shares = make_tile(2, table, densities, aims, channels, done)
    shares = whole_call(arrange_kernel, f32(bricks, 6, channels, slots), [], "arrange", (table,), shares)
    parts = lax.all_to_all(shares, ("col", "gz"), 0, 0, tiled=True)
    near = whole_call(near_kernel, f32(7, channels, slots), [], "near", (), parts, targets)
    near_low, near_high = both_ways(near, near, "row")
    state, density = whole_call(
        second_kernel, (f32(*initial_field.shape), bf16(bricks, channels, slots)),
        [vm(frame), vm(frame), vm(flat), vm(flat), vm(frame), vm(flat)], "second", (),
        kept, zframe, low, high, near_low, near, near_high, megabytes=8,
    )
    densities = lax.all_to_all(density, "row", 0, 0, tiled=True)
    shares = products(table, densities, tile, 512)
    parts = lax.all_to_all(shares, ("col", "gz"), 0, 0, tiled=True)
    potential = whole_call(last_kernel, f32(channels, slots), [], "last", (), parts)
    return (state, potential)


def solution(mesh):
    placed = (
        P(None, "row", "col", "gz"),
        P(None, "row", "col", "gz"),
        P("row", "col", "gz"),
        P(),
        P(("row", "col", "gz")),
        P(("row", "col", "gz")),
        P(None, ("row", "col", "gz")),
    )
    return jax.shard_map(
        local,
        mesh=mesh,
        in_specs=placed,
        out_specs=(P(None, "row", "col", "gz"), P(None, ("row", "col", "gz"))),
        check_vma=False,
    )
```

```python
import functools
import math

import jax
import jax.numpy as jnp
from jax import lax
from jax.experimental import pallas as pl
from jax.experimental.pallas import tpu as pltpu
from jax.sharding import PartitionSpec as P

SIZE_Y = 16
CLASSES = 16
KEPT = 19
TILES = 3
ROOM = 8

relax_weight = 0.8
wave_number = 25.0
soften = 0.05
coupling = 0.5

SINE = (6.283164044297846, -41.33714237050646, 81.34076886863805, -70.99343309793157)
TURNS = wave_number / (2.0 * math.pi)


def from_everyone(x, axis):
    copies = jnp.broadcast_to(x, (lax.axis_size(axis), *x.shape))
    return lax.all_to_all(copies, axis, split_axis=0, concat_axis=0, tiled=True)


REACH = 3
XO, YO = 3, 4
SEND = 5


def lanes(shape):
    return lax.broadcasted_iota(jnp.int32, shape, len(shape) - 1)


def turned(x, shift):
    return pltpu.roll(x, shift % x.shape[-1], x.ndim - 1)


def params(megabytes):
    return pltpu.CompilerParams(vmem_limit_bytes=megabytes << 20)


def whole_call(kernel, out_shape, scratch, name, scalars, *operands, megabytes=4, away=(), aliases={}):
    smem = pl.BlockSpec(memory_space=pltpu.SMEM)
    vmem = pl.BlockSpec(memory_space=pltpu.VMEM)
    far = pl.BlockSpec(memory_space=pltpu.HBM)
    return pl.pallas_call(
        kernel,
        in_specs=[smem] * len(scalars) + [far if n in away else vmem for n in range(len(operands))],
        out_specs=jax.tree.map(lambda _: vmem, out_shape),
        out_shape=out_shape,
        scratch_shapes=scratch,
        compiler_params=params(megabytes),
        input_output_aliases={len(scalars) + k: v for k, v in aliases.items()},
        name=name,
    )(*scalars, *operands)


def f32(*shape):
    return jax.ShapeDtypeStruct(shape, jnp.float32)


def bf16(*shape):
    return jax.ShapeDtypeStruct(shape, jnp.bfloat16)


def split(x):
    high = x.astype(jnp.bfloat16)
    return high, (x - high.astype(jnp.float32)).astype(jnp.bfloat16)


def across(a, b):
    return lax.dot_general(a, b, (((1,), (1,)), ((), ())), preferred_element_type=jnp.float32)


def compact_kernel(target_ref, target_out, note_ref, table_ref, counts, table, arrived):
    bricks, depth, slots = target_ref.shape
    lane = lanes((depth, slots))
    first = jnp.zeros((depth, slots), jnp.float32)
    for brick in range(bricks):
        first = jnp.where(lane == brick, target_ref[brick, 4:5, :], first)
    counts[...] = first.astype(jnp.int32)
    copy = pltpu.make_async_copy(counts, table, arrived)
    copy.start()
    target_out[...] = jnp.zeros_like(target_out)
    note_ref[...] = target_ref[lax.axis_index("col") * 2 + lax.axis_index("gz")]
    copy.wait()
    begin = jnp.int32(0)
    for brick in range(bricks):
        append(target_out, target_ref[brick], begin, table[0, brick])
        table_ref[brick] = begin
        begin = begin + table[0, brick]
    table_ref[bricks] = begin


def append(out, rows, begin, count):
    group, shift = begin >> 7, begin & 127
    lane = lanes(rows.shape)
    moved = pltpu.roll(rows, shift, 1)
    out[group] = jnp.where((lane >= shift) & (lane < shift + count), moved, out[group])
    out[group + 1] = jnp.where(lane < shift + count - rows.shape[1], moved, out[group + 1])


def tile_kernel(source_ref, target_ref, *refs):
    tile_ref, share_ref, columns, density = refs[-4:]
    bricks, slots = source_ref.shape[0], source_ref.shape[2]
    channels = share_ref.shape[1]
    step = pl.program_id(0)

    @pl.when(step == 0)
    def _():
        for brick in range(bricks):
            density[:, brick * slots : (brick + 1) * slots] = source_ref[brick, :channels].astype(jnp.bfloat16)

    @pl.when(jnp.max(target_ref[0, 4:5, :]) > 0.0)
    def _():
        columns[...] = jnp.transpose(target_ref[0])
        spread = [jnp.broadcast_to(columns[:, d : d + 1], (slots, slots)) for d in range(3)]
        total = jnp.zeros((channels, slots), jnp.float32)
        for pair in range(0, bricks, 2):
            both = []
            for brick in (pair, pair + 1):
                delta = [spread[d] - source_ref[brick, channels + d : channels + d + 1, :] for d in range(3)]
                square = delta[0] * delta[0] + (delta[1] * delta[1] + (delta[2] * delta[2] + 1e-30))
                turns = square * lax.rsqrt(square)
                angle = 0.25 - jnp.abs(turns - jnp.round(turns))
                angle2 = angle * angle
                wave = SINE[-1]
                for c in SINE[-2::-1]:
                    wave = wave * angle2 + c
                weight = source_ref[brick, channels + 3 : channels + 4, :]
                value = (angle * weight) * wave / (turns + soften * TURNS)
                both.append(value.astype(jnp.bfloat16))
                tile_ref[:, brick * slots : (brick + 1) * slots] = both[-1]
            at = slice(pair * slots, (pair + 2) * slots)
            total = total + across(density[:, at], jnp.concatenate(both, axis=1))
        share_ref[0] = total


def make_tile(part, sources, targets, channels, before=()):
    bricks, slots = sources.shape[0], sources.shape[2]
    far = pl.BlockSpec(memory_space=pl.ANY)
    return pl.pallas_call(
        tile_kernel,
        grid=(-(-bricks // TILES),),
        in_specs=[
            pl.BlockSpec(sources.shape, lambda b: (0, 0, 0)),
            pl.BlockSpec((1, targets.shape[1], slots), lambda b: (TILES * b + part, 0, 0)),
        ]
        + [far] * len(before),
        out_specs=[
            pl.BlockSpec((slots, bricks * slots), lambda b: (TILES * b + part, 0)),
            pl.BlockSpec((1, channels, slots), lambda b: (TILES * b + part, 0, 0)),
        ],
        out_shape=[
            jax.ShapeDtypeStruct((ROOM * bricks * slots, bricks * slots), jnp.bfloat16),
            jax.ShapeDtypeStruct((bricks + 2, channels, slots), jnp.float32),
        ],
        scratch_shapes=[
            pltpu.VMEM((slots, targets.shape[1]), jnp.float32),
            pltpu.VMEM((channels, bricks * slots), jnp.bfloat16),
        ],
        input_output_aliases={2 + n: n for n in range(len(before))},
        compiler_params=params(8),
        name="tile",
    )(sources, targets, *before)


def taken(share_ref, table_ref, brick, bricks):
    begin = table_ref[brick]
    count = table_ref[brick + 1] - begin
    group, shift = begin >> 7, begin & 127
    lane = lanes(share_ref.shape[1:])
    slots = share_ref.shape[2]
    this = pltpu.roll(share_ref[group], (slots - shift) & 127, 1)
    following = pltpu.roll(share_ref[jnp.minimum(group + 1, bricks - 1)], (slots - shift) & 127, 1)
    return jnp.where(lane < count, jnp.where(lane < slots - shift, this, following), 0.0)


def arrange_kernel(table_ref, share_ref, out_ref):
    bricks = out_ref.shape[0]
    for index in range(bricks):
        value = taken(share_ref, table_ref, index, bricks)
        for n in range(6):
            side, other = index // 2 - (n % 3 - 1), (index + n // 3) % 2
            if 0 <= side < bricks // 2:
                out_ref[side * 2 + other, n] = value
    for brick in range(bricks):
        for n in range(6):
            if not 0 <= brick // 2 + n % 3 - 1 < bricks // 2:
                out_ref[brick, n] = jnp.zeros(out_ref.shape[2:], jnp.float32)


def product_kernel(table_ref, density_ref, tile_ref, out_ref, density, shares):
    bricks, channels, slots = density_ref.shape
    step = pl.program_id(0)
    count = tile_ref.shape[0] // slots

    @pl.when(step == 0)
    def _():
        for brick in range(bricks):
            density[:, brick * slots : (brick + 1) * slots] = density_ref[brick]

    @pl.when(step * count * slots < table_ref[bricks])
    def _():
        total = across(density[...], tile_ref[...])
        for index in range(count):
            shares[step * count + index] = total[:, index * slots : (index + 1) * slots]

    @pl.when(step == pl.num_programs(0) - 1)
    def _():
        for brick in range(bricks):
            out_ref[brick] = taken(shares, table_ref, brick, bricks)


def products(table, density, tile, rows):
    bricks, channels, slots = density.shape
    width = tile.shape[1]
    steps = bricks * slots // rows

    def block(b, table_ref):
        last = (table_ref[bricks] + rows - 1) // rows - 1
        return jnp.minimum(b, last), 0

    return pl.pallas_call(
        product_kernel,
        grid_spec=pltpu.PrefetchScalarGridSpec(
            num_scalar_prefetch=1,
            grid=(steps,),
            in_specs=[pl.BlockSpec(density.shape, lambda b, t: (0, 0, 0)), pl.BlockSpec((rows, width), block)],
            out_specs=pl.BlockSpec((bricks, channels, slots), lambda b, t: (0, 0, 0)),
            scratch_shapes=[
                pltpu.VMEM((channels, width), jnp.bfloat16),
                pltpu.VMEM((bricks, channels, slots), jnp.float32),
            ],
        ),
        out_shape=jax.ShapeDtypeStruct((bricks, channels, slots), jnp.float32),
        compiler_params=params(12),
        name="product",
    )(table, density, tile)


def put_planes(up_ref, down_ref, base, field_ref, depth, offset=0):
    size_x, size_y = field_ref.shape[-3], field_ref.shape[-2]
    for e in range(field_ref.shape[0]):
        for i in range(depth):
            rows = pl.ds(base + (e * depth + i) * size_y, size_y)
            high = field_ref[e, size_x - depth + i] + offset
            low = field_ref[e, i] + offset
            up_ref[rows, :] = high.astype(jnp.bfloat16)
            down_ref[rows, :] = low.astype(jnp.bfloat16)
    return base + field_ref.shape[0] * depth * size_y


def own_cells(frame_ref, field_ref, offset=0):
    channels, size_x, size_y = field_ref.shape[:3]
    planes, rows = size_x + 2 * XO, size_y + 2 * YO
    frame_ref[...] = jnp.zeros_like(frame_ref)
    for e in range(channels):
        for x in range(size_x):
            at = (e * planes + XO + x) * rows + YO
            frame_ref[at : at + size_y, :] = field_ref[e, x].astype(jnp.float32) + offset


def put_framed_planes(up_ref, down_ref, frame_ref, channels, depth):
    rows = SIZE_Y + 2 * YO
    planes = frame_ref.shape[0] // (channels * rows)
    for e in range(channels):
        for i in range(depth):
            here = pl.ds((e * depth + i) * SIZE_Y, SIZE_Y)
            high = (e * planes + planes - XO - depth + i) * rows + YO
            low = (e * planes + XO + i) * rows + YO
            up_ref[here, :] = frame_ref[high : high + SIZE_Y, :].astype(jnp.bfloat16)
            down_ref[here, :] = frame_ref[low : low + SIZE_Y, :].astype(jnp.bfloat16)


def planes_kernel(
    factor, state_hbm, source_hbm, class_hbm, geometry_hbm, cell_hbm, live_hbm, shift_hbm,
    up_ref, down_ref, message_ref, state_ref, source_ref, class_ref, geometry_ref, cell_ref, live_ref, shift_ref, arrived,
):
    pairs = (
        (live_hbm, live_ref), (shift_hbm, shift_ref), (geometry_hbm, geometry_ref), (cell_hbm, cell_ref),
        (state_hbm, state_ref), (source_hbm, source_ref), (class_hbm, class_ref),
    )
    copies = [pltpu.make_async_copy(a, b, arrived.at[n]) for n, (a, b) in enumerate(pairs)]
    for copy in copies:
        copy.start()
    slots = cell_ref.shape[1]
    for copy in copies[:4]:
        copy.wait()
    shifts = jnp.zeros((1, slots), jnp.float32)
    for index in range(CLASSES):
        shifts = jnp.where(lanes((1, slots)) == index, shift_ref[index], shifts)
    message = jnp.concatenate(
        [
            geometry_ref[:3] * TURNS,
            geometry_ref[3:] * (factor * TURNS),
            jnp.full((1, slots), live_ref[0], jnp.int32).astype(jnp.float32),
            cell_ref[...].astype(jnp.float32),
            shifts,
            jnp.zeros((1, slots), jnp.float32),
        ],
        axis=0,
    )
    for brick in range(message_ref.shape[0]):
        message_ref[brick] = message
    for copy in copies[4:]:
        copy.wait()
    base = put_planes(up_ref, down_ref, 0, state_ref, 3)
    base = put_planes(up_ref, down_ref, base, source_ref, 2)
    put_planes(up_ref, down_ref, base, class_ref, 2, 1.0)


def own_kernel(state_ref, source_ref, class_ref, kept_ref):
    frame_ref, forcing_ref, code_ref, _, _ = parted(kept_ref)
    own_cells(frame_ref, state_ref)
    own_cells(forcing_ref, source_ref)
    own_cells(code_ref, class_ref, 1.0)


def beside(frame_ref, channels, low_ref, high_ref, base, depth):
    rows = SIZE_Y + 2 * YO
    planes = frame_ref.shape[0] // (channels * rows)
    size_x = planes - 2 * XO
    for e in range(channels):
        for i in range(depth):
            here = pl.ds(base + (e * depth + i) * SIZE_Y, SIZE_Y)
            at = (e * planes + XO - depth + i) * rows + YO
            frame_ref[at : at + SIZE_Y, :] = low_ref[here, :].astype(jnp.float32)
            at = (e * planes + XO + size_x + i) * rows + YO
            frame_ref[at : at + SIZE_Y, :] = high_ref[here, :].astype(jnp.float32)
    return base + channels * depth * SIZE_Y


def depth_rows(frames, gz, x, size_y, rows, planes, channels):
    lane = lanes((size_y, 128))
    out = jnp.zeros((size_y, 128), jnp.float32)
    for e in range(channels):
        for index, frame_ref in enumerate(frames):
            own = frame_ref.shape[0] == planes * rows
            at = ((0 if own else e) * planes + x) * rows + YO
            start = e * 16 + index * SEND + 1
            moved = turned(frame_ref[at : at + size_y, :], start + 3 - 3 * gz)
            out = jnp.where((lane >= start) & (lane < start + 3), moved, out)
    return out


def frame_kernel(full, channels, _, low_ref, high_ref, kept_ref, depth_ref):
    frame_ref, forcing_ref, code_ref, _, _ = parted(kept_ref)
    rows = SIZE_Y + 2 * YO
    planes = frame_ref.shape[0] // (channels * rows)
    base = beside(frame_ref, channels, low_ref, high_ref, 0, 3)
    frames = [frame_ref]
    if full:
        base = beside(forcing_ref, channels, low_ref, high_ref, base, 2)
        beside(code_ref, 1, low_ref, high_ref, base, 2)
        frames = [frame_ref, forcing_ref, code_ref]
    gz = lax.axis_index("gz")
    for x in range(planes):
        out = depth_rows(frames, gz, x, SIZE_Y, rows, planes, channels)
        depth_ref[x * SIZE_Y : (x + 1) * SIZE_Y, :] = out.astype(jnp.bfloat16)


def edge_kernel(full, kept_ref, other_ref, depth_ref, up_ref, down_ref):
    frame_ref, forcing_ref, code_ref, _, _ = parted(kept_ref)
    rows = SIZE_Y + 2 * YO
    planes = depth_ref.shape[0] // rows
    depth_ref[...] = jnp.zeros_like(depth_ref)
    for x in range(planes):
        here = other_ref[x * SIZE_Y : (x + 1) * SIZE_Y, :].astype(jnp.float32)
        depth_ref[x * rows + YO : x * rows + YO + SIZE_Y, :] = here

    def put(base, ref, depth, step):
        count = ref.shape[0] // rows
        for j in range(depth):
            high = ref[pl.ds(YO + SIZE_Y - depth + j, count, stride=rows), :]
            low = ref[pl.ds(YO + j, count, stride=rows), :]
            up_ref[base + j * step : base + j * step + count, :] = high.astype(jnp.bfloat16)
            down_ref[base + j * step : base + j * step + count, :] = low.astype(jnp.bfloat16)
        return base + depth * step

    if full:
        up_ref[edge_tail(full) :, :] = jnp.zeros((80, 128), jnp.bfloat16)
        down_ref[edge_tail(full) :, :] = jnp.zeros((80, 128), jnp.bfloat16)
    else:
        up_ref[edge_tail(full) :, :] = jnp.zeros((48, 128), jnp.bfloat16)
        down_ref[edge_tail(full) :, :] = jnp.zeros((48, 128), jnp.bfloat16)
    base = put(0, frame_ref, 3, 80)
    if full:
        base = put(base, forcing_ref, 2, 80)
        base = put(base, code_ref, 2, 16)
    put(base, depth_ref, 3, 16)


def edge_tail(full):
    return 400 if full else 240


def take_edges(frame_ref, low_ref, high_ref, base, depth, step):
    rows = SIZE_Y + 2 * YO
    count = frame_ref.shape[0] // rows
    for j in range(depth):
        low = low_ref[base + j * step : base + j * step + count, :].astype(jnp.float32)
        high = high_ref[base + j * step : base + j * step + count, :].astype(jnp.float32)
        frame_ref[pl.ds(YO - depth + j, count, stride=rows), :] = low
        frame_ref[pl.ds(YO + SIZE_Y + j, count, stride=rows), :] = high
    return base + depth * step


def faces(get, e_range, gz, shape):
    lane = lanes(shape)
    out = jnp.zeros(shape, jnp.float32)
    for e in e_range:
        out = jnp.where(lane == e * 16 + 4 * gz, turned(get(e), e * 16 + 1 + 3 * gz), out)
    return out


def sweep(src, dst, zsrc, zdst, forcing, coef, zforcing, zcoef, gz, x_low, x_high, channels, planes, finish=None):
    rows = SIZE_Y + 2 * YO
    shape = (rows, 128)
    lane = lanes(shape)
    keep = 1.0 - relax_weight
    inner_low = (lane > 0).astype(jnp.float32)
    inner_high = (lane < 127).astype(jnp.float32)
    border = (lane == 127 - 127 * gz).astype(jnp.float32)
    face_lane = (lane & 15) == 4 * gz

    def one_plane(x, carry):
        at = pl.multiple_of(x * rows, 8)
        other = zsrc[pl.ds(at, rows), :]
        weight = coef[pl.ds(at, rows), :]
        fresh = []
        for e in range(channels):
            row = pl.multiple_of((e * planes + x) * rows, 8)
            own = src[pl.ds(row, rows), :]
            total = src[pl.ds(row + rows, rows), :] + src[pl.ds(row - rows, rows), :]
            total = total + pltpu.roll(own, rows - 1, 0) + pltpu.roll(own, 1, 0)
            total = total + pltpu.roll(own, 127, 1) * inner_high + pltpu.roll(own, 1, 1) * inner_low
            total = total + turned(other, 126 - gz - 16 * e + 256) * border
            new = keep * own + weight * (forcing[pl.ds(row, rows), :] + total)
            if finish is None:
                dst[pl.ds(row, rows), :] = new
            else:
                finish(e, x, new)
            fresh.append(new)
        if finish is None:
            total = zsrc[pl.ds(at + rows, rows), :] + zsrc[pl.ds(at - rows, rows), :]
            total = total + pltpu.roll(other, rows - 1, 0) + pltpu.roll(other, 1, 0)
            total = total + pltpu.roll(other, 127, 1) + pltpu.roll(other, 1, 1)
            new = keep * other + zcoef[pl.ds(at, rows), :] * (zforcing[pl.ds(at, rows), :] + total)
            face = faces(lambda e: fresh[e], range(channels), gz, shape)
            zdst[pl.ds(at, rows), :] = jnp.where(face_lane, face, new)
        return carry

    lax.fori_loop(x_low, x_high, one_plane, 0, unroll=True)


def sweeps(frame, second, zframe, zsecond, forcing, coef, zforcing, zcoef, gz, channels, planes, finish):
    rows = SIZE_Y + 2 * YO
    face_lane = (lanes((rows, 128)) & 15) == 4 * gz
    for x in range(planes):
        face = faces(lambda e: frame[(e * planes + x) * rows : (e * planes + x + 1) * rows, :], range(channels), gz, (rows, 128))
        here = zframe[x * rows : (x + 1) * rows, :]
        zframe[x * rows : (x + 1) * rows, :] = jnp.where(face_lane, face, here)
    sweep(frame, second, zframe, zsecond, forcing, coef, zforcing, zcoef, gz, 1, planes - 1, channels, planes)
    sweep(second, frame, zsecond, zframe, forcing, coef, zforcing, zcoef, gz, 2, planes - 2, channels, planes)

    sweep(frame, None, zframe, None, forcing, coef, zforcing, zcoef, gz, XO, planes - XO, channels, planes, finish)


def density_of(layers, cell, live, channels):
    slots, size_z = cell.shape[1], layers.shape[1]
    pick = (lax.broadcasted_iota(jnp.int32, (size_z, slots), 0) == (cell & (size_z - 1))).astype(jnp.bfloat16)
    count = layers.shape[0] // channels
    lines = jnp.dot(layers.astype(jnp.bfloat16), pick, preferred_element_type=jnp.float32)
    used = lanes((count, slots)) < live.astype(jnp.int32)
    mask = used & (lax.broadcasted_iota(jnp.int32, (count, slots), 0) == (cell >> 7))
    found = [
        jnp.sum(jnp.where(mask, lines[e * count : (e + 1) * count, :], 0.0), axis=0, keepdims=True)
        for e in range(channels)
    ]
    return jnp.concatenate(found, axis=0).astype(jnp.bfloat16)


def parted(kept_ref):
    rows = kept_ref.shape[0] // KEPT
    frame = (KEPT - 3) // 2 * rows
    ends = [0, frame, 2 * frame] + [2 * frame + n * rows for n in range(1, 4)]
    return [kept_ref.at[ends[n] : ends[n + 1]] for n in range(5)]


def first_kernel(
    _, depth_ref, low_ref, high_ref, note_ref,
    kept_ref, density_ref, up_ref, down_ref, first, second, zfirst, zsecond, code, zcode, layers,
):
    gz = lax.axis_index("gz")
    rows = SIZE_Y + 2 * YO
    planes = depth_ref.shape[0] // rows
    state, forcing, coef, zforcing, zcoef = parted(kept_ref)
    channels = first.shape[0] // (planes * rows)
    first[...] = state[...]
    code[...] = coef[...]
    zcode[...] = depth_ref[...]
    base = take_edges(first, low_ref, high_ref, 0, 3, 80)
    base = take_edges(forcing, low_ref, high_ref, base, 2, 80)
    base = take_edges(code, low_ref, high_ref, base, 2, 16)
    take_edges(zcode, low_ref, high_ref, base, 3, 16)
    lane = lanes((rows, 128)) & 15
    outer = (lane >= 1) & (lane <= 3)
    shifts = [jnp.broadcast_to(note_ref[6:7, n : n + 1], (rows, 128)) for n in range(CLASSES)]
    for x in range(planes):
        here = pl.ds(x * rows, rows)
        packed = zcode[here, :]
        zfirst[here, :] = jnp.where(outer, packed, 0.0)
        zforcing[here, :] = jnp.where(outer, turned(packed, 128 - SEND), 0.0)
        level = jnp.where(outer, turned(packed, 128 - 2 * SEND), 0.0)
        own_level = code[here, :]
        zshift = jnp.zeros((rows, 128), jnp.float32)
        shift = jnp.zeros((rows, 128), jnp.float32)
        for index in range(CLASSES):
            zshift = jnp.where(level == index + 1.0, shifts[index], zshift)
            shift = jnp.where(own_level == index + 1.0, shifts[index], shift)
        zcoef[here, :] = jnp.where(level > 0.0, relax_weight / (6.0 + zshift), 0.0)
        coef[here, :] = jnp.where(own_level > 0.0, relax_weight / (6.0 + shift), 0.0)

    def finish(e, x, new):
        own = new[YO : YO + SIZE_Y, :]
        state[pl.ds((e * planes + x) * rows + YO, SIZE_Y), :] = own
        layers[pl.ds((e * (planes - 2 * XO) + x - XO) * SIZE_Y, SIZE_Y), :] = own

    sweeps(first, second, zfirst, zsecond, forcing, coef, zforcing, zcoef, gz, channels, planes, finish)
    put_framed_planes(up_ref, down_ref, state, channels, 3)
    density = density_of(layers[...], note_ref[5:6, :].astype(jnp.int32), note_ref[4:5, :], channels)
    message = jnp.concatenate([density.astype(jnp.float32), note_ref[...]], axis=0)
    for brick in range(density_ref.shape[0]):
        density_ref[brick] = message


def add_load(forcing, zforcing, near_ref, side, gz, channels, planes):
    rows = SIZE_Y + 2 * YO
    size_x = planes - 2 * XO
    cells = near_ref[6].astype(jnp.int32)
    slots = cells.shape[1]
    wide = 3 * slots

    def row_of(first):
        cell = jnp.concatenate([cells[first + n : first + n + 1, :] for n in range(3)], axis=1)
        shift = jnp.concatenate([jnp.full((1, slots), YO + SIZE_Y * (n - 1), jnp.int32) for n in range(3)], axis=1)
        value = coupling * jnp.concatenate([near_ref[first + n] for n in range(3)], axis=1)
        return cell & 127, ((cell >> 7) & (SIZE_Y - 1)) + shift, cell >> 11, value

    span = {-1: range(size_x - 2, size_x), 0: range(size_x), 1: range(2)}[side]
    level = lax.broadcasted_iota(jnp.int32, (rows, wide), 0)
    z, y, x, value = row_of(0)
    pick = (lax.broadcasted_iota(jnp.int32, (128, wide), 0) == z).astype(jnp.bfloat16)
    for plane in span:
        mask = (level == y) & (x == plane)
        spread = jnp.concatenate([jnp.where(mask, value[e : e + 1, :], 0.0) for e in range(channels)], axis=0)
        high, low = split(spread)
        load = across(high, pick) + across(low, pick)
        at = plane + XO + size_x * side
        for e in range(channels):
            row = (e * planes + at) * rows
            forcing[row : row + rows, :] += load[e * rows : (e + 1) * rows, :]
    z, y, x, value = row_of(3)
    lane = z - 125 * gz + 1
    step = lax.broadcasted_iota(jnp.int32, (16, wide), 0)
    ok = (step == lane) & (step >= 1) & (step <= 3)
    spread = jnp.concatenate([jnp.where(ok, value[e : e + 1, :], 0.0) for e in range(channels)], axis=0)
    high, low = split(spread)
    for plane in span:
        mask = ((level == y) & (x == plane)).astype(jnp.bfloat16)
        row = (plane + XO + size_x * side) * rows
        zforcing[row : row + rows, :] += across(mask, high) + across(mask, low)


def second_kernel(
    kept_ref, depth_ref, low_ref, high_ref, near_low, near_own, near_high,
    out_ref, density_ref, first, second, zfirst, zsecond, forcing, zforcing,
):
    gz = lax.axis_index("gz")
    rows = SIZE_Y + 2 * YO
    planes = depth_ref.shape[0] // rows
    channels = out_ref.shape[0]
    state, old, coef, zold, zcoef = parted(kept_ref)
    first[...] = state[...]
    zfirst[...] = depth_ref[...]
    forcing[...] = old[...]
    zforcing[...] = zold[...]
    base = take_edges(first, low_ref, high_ref, 0, 3, 80)
    take_edges(zfirst, low_ref, high_ref, base, 3, 16)
    for side, near in ((-1, near_low), (0, near_own), (1, near_high)):
        add_load(forcing, zforcing, near, side, gz, channels, planes)

    def finish(e, x, new):
        out_ref[e, x - XO] = new[YO : YO + SIZE_Y, :]

    sweeps(first, second, zfirst, zsecond, forcing, coef, zforcing, zcoef, gz, channels, planes, finish)
    layers = out_ref[...].reshape(-1, out_ref.shape[3])
    density = density_of(layers, near_own[6, 1:2, :].astype(jnp.int32), near_own[6, 7:8, :], channels)
    for brick in range(density_ref.shape[0]):
        density_ref[brick] = density


def near_kernel(parts_ref, targets_ref, near_ref):
    col, gz = lax.axis_index("col"), lax.axis_index("gz")
    cols = targets_ref.shape[0] // 2
    slots = targets_ref.shape[2]
    lane = lanes((8, slots))
    near_ref[6] = jnp.zeros((8, slots), jnp.float32)
    for n in range(6):
        side = jnp.clip(col + n % 3 - 1, 0, cols - 1)
        half = gz if n < 3 else 1 - gz
        about = targets_ref[side * 2 + half]
        total = parts_ref[0, n]
        for sender in range(1, parts_ref.shape[0]):
            total = total + parts_ref[sender, n]
        total = jnp.where(lane < about[4:5, :].astype(jnp.int32), total, 0.0)
        near_ref[n] = total
        near_ref[6, n : n + 1, :] = about[5:6, :]
        if n == 1:
            near_ref[6, 7:8, :] = about[4:5, :]


def last_kernel(parts_ref, own_ref):
    total = parts_ref[0]
    for sender in range(1, parts_ref.shape[0]):
        total = total + parts_ref[sender]
    own_ref[...] = total


def both_ways(up, down, axis):
    devices = lax.axis_size(axis)
    pairs = [(i, i + 1) for i in range(devices - 1)]
    return lax.ppermute(up, axis, pairs), lax.ppermute(down, axis, [(b, a) for a, b in pairs])


def local(
    initial_field, source_term, cell_class, class_shift, surface_cell, live_count, panel_geometry
):
    channels, size_x, size_y, size_z = initial_field.shape
    slots = surface_cell.shape[0]
    bricks = lax.axis_size("row")
    panels = slots * lax.axis_size("row") * lax.axis_size("col") * lax.axis_size("gz")
    factor = 1.0 / math.sqrt(panels)
    planes, rows = size_x + 2 * XO, size_y + 2 * YO
    frame, flat = (channels * planes * rows, 128), (planes * rows, 128)
    cells = surface_cell[None]
    vm = lambda shape, dtype=jnp.float32: pltpu.VMEM(shape, dtype)

    send_x = channels * 5 * size_y + 2 * size_y
    up, down, message = whole_call(
        functools.partial(planes_kernel, factor),
        (bf16(send_x, 128), bf16(send_x, 128), f32(bricks, 8, slots)),
        [vm(initial_field.shape), vm(initial_field.shape), vm((1, *cell_class.shape), jnp.int32),
         vm(panel_geometry.shape), vm(cells.shape, jnp.int32), pltpu.SMEM((1,), jnp.int32), pltpu.SMEM((CLASSES,), jnp.float32),
         pltpu.SemaphoreType.DMA((7,))],
        "planes", (), initial_field, source_term, cell_class[None], panel_geometry, cells, live_count, class_shift,
        away=(0, 1, 2, 3, 4, 5, 6), megabytes=62,
    )
    kept = whole_call(
        own_kernel, f32(2 * frame[0] + 3 * flat[0], 128), [], "own", (),
        initial_field, source_term, cell_class[None],
    )
    low, high = both_ways(up, down, "row")
    kept, depth = whole_call(
        functools.partial(frame_kernel, True, channels),
        (f32(*kept.shape), bf16(planes * size_y, 128)), [], "frame", (),
        kept, low, high, aliases={0: 0},
    )
    other = lax.ppermute(depth, "gz", [(0, 1), (1, 0)])
    targets = lax.all_to_all(message, ("col", "gz"), 0, 0, tiled=True)
    other, targets = lax.optimization_barrier((other, targets))
    zframe, up, down = whole_call(
        functools.partial(edge_kernel, True), (f32(*flat), bf16(480, 128), bf16(480, 128)), [], "edges", (),
        kept, other,
    )
    low, high = both_ways(up, down, "col")
    smem = pl.BlockSpec(memory_space=pltpu.SMEM)
    vmem = pl.BlockSpec(memory_space=pltpu.VMEM)
    aims, note, table = pl.pallas_call(
        compact_kernel,
        in_specs=[vmem],
        out_specs=(vmem, vmem, smem),
        out_shape=(f32(bricks + 2, 8, slots), f32(8, slots), jax.ShapeDtypeStruct((bricks + 1,), jnp.int32)),
        scratch_shapes=[vm((8, slots), jnp.int32), pltpu.SMEM((8, slots), jnp.int32), pltpu.SemaphoreType.DMA],
        compiler_params=params(4),
        name="compact",
    )(targets)
    low, high, aims, table = lax.optimization_barrier((low, high, aims, table))
    kept, density, up, down = whole_call(
        first_kernel,
        (f32(*kept.shape), f32(bricks, 2 * channels, slots),
         bf16(channels * 3 * size_y, 128), bf16(channels * 3 * size_y, 128)),
        [vm(frame), vm(frame), vm(flat), vm(flat), vm(flat), vm(flat),
         vm((channels * size_x * size_y, size_z))], "first", (),
        kept, zframe, low, high, note, aliases={0: 0}, megabytes=8,
    )
    low, high = both_ways(up, down, "row")
    densities = lax.all_to_all(density, "row", 0, 0, tiled=True)
    done = make_tile(0, densities, aims, channels)
    low, high, done = lax.optimization_barrier((low, high, done))
    kept, depth = whole_call(
        functools.partial(frame_kernel, False, channels),
        (f32(*kept.shape), bf16(planes * size_y, 128)), [], "frame", (),
        kept, low, high, aliases={0: 0},
    )
    other = lax.ppermute(depth, "gz", [(0, 1), (1, 0)])
    densities, depth = lax.optimization_barrier((densities, depth))
    done = make_tile(1, densities, aims, channels, done)
    other, done = lax.optimization_barrier((other, done))
    zframe, up, down = whole_call(
        functools.partial(edge_kernel, False), (f32(*flat), bf16(288, 128), bf16(288, 128)), [], "edges", (),
        kept, other,
    )
    low, high = both_ways(up, down, "col")
    densities, up = lax.optimization_barrier((densities, up))
    tile, shares = make_tile(2, densities, aims, channels, done)
    shares = whole_call(arrange_kernel, f32(bricks, 6, channels, slots), [], "arrange", (table,), shares)
    parts = lax.all_to_all(shares, ("col", "gz"), 0, 0, tiled=True)
    near = whole_call(near_kernel, f32(7, channels, slots), [], "near", (), parts, targets)
    near_low, near_high = both_ways(near, near, "row")
    state, density = whole_call(
        second_kernel, (f32(*initial_field.shape), bf16(bricks, channels, slots)),
        [vm(frame), vm(frame), vm(flat), vm(flat), vm(frame), vm(flat)], "second", (),
        kept, zframe, low, high, near_low, near, near_high, megabytes=8,
    )
    densities = lax.all_to_all(density, "row", 0, 0, tiled=True)
    shares = products(table, densities, tile, 512)
    parts = lax.all_to_all(shares, ("col", "gz"), 0, 0, tiled=True)
    potential = whole_call(last_kernel, f32(channels, slots), [], "last", (), parts)
    return (state, potential)


def solution(mesh):
    placed = (
        P(None, "row", "col", "gz"),
        P(None, "row", "col", "gz"),
        P("row", "col", "gz"),
        P(),
        P(("row", "col", "gz")),
        P(("row", "col", "gz")),
        P(None, ("row", "col", "gz")),
    )
    return jax.shard_map(
        local,
        mesh=mesh,
        in_specs=placed,
        out_specs=(P(None, "row", "col", "gz"), P(None, ("row", "col", "gz"))),
        check_vma=False,
    )
```

```python
import functools
import math

import jax
import jax.numpy as jnp
from jax import lax
from jax.experimental import pallas as pl
from jax.experimental.pallas import tpu as pltpu
from jax.sharding import PartitionSpec as P

SIZE_Y = 16
CLASSES = 16
KEPT = 19
TILES = 3
ROOM = 8

relax_weight = 0.8
wave_number = 25.0
soften = 0.05
coupling = 0.5

SINE = (6.283164044297846, -41.33714237050646, 81.34076886863805, -70.99343309793157)
TURNS = wave_number / (2.0 * math.pi)


def from_everyone(x, axis):
    copies = jnp.broadcast_to(x, (lax.axis_size(axis), *x.shape))
    return lax.all_to_all(copies, axis, split_axis=0, concat_axis=0, tiled=True)


REACH = 3
XO, YO = 3, 4
SEND = 5


def lanes(shape):
    return lax.broadcasted_iota(jnp.int32, shape, len(shape) - 1)


def turned(x, shift):
    return pltpu.roll(x, shift % x.shape[-1], x.ndim - 1)


def params(megabytes):
    return pltpu.CompilerParams(vmem_limit_bytes=megabytes << 20)


def whole_call(kernel, out_shape, scratch, name, scalars, *operands, megabytes=4, away=(), aliases={}):
    smem = pl.BlockSpec(memory_space=pltpu.SMEM)
    vmem = pl.BlockSpec(memory_space=pltpu.VMEM)
    far = pl.BlockSpec(memory_space=pltpu.HBM)
    return pl.pallas_call(
        kernel,
        in_specs=[smem] * len(scalars) + [far if n in away else vmem for n in range(len(operands))],
        out_specs=jax.tree.map(lambda _: vmem, out_shape),
        out_shape=out_shape,
        scratch_shapes=scratch,
        compiler_params=params(megabytes),
        input_output_aliases={len(scalars) + k: v for k, v in aliases.items()},
        name=name,
    )(*scalars, *operands)


def f32(*shape):
    return jax.ShapeDtypeStruct(shape, jnp.float32)


def bf16(*shape):
    return jax.ShapeDtypeStruct(shape, jnp.bfloat16)


def split(x):
    high = x.astype(jnp.bfloat16)
    return high, (x - high.astype(jnp.float32)).astype(jnp.bfloat16)


def across(a, b):
    return lax.dot_general(a, b, (((1,), (1,)), ((), ())), preferred_element_type=jnp.float32)


def compact_kernel(target_ref, target_out, note_ref, table_ref, counts, table, arrived):
    bricks, depth, slots = target_ref.shape
    lane = lanes((depth, slots))
    first = jnp.zeros((depth, slots), jnp.float32)
    for brick in range(bricks):
        first = jnp.where(lane == brick, target_ref[brick, 4:5, :], first)
    counts[...] = first.astype(jnp.int32)
    copy = pltpu.make_async_copy(counts, table, arrived)
    copy.start()
    target_out[...] = jnp.zeros_like(target_out)
    note_ref[...] = target_ref[lax.axis_index("col") * 2 + lax.axis_index("gz")]
    copy.wait()
    begin = jnp.int32(0)
    for brick in range(bricks):
        append(target_out, target_ref[brick], begin, table[0, brick])
        table_ref[brick] = begin
        begin = begin + table[0, brick]
    table_ref[bricks] = begin


def append(out, rows, begin, count):
    group, shift = begin >> 7, begin & 127
    lane = lanes(rows.shape)
    moved = pltpu.roll(rows, shift, 1)
    out[group] = jnp.where((lane >= shift) & (lane < shift + count), moved, out[group])
    out[group + 1] = jnp.where(lane < shift + count - rows.shape[1], moved, out[group + 1])


def tile_kernel(source_ref, target_ref, *refs):
    tile_ref, share_ref, columns, density = refs[-4:]
    bricks, slots = source_ref.shape[0], source_ref.shape[2]
    channels = share_ref.shape[1]
    step = pl.program_id(0)

    @pl.when(step == 0)
    def _():
        for brick in range(bricks):
            density[:, brick * slots : (brick + 1) * slots] = source_ref[brick, :channels].astype(jnp.bfloat16)

    @pl.when(jnp.max(target_ref[0, 4:5, :]) > 0.0)
    def _():
        columns[...] = jnp.transpose(target_ref[0])
        spread = [jnp.broadcast_to(columns[:, d : d + 1], (slots, slots)) for d in range(3)]
        total = jnp.zeros((channels, slots), jnp.float32)
        for pair in range(0, bricks, 2):
            both = []
            for brick in (pair, pair + 1):
                delta = [spread[d] - source_ref[brick, channels + d : channels + d + 1, :] for d in range(3)]
                square = delta[0] * delta[0] + (delta[1] * delta[1] + (delta[2] * delta[2] + 1e-30))
                turns = square * lax.rsqrt(square)
                angle = 0.25 - jnp.abs(turns - jnp.round(turns))
                angle2 = angle * angle
                wave = SINE[-1]
                for c in SINE[-2::-1]:
                    wave = wave * angle2 + c
                weight = source_ref[brick, channels + 3 : channels + 4, :]
                value = (angle * weight) * wave / (turns + soften * TURNS)
                both.append(value.astype(jnp.bfloat16))
                tile_ref[:, brick * slots : (brick + 1) * slots] = both[-1]
            at = slice(pair * slots, (pair + 2) * slots)
            total = total + across(density[:, at], jnp.concatenate(both, axis=1))
        share_ref[0] = total


def make_tile(part, sources, targets, channels, before=()):
    bricks, slots = sources.shape[0], sources.shape[2]
    far = pl.BlockSpec(memory_space=pl.ANY)
    return pl.pallas_call(
        tile_kernel,
        grid=(-(-bricks // TILES),),
        in_specs=[
            pl.BlockSpec(sources.shape, lambda b: (0, 0, 0)),
            pl.BlockSpec((1, targets.shape[1], slots), lambda b: (TILES * b + part, 0, 0)),
        ]
        + [far] * len(before),
        out_specs=[
            pl.BlockSpec((slots, bricks * slots), lambda b: (TILES * b + part, 0)),
            pl.BlockSpec((1, channels, slots), lambda b: (TILES * b + part, 0, 0)),
        ],
        out_shape=[
            jax.ShapeDtypeStruct((ROOM * bricks * slots, bricks * slots), jnp.bfloat16),
            jax.ShapeDtypeStruct((bricks + 2, channels, slots), jnp.float32),
        ],
        scratch_shapes=[
            pltpu.VMEM((slots, targets.shape[1]), jnp.float32),
            pltpu.VMEM((channels, bricks * slots), jnp.bfloat16),
        ],
        input_output_aliases={2 + n: n for n in range(len(before))},
        compiler_params=params(8),
        name="tile",
    )(sources, targets, *before)


def taken(share_ref, table_ref, brick, bricks):
    begin = table_ref[brick]
    count = table_ref[brick + 1] - begin
    group, shift = begin >> 7, begin & 127
    lane = lanes(share_ref.shape[1:])
    slots = share_ref.shape[2]
    this = pltpu.roll(share_ref[group], (slots - shift) & 127, 1)
    following = pltpu.roll(share_ref[jnp.minimum(group + 1, bricks - 1)], (slots - shift) & 127, 1)
    return jnp.where(lane < count, jnp.where(lane < slots - shift, this, following), 0.0)


def arrange_kernel(table_ref, share_ref, out_ref):
    bricks = out_ref.shape[0]
    for index in range(bricks):
        value = taken(share_ref, table_ref, index, bricks)
        for n in range(6):
            side, other = index // 2 - (n % 3 - 1), (index + n // 3) % 2
            if 0 <= side < bricks // 2:
                out_ref[side * 2 + other, n] = value
    for brick in range(bricks):
        for n in range(6):
            if not 0 <= brick // 2 + n % 3 - 1 < bricks // 2:
                out_ref[brick, n] = jnp.zeros(out_ref.shape[2:], jnp.float32)


def product_kernel(table_ref, density_ref, tile_ref, out_ref, density, shares):
    bricks, channels, slots = density_ref.shape
    step = pl.program_id(0)
    count = tile_ref.shape[0] // slots

    @pl.when(step == 0)
    def _():
        for brick in range(bricks):
            density[:, brick * slots : (brick + 1) * slots] = density_ref[brick]

    @pl.when(step * count * slots < table_ref[bricks])
    def _():
        total = across(density[...], tile_ref[...])
        for index in range(count):
            shares[step * count + index] = total[:, index * slots : (index + 1) * slots]

    @pl.when(step == pl.num_programs(0) - 1)
    def _():
        for brick in range(bricks):
            out_ref[brick] = taken(shares, table_ref, brick, bricks)


def products(table, density, tile, rows):
    bricks, channels, slots = density.shape
    width = tile.shape[1]
    steps = bricks * slots // rows

    def block(b, table_ref):
        last = (table_ref[bricks] + rows - 1) // rows - 1
        return jnp.minimum(b, last), 0

    return pl.pallas_call(
        product_kernel,
        grid_spec=pltpu.PrefetchScalarGridSpec(
            num_scalar_prefetch=1,
            grid=(steps,),
            in_specs=[pl.BlockSpec(density.shape, lambda b, t: (0, 0, 0)), pl.BlockSpec((rows, width), block)],
            out_specs=pl.BlockSpec((bricks, channels, slots), lambda b, t: (0, 0, 0)),
            scratch_shapes=[
                pltpu.VMEM((channels, width), jnp.bfloat16),
                pltpu.VMEM((bricks, channels, slots), jnp.float32),
            ],
        ),
        out_shape=jax.ShapeDtypeStruct((bricks, channels, slots), jnp.float32),
        compiler_params=params(12),
        name="product",
    )(table, density, tile)


def put_planes(up_ref, down_ref, base, field_ref, depth, offset=0):
    size_x, size_y = field_ref.shape[-3], field_ref.shape[-2]
    for e in range(field_ref.shape[0]):
        for i in range(depth):
            rows = pl.ds(base + (e * depth + i) * size_y, size_y)
            high = field_ref[e, size_x - depth + i] + offset
            low = field_ref[e, i] + offset
            up_ref[rows, :] = high.astype(jnp.bfloat16)
            down_ref[rows, :] = low.astype(jnp.bfloat16)
    return base + field_ref.shape[0] * depth * size_y


def own_cells(frame_ref, field_ref, offset=0):
    channels, size_x, size_y = field_ref.shape[:3]
    planes, rows = size_x + 2 * XO, size_y + 2 * YO
    frame_ref[...] = jnp.zeros_like(frame_ref)
    for e in range(channels):
        for x in range(size_x):
            at = (e * planes + XO + x) * rows + YO
            frame_ref[at : at + size_y, :] = field_ref[e, x].astype(jnp.float32) + offset


def put_framed_planes(up_ref, down_ref, frame_ref, channels, depth):
    rows = SIZE_Y + 2 * YO
    planes = frame_ref.shape[0] // (channels * rows)
    for e in range(channels):
        for i in range(depth):
            here = pl.ds((e * depth + i) * SIZE_Y, SIZE_Y)
            high = (e * planes + planes - XO - depth + i) * rows + YO
            low = (e * planes + XO + i) * rows + YO
            up_ref[here, :] = frame_ref[high : high + SIZE_Y, :].astype(jnp.bfloat16)
            down_ref[here, :] = frame_ref[low : low + SIZE_Y, :].astype(jnp.bfloat16)


def planes_kernel(
    factor, state_hbm, source_hbm, class_hbm, geometry_hbm, cell_hbm, live_hbm, shift_hbm,
    up_ref, down_ref, message_ref, state_ref, source_ref, class_ref, geometry_ref, cell_ref, live_ref, shift_ref, arrived,
):
    pairs = (
        (live_hbm, live_ref), (shift_hbm, shift_ref), (geometry_hbm, geometry_ref), (cell_hbm, cell_ref),
        (state_hbm, state_ref), (source_hbm, source_ref), (class_hbm, class_ref),
    )
    copies = [pltpu.make_async_copy(a, b, arrived.at[n]) for n, (a, b) in enumerate(pairs)]
    for copy in copies:
        copy.start()
    slots = cell_ref.shape[1]
    for copy in copies[:4]:
        copy.wait()
    shifts = jnp.zeros((1, slots), jnp.float32)
    for index in range(CLASSES):
        shifts = jnp.where(lanes((1, slots)) == index, shift_ref[index], shifts)
    message = jnp.concatenate(
        [
            geometry_ref[:3] * TURNS,
            geometry_ref[3:] * (factor * TURNS),
            jnp.full((1, slots), live_ref[0], jnp.int32).astype(jnp.float32),
            cell_ref[...].astype(jnp.float32),
            shifts,
            jnp.zeros((1, slots), jnp.float32),
        ],
        axis=0,
    )
    for brick in range(message_ref.shape[0]):
        message_ref[brick] = message
    for copy in copies[4:]:
        copy.wait()
    base = put_planes(up_ref, down_ref, 0, state_ref, 3)
    base = put_planes(up_ref, down_ref, base, source_ref, 2)
    put_planes(up_ref, down_ref, base, class_ref, 2, 1.0)


def own_kernel(state_ref, source_ref, class_ref, kept_ref):
    frame_ref, forcing_ref, code_ref, _, _ = parted(kept_ref)
    own_cells(frame_ref, state_ref)
    own_cells(forcing_ref, source_ref)
    own_cells(code_ref, class_ref, 1.0)


def beside(frame_ref, channels, low_ref, high_ref, base, depth):
    rows = SIZE_Y + 2 * YO
    planes = frame_ref.shape[0] // (channels * rows)
    size_x = planes - 2 * XO
    for e in range(channels):
        for i in range(depth):
            here = pl.ds(base + (e * depth + i) * SIZE_Y, SIZE_Y)
            at = (e * planes + XO - depth + i) * rows + YO
            frame_ref[at : at + SIZE_Y, :] = low_ref[here, :].astype(jnp.float32)
            at = (e * planes + XO + size_x + i) * rows + YO
            frame_ref[at : at + SIZE_Y, :] = high_ref[here, :].astype(jnp.float32)
    return base + channels * depth * SIZE_Y


def depth_rows(frames, gz, x, size_y, rows, planes, channels):
    lane = lanes((size_y, 128))
    out = jnp.zeros((size_y, 128), jnp.float32)
    for e in range(channels):
        for index, frame_ref in enumerate(frames):
            own = frame_ref.shape[0] == planes * rows
            at = ((0 if own else e) * planes + x) * rows + YO
            start = e * 16 + index * SEND + 1
            moved = turned(frame_ref[at : at + size_y, :], start + 3 - 3 * gz)
            out = jnp.where((lane >= start) & (lane < start + 3), moved, out)
    return out


def frame_kernel(full, channels, _, low_ref, high_ref, kept_ref, depth_ref):
    frame_ref, forcing_ref, code_ref, _, _ = parted(kept_ref)
    rows = SIZE_Y + 2 * YO
    planes = frame_ref.shape[0] // (channels * rows)
    base = beside(frame_ref, channels, low_ref, high_ref, 0, 3)
    frames = [frame_ref]
    if full:
        base = beside(forcing_ref, channels, low_ref, high_ref, base, 2)
        beside(code_ref, 1, low_ref, high_ref, base, 2)
        frames = [frame_ref, forcing_ref, code_ref]
    gz = lax.axis_index("gz")
    for x in range(planes):
        out = depth_rows(frames, gz, x, SIZE_Y, rows, planes, channels)
        depth_ref[x * SIZE_Y : (x + 1) * SIZE_Y, :] = out.astype(jnp.bfloat16)


def edge_kernel(full, kept_ref, other_ref, depth_ref, up_ref, down_ref):
    frame_ref, forcing_ref, code_ref, _, _ = parted(kept_ref)
    rows = SIZE_Y + 2 * YO
    planes = depth_ref.shape[0] // rows
    depth_ref[...] = jnp.zeros_like(depth_ref)
    for x in range(planes):
        here = other_ref[x * SIZE_Y : (x + 1) * SIZE_Y, :].astype(jnp.float32)
        depth_ref[x * rows + YO : x * rows + YO + SIZE_Y, :] = here

    def put(base, ref, depth, step):
        count = ref.shape[0] // rows
        for j in range(depth):
            high = ref[pl.ds(YO + SIZE_Y - depth + j, count, stride=rows), :]
            low = ref[pl.ds(YO + j, count, stride=rows), :]
            up_ref[base + j * step : base + j * step + count, :] = high.astype(jnp.bfloat16)
            down_ref[base + j * step : base + j * step + count, :] = low.astype(jnp.bfloat16)
        return base + depth * step

    if full:
        up_ref[edge_tail(full) :, :] = jnp.zeros((80, 128), jnp.bfloat16)
        down_ref[edge_tail(full) :, :] = jnp.zeros((80, 128), jnp.bfloat16)
    else:
        up_ref[edge_tail(full) :, :] = jnp.zeros((48, 128), jnp.bfloat16)
        down_ref[edge_tail(full) :, :] = jnp.zeros((48, 128), jnp.bfloat16)
    base = put(0, frame_ref, 3, 80)
    if full:
        base = put(base, forcing_ref, 2, 80)
        base = put(base, code_ref, 2, 16)
    put(base, depth_ref, 3, 16)


def edge_tail(full):
    return 400 if full else 240


def take_edges(frame_ref, low_ref, high_ref, base, depth, step):
    rows = SIZE_Y + 2 * YO
    count = frame_ref.shape[0] // rows
    for j in range(depth):
        low = low_ref[base + j * step : base + j * step + count, :].astype(jnp.float32)
        high = high_ref[base + j * step : base + j * step + count, :].astype(jnp.float32)
        frame_ref[pl.ds(YO - depth + j, count, stride=rows), :] = low
        frame_ref[pl.ds(YO + SIZE_Y + j, count, stride=rows), :] = high
    return base + depth * step


def faces(get, e_range, gz, shape):
    lane = lanes(shape)
    out = jnp.zeros(shape, jnp.float32)
    for e in e_range:
        out = jnp.where(lane == e * 16 + 4 * gz, turned(get(e), e * 16 + 1 + 3 * gz), out)
    return out


def sweep(src, dst, zsrc, zdst, forcing, coef, zforcing, zcoef, gz, x_low, x_high, channels, planes, finish=None):
    rows = SIZE_Y + 2 * YO
    shape = (rows, 128)
    lane = lanes(shape)
    keep = 1.0 - relax_weight
    inner_low = (lane > 0).astype(jnp.float32)
    inner_high = (lane < 127).astype(jnp.float32)
    border = (lane == 127 - 127 * gz).astype(jnp.float32)
    face_lane = (lane & 15) == 4 * gz

    def one_plane(x, carry):
        at = pl.multiple_of(x * rows, 8)
        other = zsrc[pl.ds(at, rows), :]
        weight = coef[pl.ds(at, rows), :]
        fresh = []
        for e in range(channels):
            row = pl.multiple_of((e * planes + x) * rows, 8)
            own = src[pl.ds(row, rows), :]
            total = src[pl.ds(row + rows, rows), :] + src[pl.ds(row - rows, rows), :]
            total = total + pltpu.roll(own, rows - 1, 0) + pltpu.roll(own, 1, 0)
            total = total + pltpu.roll(own, 127, 1) * inner_high + pltpu.roll(own, 1, 1) * inner_low
            total = total + turned(other, 126 - gz - 16 * e + 256) * border
            new = keep * own + weight * (forcing[pl.ds(row, rows), :] + total)
            if finish is None:
                dst[pl.ds(row, rows), :] = new
            else:
                finish(e, x, new)
            fresh.append(new)
        if finish is None:
            total = zsrc[pl.ds(at + rows, rows), :] + zsrc[pl.ds(at - rows, rows), :]
            total = total + pltpu.roll(other, rows - 1, 0) + pltpu.roll(other, 1, 0)
            total = total + pltpu.roll(other, 127, 1) + pltpu.roll(other, 1, 1)
            new = keep * other + zcoef[pl.ds(at, rows), :] * (zforcing[pl.ds(at, rows), :] + total)
            face = faces(lambda e: fresh[e], range(channels), gz, shape)
            zdst[pl.ds(at, rows), :] = jnp.where(face_lane, face, new)
        return carry

    lax.fori_loop(x_low, x_high, one_plane, 0, unroll=True)


def sweeps(frame, second, zframe, zsecond, forcing, coef, zforcing, zcoef, gz, channels, planes, finish):
    rows = SIZE_Y + 2 * YO
    face_lane = (lanes((rows, 128)) & 15) == 4 * gz
    for x in range(planes):
        face = faces(lambda e: frame[(e * planes + x) * rows : (e * planes + x + 1) * rows, :], range(channels), gz, (rows, 128))
        here = zframe[x * rows : (x + 1) * rows, :]
        zframe[x * rows : (x + 1) * rows, :] = jnp.where(face_lane, face, here)
    sweep(frame, second, zframe, zsecond, forcing, coef, zforcing, zcoef, gz, 1, planes - 1, channels, planes)
    sweep(second, frame, zsecond, zframe, forcing, coef, zforcing, zcoef, gz, 2, planes - 2, channels, planes)

    sweep(frame, None, zframe, None, forcing, coef, zforcing, zcoef, gz, XO, planes - XO, channels, planes, finish)


def density_of(layers, cell, live, channels):
    slots, size_z = cell.shape[1], layers.shape[1]
    pick = (lax.broadcasted_iota(jnp.int32, (size_z, slots), 0) == (cell & (size_z - 1))).astype(jnp.bfloat16)
    count = layers.shape[0] // channels
    lines = jnp.dot(layers.astype(jnp.bfloat16), pick, preferred_element_type=jnp.float32)
    used = lanes((count, slots)) < live.astype(jnp.int32)
    mask = used & (lax.broadcasted_iota(jnp.int32, (count, slots), 0) == (cell >> 7))
    found = [
        jnp.sum(jnp.where(mask, lines[e * count : (e + 1) * count, :], 0.0), axis=0, keepdims=True)
        for e in range(channels)
    ]
    return jnp.concatenate(found, axis=0).astype(jnp.bfloat16)


def parted(kept_ref):
    rows = kept_ref.shape[0] // KEPT
    frame = (KEPT - 3) // 2 * rows
    ends = [0, frame, 2 * frame] + [2 * frame + n * rows for n in range(1, 4)]
    return [kept_ref.at[ends[n] : ends[n + 1]] for n in range(5)]


def first_kernel(
    _, depth_ref, low_ref, high_ref, note_ref,
    kept_ref, density_ref, up_ref, down_ref, first, second, zfirst, zsecond, code, zcode, layers,
):
    gz = lax.axis_index("gz")
    rows = SIZE_Y + 2 * YO
    planes = depth_ref.shape[0] // rows
    state, forcing, coef, zforcing, zcoef = parted(kept_ref)
    channels = first.shape[0] // (planes * rows)
    first[...] = state[...]
    code[...] = coef[...]
    zcode[...] = depth_ref[...]
    base = take_edges(first, low_ref, high_ref, 0, 3, 80)
    base = take_edges(forcing, low_ref, high_ref, base, 2, 80)
    base = take_edges(code, low_ref, high_ref, base, 2, 16)
    take_edges(zcode, low_ref, high_ref, base, 3, 16)
    lane = lanes((rows, 128)) & 15
    outer = (lane >= 1) & (lane <= 3)
    shifts = [jnp.broadcast_to(note_ref[6:7, n : n + 1], (rows, 128)) for n in range(CLASSES)]
    for x in range(planes):
        here = pl.ds(x * rows, rows)
        packed = zcode[here, :]
        zfirst[here, :] = jnp.where(outer, packed, 0.0)
        zforcing[here, :] = jnp.where(outer, turned(packed, 128 - SEND), 0.0)
        level = jnp.where(outer, turned(packed, 128 - 2 * SEND), 0.0)
        own_level = code[here, :]
        zshift = jnp.zeros((rows, 128), jnp.float32)
        shift = jnp.zeros((rows, 128), jnp.float32)
        for index in range(CLASSES):
            zshift = jnp.where(level == index + 1.0, shifts[index], zshift)
            shift = jnp.where(own_level == index + 1.0, shifts[index], shift)
        zcoef[here, :] = jnp.where(level > 0.0, relax_weight / (6.0 + zshift), 0.0)
        coef[here, :] = jnp.where(own_level > 0.0, relax_weight / (6.0 + shift), 0.0)

    def finish(e, x, new):
        own = new[YO : YO + SIZE_Y, :]
        state[pl.ds((e * planes + x) * rows + YO, SIZE_Y), :] = own
        layers[pl.ds((e * (planes - 2 * XO) + x - XO) * SIZE_Y, SIZE_Y), :] = own

    sweeps(first, second, zfirst, zsecond, forcing, coef, zforcing, zcoef, gz, channels, planes, finish)
    put_framed_planes(up_ref, down_ref, state, channels, 3)
    density = density_of(layers[...], note_ref[5:6, :].astype(jnp.int32), note_ref[4:5, :], channels)
    message = jnp.concatenate([density.astype(jnp.float32), note_ref[...]], axis=0)
    for brick in range(density_ref.shape[0]):
        density_ref[brick] = message


def add_load(forcing, zforcing, near_ref, side, gz, channels, planes):
    rows = SIZE_Y + 2 * YO
    size_x = planes - 2 * XO
    cells = near_ref[6].astype(jnp.int32)
    slots = cells.shape[1]
    wide = 3 * slots

    def row_of(first):
        cell = jnp.concatenate([cells[first + n : first + n + 1, :] for n in range(3)], axis=1)
        shift = jnp.concatenate([jnp.full((1, slots), YO + SIZE_Y * (n - 1), jnp.int32) for n in range(3)], axis=1)
        value = coupling * jnp.concatenate([near_ref[first + n] for n in range(3)], axis=1)
        return cell & 127, ((cell >> 7) & (SIZE_Y - 1)) + shift, cell >> 11, value

    span = {-1: range(size_x - 2, size_x), 0: range(size_x), 1: range(2)}[side]
    level = lax.broadcasted_iota(jnp.int32, (rows, wide), 0)
    z, y, x, value = row_of(0)
    pick = (lax.broadcasted_iota(jnp.int32, (128, wide), 0) == z).astype(jnp.bfloat16)
    for plane in span:
        mask = (level == y) & (x == plane)
        spread = jnp.concatenate([jnp.where(mask, value[e : e + 1, :], 0.0) for e in range(channels)], axis=0)
        high, low = split(spread)
        load = across(high, pick) + across(low, pick)
        at = plane + XO + size_x * side
        for e in range(channels):
            row = (e * planes + at) * rows
            forcing[row : row + rows, :] += load[e * rows : (e + 1) * rows, :]
    z, y, x, value = row_of(3)
    lane = z - 125 * gz + 1
    step = lax.broadcasted_iota(jnp.int32, (16, wide), 0)
    ok = (step == lane) & (step >= 1) & (step <= 3)
    spread = jnp.concatenate([jnp.where(ok, value[e : e + 1, :], 0.0) for e in range(channels)], axis=0)
    high, low = split(spread)
    for plane in span:
        mask = ((level == y) & (x == plane)).astype(jnp.bfloat16)
        row = (plane + XO + size_x * side) * rows
        zforcing[row : row + rows, :] += across(mask, high) + across(mask, low)


def ready_kernel(channels, _, unused, low_ref, high_ref, near_own, kept_ref, depth_ref):
    gz = lax.axis_index("gz")
    planes = depth_ref.shape[0] // (SIZE_Y + 2 * YO)
    state, forcing, _, zforcing, _ = parted(kept_ref)
    base = take_edges(state, low_ref, high_ref, 0, 3, 80)
    take_edges(depth_ref, low_ref, high_ref, base, 3, 16)
    add_load(forcing, zforcing, near_own, 0, gz, channels, planes)


def second_kernel(
    _, unused, near_low, near_own, near_high, out_ref, density_ref, kept_ref, zfirst, second, zsecond,
):
    gz = lax.axis_index("gz")
    planes = zfirst.shape[0] // (SIZE_Y + 2 * YO)
    channels = out_ref.shape[0]
    first, forcing, coef, zforcing, zcoef = parted(kept_ref)
    for side, near in ((-1, near_low), (1, near_high)):
        add_load(forcing, zforcing, near, side, gz, channels, planes)

    def finish(e, x, new):
        out_ref[e, x - XO] = new[YO : YO + SIZE_Y, :]

    sweeps(first, second, zfirst, zsecond, forcing, coef, zforcing, zcoef, gz, channels, planes, finish)
    layers = out_ref[...].reshape(-1, out_ref.shape[3])
    density = density_of(layers, near_own[6, 1:2, :].astype(jnp.int32), near_own[6, 7:8, :], channels)
    for brick in range(density_ref.shape[0]):
        density_ref[brick] = density


def near_kernel(parts_ref, targets_ref, near_ref):
    col, gz = lax.axis_index("col"), lax.axis_index("gz")
    cols = targets_ref.shape[0] // 2
    slots = targets_ref.shape[2]
    lane = lanes((8, slots))
    near_ref[6] = jnp.zeros((8, slots), jnp.float32)
    for n in range(6):
        side = jnp.clip(col + n % 3 - 1, 0, cols - 1)
        half = gz if n < 3 else 1 - gz
        about = targets_ref[side * 2 + half]
        total = parts_ref[0, n]
        for sender in range(1, parts_ref.shape[0]):
            total = total + parts_ref[sender, n]
        total = jnp.where(lane < about[4:5, :].astype(jnp.int32), total, 0.0)
        near_ref[n] = total
        near_ref[6, n : n + 1, :] = about[5:6, :]
        if n == 1:
            near_ref[6, 7:8, :] = about[4:5, :]


def last_kernel(parts_ref, own_ref):
    total = parts_ref[0]
    for sender in range(1, parts_ref.shape[0]):
        total = total + parts_ref[sender]
    own_ref[...] = total


def both_ways(up, down, axis):
    devices = lax.axis_size(axis)
    pairs = [(i, i + 1) for i in range(devices - 1)]
    return lax.ppermute(up, axis, pairs), lax.ppermute(down, axis, [(b, a) for a, b in pairs])


def local(
    initial_field, source_term, cell_class, class_shift, surface_cell, live_count, panel_geometry
):
    channels, size_x, size_y, size_z = initial_field.shape
    slots = surface_cell.shape[0]
    bricks = lax.axis_size("row")
    panels = slots * lax.axis_size("row") * lax.axis_size("col") * lax.axis_size("gz")
    factor = 1.0 / math.sqrt(panels)
    planes, rows = size_x + 2 * XO, size_y + 2 * YO
    frame, flat = (channels * planes * rows, 128), (planes * rows, 128)
    cells = surface_cell[None]
    vm = lambda shape, dtype=jnp.float32: pltpu.VMEM(shape, dtype)

    send_x = channels * 5 * size_y + 2 * size_y
    up, down, message = whole_call(
        functools.partial(planes_kernel, factor),
        (bf16(send_x, 128), bf16(send_x, 128), f32(bricks, 8, slots)),
        [vm(initial_field.shape), vm(initial_field.shape), vm((1, *cell_class.shape), jnp.int32),
         vm(panel_geometry.shape), vm(cells.shape, jnp.int32), pltpu.SMEM((1,), jnp.int32), pltpu.SMEM((CLASSES,), jnp.float32),
         pltpu.SemaphoreType.DMA((7,))],
        "planes", (), initial_field, source_term, cell_class[None], panel_geometry, cells, live_count, class_shift,
        away=(0, 1, 2, 3, 4, 5, 6), megabytes=62,
    )
    kept = whole_call(
        own_kernel, f32(2 * frame[0] + 3 * flat[0], 128), [], "own", (),
        initial_field, source_term, cell_class[None],
    )
    low, high = both_ways(up, down, "row")
    kept, depth = whole_call(
        functools.partial(frame_kernel, True, channels),
        (f32(*kept.shape), bf16(planes * size_y, 128)), [], "frame", (),
        kept, low, high, aliases={0: 0},
    )
    other = lax.ppermute(depth, "gz", [(0, 1), (1, 0)])
    targets = lax.all_to_all(message, ("col", "gz"), 0, 0, tiled=True)
    other, targets = lax.optimization_barrier((other, targets))
    zframe, up, down = whole_call(
        functools.partial(edge_kernel, True), (f32(*flat), bf16(480, 128), bf16(480, 128)), [], "edges", (),
        kept, other,
    )
    low, high = both_ways(up, down, "col")
    smem = pl.BlockSpec(memory_space=pltpu.SMEM)
    vmem = pl.BlockSpec(memory_space=pltpu.VMEM)
    aims, note, table = pl.pallas_call(
        compact_kernel,
        in_specs=[vmem],
        out_specs=(vmem, vmem, smem),
        out_shape=(f32(bricks + 2, 8, slots), f32(8, slots), jax.ShapeDtypeStruct((bricks + 1,), jnp.int32)),
        scratch_shapes=[vm((8, slots), jnp.int32), pltpu.SMEM((8, slots), jnp.int32), pltpu.SemaphoreType.DMA],
        compiler_params=params(4),
        name="compact",
    )(targets)
    low, high, aims, table = lax.optimization_barrier((low, high, aims, table))
    kept, density, up, down = whole_call(
        first_kernel,
        (f32(*kept.shape), f32(bricks, 2 * channels, slots),
         bf16(channels * 3 * size_y, 128), bf16(channels * 3 * size_y, 128)),
        [vm(frame), vm(frame), vm(flat), vm(flat), vm(flat), vm(flat),
         vm((channels * size_x * size_y, size_z))], "first", (),
        kept, zframe, low, high, note, aliases={0: 0}, megabytes=8,
    )
    low, high = both_ways(up, down, "row")
    densities = lax.all_to_all(density, "row", 0, 0, tiled=True)
    done = make_tile(0, densities, aims, channels)
    low, high, done = lax.optimization_barrier((low, high, done))
    kept, depth = whole_call(
        functools.partial(frame_kernel, False, channels),
        (f32(*kept.shape), bf16(planes * size_y, 128)), [], "frame", (),
        kept, low, high, aliases={0: 0},
    )
    other = lax.ppermute(depth, "gz", [(0, 1), (1, 0)])
    densities, depth = lax.optimization_barrier((densities, depth))
    done = make_tile(1, densities, aims, channels, done)
    other, done = lax.optimization_barrier((other, done))
    zframe, up, down = whole_call(
        functools.partial(edge_kernel, False), (f32(*flat), bf16(288, 128), bf16(288, 128)), [], "edges", (),
        kept, other,
    )
    low, high = both_ways(up, down, "col")
    densities, up = lax.optimization_barrier((densities, up))
    tile, shares = make_tile(2, densities, aims, channels, done)
    shares = whole_call(arrange_kernel, f32(bricks, 6, channels, slots), [], "arrange", (table,), shares)
    parts = lax.all_to_all(shares, ("col", "gz"), 0, 0, tiled=True)
    near = whole_call(near_kernel, f32(7, channels, slots), [], "near", (), parts, targets)
    near_low, near_high = both_ways(near, near, "row")
    kept, zframe = whole_call(
        functools.partial(ready_kernel, channels), (f32(*kept.shape), f32(*flat)), [], "ready", (),
        kept, zframe, low, high, near, aliases={0: 0, 1: 1},
    )
    state, density, _, _ = whole_call(
        second_kernel,
        (f32(*initial_field.shape), bf16(bricks, channels, slots), f32(*kept.shape), f32(*flat)),
        [vm(frame), vm(flat)], "second", (),
        kept, zframe, near_low, near, near_high, aliases={0: 2, 1: 3}, megabytes=8,
    )
    densities = lax.all_to_all(density, "row", 0, 0, tiled=True)
    shares = products(table, densities, tile, 512)
    parts = lax.all_to_all(shares, ("col", "gz"), 0, 0, tiled=True)
    potential = whole_call(last_kernel, f32(channels, slots), [], "last", (), parts)
    return (state, potential)


def solution(mesh):
    placed = (
        P(None, "row", "col", "gz"),
        P(None, "row", "col", "gz"),
        P("row", "col", "gz"),
        P(),
        P(("row", "col", "gz")),
        P(("row", "col", "gz")),
        P(None, ("row", "col", "gz")),
    )
    return jax.shard_map(
        local,
        mesh=mesh,
        in_specs=placed,
        out_specs=(P(None, "row", "col", "gz"), P(None, ("row", "col", "gz"))),
        check_vma=False,
    )
```

```python
import functools
import math

import jax
import jax.numpy as jnp
from jax import lax
from jax.experimental import pallas as pl
from jax.experimental.pallas import tpu as pltpu
from jax.sharding import PartitionSpec as P

SIZE_Y = 16
CLASSES = 16
KEPT = 19
TILES = 3
ROOM = 8

relax_weight = 0.8
wave_number = 25.0
soften = 0.05
coupling = 0.5

SINE = (6.283164044297846, -41.33714237050646, 81.34076886863805, -70.99343309793157)
TURNS = wave_number / (2.0 * math.pi)


def from_everyone(x, axis):
    copies = jnp.broadcast_to(x, (lax.axis_size(axis), *x.shape))
    return lax.all_to_all(copies, axis, split_axis=0, concat_axis=0, tiled=True)


REACH = 3
XO, YO = 3, 4
SEND = 5


def lanes(shape):
    return lax.broadcasted_iota(jnp.int32, shape, len(shape) - 1)


def turned(x, shift):
    return pltpu.roll(x, shift % x.shape[-1], x.ndim - 1)


def params(megabytes):
    return pltpu.CompilerParams(vmem_limit_bytes=megabytes << 20)


def whole_call(kernel, out_shape, scratch, name, scalars, *operands, megabytes=4, away=(), aliases={}):
    smem = pl.BlockSpec(memory_space=pltpu.SMEM)
    vmem = pl.BlockSpec(memory_space=pltpu.VMEM)
    far = pl.BlockSpec(memory_space=pltpu.HBM)
    return pl.pallas_call(
        kernel,
        in_specs=[smem] * len(scalars) + [far if n in away else vmem for n in range(len(operands))],
        out_specs=jax.tree.map(lambda _: vmem, out_shape),
        out_shape=out_shape,
        scratch_shapes=scratch,
        compiler_params=params(megabytes),
        input_output_aliases={len(scalars) + k: v for k, v in aliases.items()},
        name=name,
    )(*scalars, *operands)


def f32(*shape):
    return jax.ShapeDtypeStruct(shape, jnp.float32)


def bf16(*shape):
    return jax.ShapeDtypeStruct(shape, jnp.bfloat16)


def split(x):
    high = x.astype(jnp.bfloat16)
    return high, (x - high.astype(jnp.float32)).astype(jnp.bfloat16)


def across(a, b):
    return lax.dot_general(a, b, (((1,), (1,)), ((), ())), preferred_element_type=jnp.float32)


def compact_kernel(target_ref, target_out, note_ref, counts, table_ref, table, arrived):
    bricks, depth, slots = target_ref.shape
    lane = lanes((depth, slots))
    first = jnp.zeros((depth, slots), jnp.float32)
    for brick in range(bricks):
        first = jnp.where(lane == brick, target_ref[brick, 4:5, :], first)
    counts[...] = first.astype(jnp.int32)
    copy = pltpu.make_async_copy(counts, table, arrived)
    copy.start()
    target_out[...] = jnp.zeros_like(target_out)
    note_ref[...] = target_ref[lax.axis_index("col") * 2 + lax.axis_index("gz")]
    copy.wait()
    begin = jnp.int32(0)
    for brick in range(bricks):
        append(target_out, target_ref[brick], begin, table[0, brick])
        table_ref[brick] = begin
        begin = begin + table[0, brick]
    table_ref[bricks] = begin


def append(out, rows, begin, count):
    group, shift = begin >> 7, begin & 127
    lane = lanes(rows.shape)
    moved = pltpu.roll(rows, shift, 1)
    out[group] = jnp.where((lane >= shift) & (lane < shift + count), moved, out[group])
    out[group + 1] = jnp.where(lane < shift + count - rows.shape[1], moved, out[group + 1])


def tile_kernel(source_ref, target_ref, *refs):
    tile_ref, share_ref, columns, density = refs[-4:]
    bricks, slots = source_ref.shape[0], source_ref.shape[2]
    channels = share_ref.shape[1]
    step = pl.program_id(0)

    @pl.when(step == 0)
    def _():
        for brick in range(bricks):
            density[:, brick * slots : (brick + 1) * slots] = source_ref[brick, :channels].astype(jnp.bfloat16)

    @pl.when(jnp.max(target_ref[0, 4:5, :]) > 0.0)
    def _():
        columns[...] = jnp.transpose(target_ref[0])
        spread = [jnp.broadcast_to(columns[:, d : d + 1], (slots, slots)) for d in range(3)]
        total = jnp.zeros((channels, slots), jnp.float32)
        for pair in range(0, bricks, 2):
            both = []
            for brick in (pair, pair + 1):
                delta = [spread[d] - source_ref[brick, channels + d : channels + d + 1, :] for d in range(3)]
                square = delta[0] * delta[0] + (delta[1] * delta[1] + (delta[2] * delta[2] + 1e-30))
                turns = square * lax.rsqrt(square)
                angle = 0.25 - jnp.abs(turns - jnp.round(turns))
                angle2 = angle * angle
                wave = SINE[-1]
                for c in SINE[-2::-1]:
                    wave = wave * angle2 + c
                weight = source_ref[brick, channels + 3 : channels + 4, :]
                value = (angle * weight) * wave / (turns + soften * TURNS)
                both.append(value.astype(jnp.bfloat16))
                tile_ref[:, brick * slots : (brick + 1) * slots] = both[-1]
            at = slice(pair * slots, (pair + 2) * slots)
            total = total + across(density[:, at], jnp.concatenate(both, axis=1))
        share_ref[0] = total


def make_tile(part, sources, targets, channels, before=()):
    bricks, slots = sources.shape[0], sources.shape[2]
    far = pl.BlockSpec(memory_space=pl.ANY)
    return pl.pallas_call(
        tile_kernel,
        grid=(-(-bricks // TILES),),
        in_specs=[
            pl.BlockSpec(sources.shape, lambda b: (0, 0, 0)),
            pl.BlockSpec((1, targets.shape[1], slots), lambda b: (TILES * b + part, 0, 0)),
        ]
        + [far] * len(before),
        out_specs=[
            pl.BlockSpec((slots, bricks * slots), lambda b: (TILES * b + part, 0)),
            pl.BlockSpec((1, channels, slots), lambda b: (TILES * b + part, 0, 0)),
        ],
        out_shape=[
            jax.ShapeDtypeStruct((ROOM * bricks * slots, bricks * slots), jnp.bfloat16),
            jax.ShapeDtypeStruct((bricks + 2, channels, slots), jnp.float32),
        ],
        scratch_shapes=[
            pltpu.VMEM((slots, targets.shape[1]), jnp.float32),
            pltpu.VMEM((channels, bricks * slots), jnp.bfloat16),
        ],
        input_output_aliases={2 + n: n for n in range(len(before))},
        compiler_params=params(8),
        name="tile",
    )(sources, targets, *before)


def taken(share_ref, begin, count, bricks):
    group, shift = begin >> 7, begin & 127
    lane = lanes(share_ref.shape[1:])
    slots = share_ref.shape[2]
    this = pltpu.roll(share_ref[group], (slots - shift) & 127, 1)
    following = pltpu.roll(share_ref[jnp.minimum(group + 1, bricks - 1)], (slots - shift) & 127, 1)
    return jnp.where(lane < count, jnp.where(lane < slots - shift, this, following), 0.0)


def arrange_kernel(counts, share_ref, out_ref, table, arrived):
    copy = pltpu.make_async_copy(counts, table, arrived)
    copy.start()
    bricks = out_ref.shape[0]
    for brick in range(bricks):
        for n in range(6):
            if not 0 <= brick // 2 + n % 3 - 1 < bricks // 2:
                out_ref[brick, n] = jnp.zeros(out_ref.shape[2:], jnp.float32)
    copy.wait()
    begin = jnp.int32(0)
    for index in range(bricks):
        value = taken(share_ref, begin, table[0, index], bricks)
        begin = begin + table[0, index]
        for n in range(6):
            side, other = index // 2 - (n % 3 - 1), (index + n // 3) % 2
            if 0 <= side < bricks // 2:
                out_ref[side * 2 + other, n] = value


def product_kernel(table_ref, density_ref, tile_ref, out_ref, density, shares):
    bricks, channels, slots = density_ref.shape
    step = pl.program_id(0)
    count = tile_ref.shape[0] // slots

    @pl.when(step == 0)
    def _():
        for brick in range(bricks):
            density[:, brick * slots : (brick + 1) * slots] = density_ref[brick]

    @pl.when(step * count * slots < table_ref[bricks])
    def _():
        total = across(density[...], tile_ref[...])
        for index in range(count):
            shares[step * count + index] = total[:, index * slots : (index + 1) * slots]

    @pl.when(step == pl.num_programs(0) - 1)
    def _():
        for brick in range(bricks):
            begin = table_ref[brick]
            out_ref[brick] = taken(shares, begin, table_ref[brick + 1] - begin, bricks)


def products(table, density, tile, rows):
    bricks, channels, slots = density.shape
    width = tile.shape[1]
    steps = bricks * slots // rows

    def block(b, table_ref):
        last = (table_ref[bricks] + rows - 1) // rows - 1
        return jnp.minimum(b, last), 0

    return pl.pallas_call(
        product_kernel,
        grid_spec=pltpu.PrefetchScalarGridSpec(
            num_scalar_prefetch=1,
            grid=(steps,),
            in_specs=[pl.BlockSpec(density.shape, lambda b, t: (0, 0, 0)), pl.BlockSpec((rows, width), block)],
            out_specs=pl.BlockSpec((bricks, channels, slots), lambda b, t: (0, 0, 0)),
            scratch_shapes=[
                pltpu.VMEM((channels, width), jnp.bfloat16),
                pltpu.VMEM((bricks, channels, slots), jnp.float32),
            ],
        ),
        out_shape=jax.ShapeDtypeStruct((bricks, channels, slots), jnp.float32),
        compiler_params=params(12),
        name="product",
    )(table, density, tile)


def put_planes(up_ref, down_ref, base, field_ref, depth, offset=0):
    size_x, size_y = field_ref.shape[-3], field_ref.shape[-2]
    for e in range(field_ref.shape[0]):
        for i in range(depth):
            rows = pl.ds(base + (e * depth + i) * size_y, size_y)
            high = field_ref[e, size_x - depth + i] + offset
            low = field_ref[e, i] + offset
            up_ref[rows, :] = high.astype(jnp.bfloat16)
            down_ref[rows, :] = low.astype(jnp.bfloat16)
    return base + field_ref.shape[0] * depth * size_y


def own_cells(frame_ref, field_ref, offset=0):
    channels, size_x, size_y = field_ref.shape[:3]
    planes, rows = size_x + 2 * XO, size_y + 2 * YO
    frame_ref[...] = jnp.zeros_like(frame_ref)
    for e in range(channels):
        for x in range(size_x):
            at = (e * planes + XO + x) * rows + YO
            frame_ref[at : at + size_y, :] = field_ref[e, x].astype(jnp.float32) + offset


def put_framed_planes(up_ref, down_ref, frame_ref, channels, depth):
    rows = SIZE_Y + 2 * YO
    planes = frame_ref.shape[0] // (channels * rows)
    for e in range(channels):
        for i in range(depth):
            here = pl.ds((e * depth + i) * SIZE_Y, SIZE_Y)
            high = (e * planes + planes - XO - depth + i) * rows + YO
            low = (e * planes + XO + i) * rows + YO
            up_ref[here, :] = frame_ref[high : high + SIZE_Y, :].astype(jnp.bfloat16)
            down_ref[here, :] = frame_ref[low : low + SIZE_Y, :].astype(jnp.bfloat16)


def planes_kernel(
    factor, state_hbm, source_hbm, class_hbm, geometry_hbm, cell_hbm, live_hbm, shift_hbm,
    up_ref, down_ref, message_ref, state_ref, source_ref, class_ref, geometry_ref, cell_ref, live_ref, shift_ref, arrived,
):
    pairs = (
        (live_hbm, live_ref), (shift_hbm, shift_ref), (geometry_hbm, geometry_ref), (cell_hbm, cell_ref),
        (state_hbm, state_ref), (source_hbm, source_ref), (class_hbm, class_ref),
    )
    copies = [pltpu.make_async_copy(a, b, arrived.at[n]) for n, (a, b) in enumerate(pairs)]
    for copy in copies:
        copy.start()
    slots = cell_ref.shape[1]
    for copy in copies[:4]:
        copy.wait()
    shifts = jnp.zeros((1, slots), jnp.float32)
    for index in range(CLASSES):
        shifts = jnp.where(lanes((1, slots)) == index, shift_ref[index], shifts)
    message = jnp.concatenate(
        [
            geometry_ref[:3] * TURNS,
            geometry_ref[3:] * (factor * TURNS),
            jnp.full((1, slots), live_ref[0], jnp.int32).astype(jnp.float32),
            cell_ref[...].astype(jnp.float32),
            shifts,
            jnp.zeros((1, slots), jnp.float32),
        ],
        axis=0,
    )
    for brick in range(message_ref.shape[0]):
        message_ref[brick] = message
    for copy in copies[4:]:
        copy.wait()
    base = put_planes(up_ref, down_ref, 0, state_ref, 3)
    base = put_planes(up_ref, down_ref, base, source_ref, 2)
    put_planes(up_ref, down_ref, base, class_ref, 2, 1.0)


def own_kernel(state_ref, source_ref, class_ref, kept_ref):
    frame_ref, forcing_ref, code_ref, _, _ = parted(kept_ref)
    own_cells(frame_ref, state_ref)
    own_cells(forcing_ref, source_ref)
    own_cells(code_ref, class_ref, 1.0)


def beside(frame_ref, channels, low_ref, high_ref, base, depth):
    rows = SIZE_Y + 2 * YO
    planes = frame_ref.shape[0] // (channels * rows)
    size_x = planes - 2 * XO
    for e in range(channels):
        for i in range(depth):
            here = pl.ds(base + (e * depth + i) * SIZE_Y, SIZE_Y)
            at = (e * planes + XO - depth + i) * rows + YO
            frame_ref[at : at + SIZE_Y, :] = low_ref[here, :].astype(jnp.float32)
            at = (e * planes + XO + size_x + i) * rows + YO
            frame_ref[at : at + SIZE_Y, :] = high_ref[here, :].astype(jnp.float32)
    return base + channels * depth * SIZE_Y


def depth_rows(frames, gz, x, size_y, rows, planes, channels):
    lane = lanes((size_y, 128))
    out = jnp.zeros((size_y, 128), jnp.float32)
    for e in range(channels):
        for index, frame_ref in enumerate(frames):
            own = frame_ref.shape[0] == planes * rows
            at = ((0 if own else e) * planes + x) * rows + YO
            start = e * 16 + index * SEND + 1
            moved = turned(frame_ref[at : at + size_y, :], start + 3 - 3 * gz)
            out = jnp.where((lane >= start) & (lane < start + 3), moved, out)
    return out


def frame_kernel(full, channels, _, low_ref, high_ref, kept_ref, depth_ref):
    frame_ref, forcing_ref, code_ref, _, _ = parted(kept_ref)
    rows = SIZE_Y + 2 * YO
    planes = frame_ref.shape[0] // (channels * rows)
    base = beside(frame_ref, channels, low_ref, high_ref, 0, 3)
    frames = [frame_ref]
    if full:
        base = beside(forcing_ref, channels, low_ref, high_ref, base, 2)
        beside(code_ref, 1, low_ref, high_ref, base, 2)
        frames = [frame_ref, forcing_ref, code_ref]
    gz = lax.axis_index("gz")
    for x in range(planes):
        out = depth_rows(frames, gz, x, SIZE_Y, rows, planes, channels)
        depth_ref[x * SIZE_Y : (x + 1) * SIZE_Y, :] = out.astype(jnp.bfloat16)


def edge_kernel(full, kept_ref, other_ref, depth_ref, up_ref, down_ref):
    frame_ref, forcing_ref, code_ref, _, _ = parted(kept_ref)
    rows = SIZE_Y + 2 * YO
    planes = depth_ref.shape[0] // rows
    depth_ref[...] = jnp.zeros_like(depth_ref)
    for x in range(planes):
        here = other_ref[x * SIZE_Y : (x + 1) * SIZE_Y, :].astype(jnp.float32)
        depth_ref[x * rows + YO : x * rows + YO + SIZE_Y, :] = here

    def put(base, ref, depth, step):
        count = ref.shape[0] // rows
        for j in range(depth):
            high = ref[pl.ds(YO + SIZE_Y - depth + j, count, stride=rows), :]
            low = ref[pl.ds(YO + j, count, stride=rows), :]
            up_ref[base + j * step : base + j * step + count, :] = high.astype(jnp.bfloat16)
            down_ref[base + j * step : base + j * step + count, :] = low.astype(jnp.bfloat16)
        return base + depth * step

    if full:
        up_ref[edge_tail(full) :, :] = jnp.zeros((80, 128), jnp.bfloat16)
        down_ref[edge_tail(full) :, :] = jnp.zeros((80, 128), jnp.bfloat16)
    else:
        up_ref[edge_tail(full) :, :] = jnp.zeros((48, 128), jnp.bfloat16)
        down_ref[edge_tail(full) :, :] = jnp.zeros((48, 128), jnp.bfloat16)
    base = put(0, frame_ref, 3, 80)
    if full:
        base = put(base, forcing_ref, 2, 80)
        base = put(base, code_ref, 2, 16)
    put(base, depth_ref, 3, 16)


def edge_tail(full):
    return 400 if full else 240


def take_edges(frame_ref, low_ref, high_ref, base, depth, step):
    rows = SIZE_Y + 2 * YO
    count = frame_ref.shape[0] // rows
    for j in range(depth):
        low = low_ref[base + j * step : base + j * step + count, :].astype(jnp.float32)
        high = high_ref[base + j * step : base + j * step + count, :].astype(jnp.float32)
        frame_ref[pl.ds(YO - depth + j, count, stride=rows), :] = low
        frame_ref[pl.ds(YO + SIZE_Y + j, count, stride=rows), :] = high
    return base + depth * step


def faces(get, e_range, gz, shape):
    lane = lanes(shape)
    out = jnp.zeros(shape, jnp.float32)
    for e in e_range:
        out = jnp.where(lane == e * 16 + 4 * gz, turned(get(e), e * 16 + 1 + 3 * gz), out)
    return out


def sweep(src, dst, zsrc, zdst, forcing, coef, zforcing, zcoef, gz, x_low, x_high, channels, planes, finish=None):
    rows = SIZE_Y + 2 * YO
    shape = (rows, 128)
    lane = lanes(shape)
    keep = 1.0 - relax_weight
    inner_low = (lane > 0).astype(jnp.float32)
    inner_high = (lane < 127).astype(jnp.float32)
    border = (lane == 127 - 127 * gz).astype(jnp.float32)
    face_lane = (lane & 15) == 4 * gz

    def one_plane(x, carry):
        at = pl.multiple_of(x * rows, 8)
        other = zsrc[pl.ds(at, rows), :]
        weight = coef[pl.ds(at, rows), :]
        fresh = []
        for e in range(channels):
            row = pl.multiple_of((e * planes + x) * rows, 8)
            own = src[pl.ds(row, rows), :]
            total = src[pl.ds(row + rows, rows), :] + src[pl.ds(row - rows, rows), :]
            total = total + pltpu.roll(own, rows - 1, 0) + pltpu.roll(own, 1, 0)
            total = total + pltpu.roll(own, 127, 1) * inner_high + pltpu.roll(own, 1, 1) * inner_low
            total = total + turned(other, 126 - gz - 16 * e + 256) * border
            new = keep * own + weight * (forcing[pl.ds(row, rows), :] + total)
            if finish is None:
                dst[pl.ds(row, rows), :] = new
            else:
                finish(e, x, new)
            fresh.append(new)
        if finish is None:
            total = zsrc[pl.ds(at + rows, rows), :] + zsrc[pl.ds(at - rows, rows), :]
            total = total + pltpu.roll(other, rows - 1, 0) + pltpu.roll(other, 1, 0)
            total = total + pltpu.roll(other, 127, 1) + pltpu.roll(other, 1, 1)
            new = keep * other + zcoef[pl.ds(at, rows), :] * (zforcing[pl.ds(at, rows), :] + total)
            face = faces(lambda e: fresh[e], range(channels), gz, shape)
            zdst[pl.ds(at, rows), :] = jnp.where(face_lane, face, new)
        return carry

    lax.fori_loop(x_low, x_high, one_plane, 0, unroll=True)


def sweeps(frame, second, zframe, zsecond, forcing, coef, zforcing, zcoef, gz, channels, planes, finish):
    rows = SIZE_Y + 2 * YO
    face_lane = (lanes((rows, 128)) & 15) == 4 * gz
    for x in range(planes):
        face = faces(lambda e: frame[(e * planes + x) * rows : (e * planes + x + 1) * rows, :], range(channels), gz, (rows, 128))
        here = zframe[x * rows : (x + 1) * rows, :]
        zframe[x * rows : (x + 1) * rows, :] = jnp.where(face_lane, face, here)
    sweep(frame, second, zframe, zsecond, forcing, coef, zforcing, zcoef, gz, 1, planes - 1, channels, planes)
    sweep(second, frame, zsecond, zframe, forcing, coef, zforcing, zcoef, gz, 2, planes - 2, channels, planes)

    sweep(frame, None, zframe, None, forcing, coef, zforcing, zcoef, gz, XO, planes - XO, channels, planes, finish)


def density_of(layers, cell, live, channels):
    slots, size_z = cell.shape[1], layers.shape[1]
    pick = (lax.broadcasted_iota(jnp.int32, (size_z, slots), 0) == (cell & (size_z - 1))).astype(jnp.bfloat16)
    count = layers.shape[0] // channels
    lines = jnp.dot(layers.astype(jnp.bfloat16), pick, preferred_element_type=jnp.float32)
    used = lanes((count, slots)) < live.astype(jnp.int32)
    mask = used & (lax.broadcasted_iota(jnp.int32, (count, slots), 0) == (cell >> 7))
    found = [
        jnp.sum(jnp.where(mask, lines[e * count : (e + 1) * count, :], 0.0), axis=0, keepdims=True)
        for e in range(channels)
    ]
    return jnp.concatenate(found, axis=0).astype(jnp.bfloat16)


def parted(kept_ref):
    rows = kept_ref.shape[0] // KEPT
    frame = (KEPT - 3) // 2 * rows
    ends = [0, frame, 2 * frame] + [2 * frame + n * rows for n in range(1, 4)]
    return [kept_ref.at[ends[n] : ends[n + 1]] for n in range(5)]


def first_kernel(
    _, depth_ref, low_ref, high_ref, note_ref,
    kept_ref, density_ref, up_ref, down_ref, first, second, zfirst, zsecond, code, zcode, layers,
):
    gz = lax.axis_index("gz")
    rows = SIZE_Y + 2 * YO
    planes = depth_ref.shape[0] // rows
    state, forcing, coef, zforcing, zcoef = parted(kept_ref)
    channels = first.shape[0] // (planes * rows)
    first[...] = state[...]
    code[...] = coef[...]
    zcode[...] = depth_ref[...]
    base = take_edges(first, low_ref, high_ref, 0, 3, 80)
    base = take_edges(forcing, low_ref, high_ref, base, 2, 80)
    base = take_edges(code, low_ref, high_ref, base, 2, 16)
    take_edges(zcode, low_ref, high_ref, base, 3, 16)
    lane = lanes((rows, 128)) & 15
    outer = (lane >= 1) & (lane <= 3)
    shifts = [jnp.broadcast_to(note_ref[6:7, n : n + 1], (rows, 128)) for n in range(CLASSES)]
    for x in range(planes):
        here = pl.ds(x * rows, rows)
        packed = zcode[here, :]
        zfirst[here, :] = jnp.where(outer, packed, 0.0)
        zforcing[here, :] = jnp.where(outer, turned(packed, 128 - SEND), 0.0)
        level = jnp.where(outer, turned(packed, 128 - 2 * SEND), 0.0)
        own_level = code[here, :]
        zshift = jnp.zeros((rows, 128), jnp.float32)
        shift = jnp.zeros((rows, 128), jnp.float32)
        for index in range(CLASSES):
            zshift = jnp.where(level == index + 1.0, shifts[index], zshift)
            shift = jnp.where(own_level == index + 1.0, shifts[index], shift)
        zcoef[here, :] = jnp.where(level > 0.0, relax_weight / (6.0 + zshift), 0.0)
        coef[here, :] = jnp.where(own_level > 0.0, relax_weight / (6.0 + shift), 0.0)

    def finish(e, x, new):
        own = new[YO : YO + SIZE_Y, :]
        state[pl.ds((e * planes + x) * rows + YO, SIZE_Y), :] = own
        layers[pl.ds((e * (planes - 2 * XO) + x - XO) * SIZE_Y, SIZE_Y), :] = own

    sweeps(first, second, zfirst, zsecond, forcing, coef, zforcing, zcoef, gz, channels, planes, finish)
    put_framed_planes(up_ref, down_ref, state, channels, 3)
    density = density_of(layers[...], note_ref[5:6, :].astype(jnp.int32), note_ref[4:5, :], channels)
    message = jnp.concatenate([density.astype(jnp.float32), note_ref[...]], axis=0)
    for brick in range(density_ref.shape[0]):
        density_ref[brick] = message


def add_load(forcing, zforcing, near_ref, side, gz, channels, planes):
    rows = SIZE_Y + 2 * YO
    size_x = planes - 2 * XO
    cells = near_ref[6].astype(jnp.int32)
    slots = cells.shape[1]
    wide = 3 * slots

    def row_of(first):
        cell = jnp.concatenate([cells[first + n : first + n + 1, :] for n in range(3)], axis=1)
        shift = jnp.concatenate([jnp.full((1, slots), YO + SIZE_Y * (n - 1), jnp.int32) for n in range(3)], axis=1)
        value = coupling * jnp.concatenate([near_ref[first + n] for n in range(3)], axis=1)
        return cell & 127, ((cell >> 7) & (SIZE_Y - 1)) + shift, cell >> 11, value

    span = {-1: range(size_x - 2, size_x), 0: range(size_x), 1: range(2)}[side]
    level = lax.broadcasted_iota(jnp.int32, (rows, wide), 0)
    z, y, x, value = row_of(0)
    pick = (lax.broadcasted_iota(jnp.int32, (128, wide), 0) == z).astype(jnp.bfloat16)
    for plane in span:
        mask = (level == y) & (x == plane)
        spread = jnp.concatenate([jnp.where(mask, value[e : e + 1, :], 0.0) for e in range(channels)], axis=0)
        high, low = split(spread)
        load = across(high, pick) + across(low, pick)
        at = plane + XO + size_x * side
        for e in range(channels):
            row = (e * planes + at) * rows
            forcing[row : row + rows, :] += load[e * rows : (e + 1) * rows, :]
    z, y, x, value = row_of(3)
    lane = z - 125 * gz + 1
    step = lax.broadcasted_iota(jnp.int32, (16, wide), 0)
    ok = (step == lane) & (step >= 1) & (step <= 3)
    spread = jnp.concatenate([jnp.where(ok, value[e : e + 1, :], 0.0) for e in range(channels)], axis=0)
    high, low = split(spread)
    for plane in span:
        mask = ((level == y) & (x == plane)).astype(jnp.bfloat16)
        row = (plane + XO + size_x * side) * rows
        zforcing[row : row + rows, :] += across(mask, high) + across(mask, low)


def ready_kernel(channels, _, unused, low_ref, high_ref, near_own, kept_ref, depth_ref):
    gz = lax.axis_index("gz")
    planes = depth_ref.shape[0] // (SIZE_Y + 2 * YO)
    state, forcing, _, zforcing, _ = parted(kept_ref)
    base = take_edges(state, low_ref, high_ref, 0, 3, 80)
    take_edges(depth_ref, low_ref, high_ref, base, 3, 16)
    add_load(forcing, zforcing, near_own, 0, gz, channels, planes)


def second_kernel(
    _, unused, near_low, near_own, near_high, out_ref, density_ref, kept_ref, zfirst, second, zsecond,
):
    gz = lax.axis_index("gz")
    planes = zfirst.shape[0] // (SIZE_Y + 2 * YO)
    channels = out_ref.shape[0]
    first, forcing, coef, zforcing, zcoef = parted(kept_ref)
    for side, near in ((-1, near_low), (1, near_high)):
        add_load(forcing, zforcing, near, side, gz, channels, planes)

    def finish(e, x, new):
        out_ref[e, x - XO] = new[YO : YO + SIZE_Y, :]

    sweeps(first, second, zfirst, zsecond, forcing, coef, zforcing, zcoef, gz, channels, planes, finish)
    layers = out_ref[...].reshape(-1, out_ref.shape[3])
    density = density_of(layers, near_own[6, 1:2, :].astype(jnp.int32), near_own[6, 7:8, :], channels)
    for brick in range(density_ref.shape[0]):
        density_ref[brick] = density


def near_kernel(parts_ref, targets_ref, near_ref):
    col, gz = lax.axis_index("col"), lax.axis_index("gz")
    cols = targets_ref.shape[0] // 2
    slots = targets_ref.shape[2]
    lane = lanes((8, slots))
    near_ref[6] = jnp.zeros((8, slots), jnp.float32)
    for n in range(6):
        side = jnp.clip(col + n % 3 - 1, 0, cols - 1)
        half = gz if n < 3 else 1 - gz
        about = targets_ref[side * 2 + half]
        total = parts_ref[0, n]
        for sender in range(1, parts_ref.shape[0]):
            total = total + parts_ref[sender, n]
        total = jnp.where(lane < about[4:5, :].astype(jnp.int32), total, 0.0)
        near_ref[n] = total
        near_ref[6, n : n + 1, :] = about[5:6, :]
        if n == 1:
            near_ref[6, 7:8, :] = about[4:5, :]


def last_kernel(parts_ref, own_ref):
    total = parts_ref[0]
    for sender in range(1, parts_ref.shape[0]):
        total = total + parts_ref[sender]
    own_ref[...] = total


def both_ways(up, down, axis):
    devices = lax.axis_size(axis)
    pairs = [(i, i + 1) for i in range(devices - 1)]
    return lax.ppermute(up, axis, pairs), lax.ppermute(down, axis, [(b, a) for a, b in pairs])


def local(
    initial_field, source_term, cell_class, class_shift, surface_cell, live_count, panel_geometry
):
    channels, size_x, size_y, size_z = initial_field.shape
    slots = surface_cell.shape[0]
    bricks = lax.axis_size("row")
    panels = slots * lax.axis_size("row") * lax.axis_size("col") * lax.axis_size("gz")
    factor = 1.0 / math.sqrt(panels)
    planes, rows = size_x + 2 * XO, size_y + 2 * YO
    frame, flat = (channels * planes * rows, 128), (planes * rows, 128)
    cells = surface_cell[None]
    vm = lambda shape, dtype=jnp.float32: pltpu.VMEM(shape, dtype)

    send_x = channels * 5 * size_y + 2 * size_y
    up, down, message = whole_call(
        functools.partial(planes_kernel, factor),
        (bf16(send_x, 128), bf16(send_x, 128), f32(bricks, 8, slots)),
        [vm(initial_field.shape), vm(initial_field.shape), vm((1, *cell_class.shape), jnp.int32),
         vm(panel_geometry.shape), vm(cells.shape, jnp.int32), pltpu.SMEM((1,), jnp.int32), pltpu.SMEM((CLASSES,), jnp.float32),
         pltpu.SemaphoreType.DMA((7,))],
        "planes", (), initial_field, source_term, cell_class[None], panel_geometry, cells, live_count, class_shift,
        away=(0, 1, 2, 3, 4, 5, 6), megabytes=62,
    )
    kept = whole_call(
        own_kernel, f32(2 * frame[0] + 3 * flat[0], 128), [], "own", (),
        initial_field, source_term, cell_class[None],
    )
    low, high = both_ways(up, down, "row")
    kept, depth = whole_call(
        functools.partial(frame_kernel, True, channels),
        (f32(*kept.shape), bf16(planes * size_y, 128)), [], "frame", (),
        kept, low, high, aliases={0: 0},
    )
    other = lax.ppermute(depth, "gz", [(0, 1), (1, 0)])
    targets = lax.all_to_all(message, ("col", "gz"), 0, 0, tiled=True)
    other, targets = lax.optimization_barrier((other, targets))
    zframe, up, down = whole_call(
        functools.partial(edge_kernel, True), (f32(*flat), bf16(480, 128), bf16(480, 128)), [], "edges", (),
        kept, other,
    )
    low, high = both_ways(up, down, "col")
    smem = pl.BlockSpec(memory_space=pltpu.SMEM)
    vmem = pl.BlockSpec(memory_space=pltpu.VMEM)
    aims, note, counts, table = pl.pallas_call(
        compact_kernel,
        in_specs=[vmem],
        out_specs=(vmem, vmem, vmem, smem),
        out_shape=(f32(bricks + 2, 8, slots), f32(8, slots), jax.ShapeDtypeStruct((8, slots), jnp.int32), jax.ShapeDtypeStruct((bricks + 1,), jnp.int32)),
        scratch_shapes=[pltpu.SMEM((8, slots), jnp.int32), pltpu.SemaphoreType.DMA],
        compiler_params=params(4),
        name="compact",
    )(targets)
    low, high, aims, table = lax.optimization_barrier((low, high, aims, table))
    kept, density, up, down = whole_call(
        first_kernel,
        (f32(*kept.shape), f32(bricks, 2 * channels, slots),
         bf16(channels * 3 * size_y, 128), bf16(channels * 3 * size_y, 128)),
        [vm(frame), vm(frame), vm(flat), vm(flat), vm(flat), vm(flat),
         vm((channels * size_x * size_y, size_z))], "first", (),
        kept, zframe, low, high, note, aliases={0: 0}, megabytes=8,
    )
    low, high = both_ways(up, down, "row")
    densities = lax.all_to_all(density, "row", 0, 0, tiled=True)
    done = make_tile(0, densities, aims, channels)
    low, high, done = lax.optimization_barrier((low, high, done))
    kept, depth = whole_call(
        functools.partial(frame_kernel, False, channels),
        (f32(*kept.shape), bf16(planes * size_y, 128)), [], "frame", (),
        kept, low, high, aliases={0: 0},
    )
    other = lax.ppermute(depth, "gz", [(0, 1), (1, 0)])
    densities, depth = lax.optimization_barrier((densities, depth))
    done = make_tile(1, densities, aims, channels, done)
    other, done = lax.optimization_barrier((other, done))
    zframe, up, down = whole_call(
        functools.partial(edge_kernel, False), (f32(*flat), bf16(288, 128), bf16(288, 128)), [], "edges", (),
        kept, other,
    )
    low, high = both_ways(up, down, "col")
    densities, up = lax.optimization_barrier((densities, up))
    tile, shares = make_tile(2, densities, aims, channels, done)
    shares = whole_call(
        arrange_kernel, f32(bricks, 6, channels, slots),
        [pltpu.SMEM((8, slots), jnp.int32), pltpu.SemaphoreType.DMA], "arrange", (), counts, shares,
    )
    parts = lax.all_to_all(shares, ("col", "gz"), 0, 0, tiled=True)
    near = whole_call(near_kernel, f32(7, channels, slots), [], "near", (), parts, targets)
    near_low, near_high = both_ways(near, near, "row")
    kept, zframe = whole_call(
        functools.partial(ready_kernel, channels), (f32(*kept.shape), f32(*flat)), [], "ready", (),
        kept, zframe, low, high, near, aliases={0: 0, 1: 1},
    )
    state, density, _, _ = whole_call(
        second_kernel,
        (f32(*initial_field.shape), bf16(bricks, channels, slots), f32(*kept.shape), f32(*flat)),
        [vm(frame), vm(flat)], "second", (),
        kept, zframe, near_low, near, near_high, aliases={0: 2, 1: 3}, megabytes=8,
    )
    densities = lax.all_to_all(density, "row", 0, 0, tiled=True)
    shares = products(table, densities, tile, 512)
    parts = lax.all_to_all(shares, ("col", "gz"), 0, 0, tiled=True)
    potential = whole_call(last_kernel, f32(channels, slots), [], "last", (), parts)
    return (state, potential)


def solution(mesh):
    placed = (
        P(None, "row", "col", "gz"),
        P(None, "row", "col", "gz"),
        P("row", "col", "gz"),
        P(),
        P(("row", "col", "gz")),
        P(("row", "col", "gz")),
        P(None, ("row", "col", "gz")),
    )
    return jax.shard_map(
        local,
        mesh=mesh,
        in_specs=placed,
        out_specs=(P(None, "row", "col", "gz"), P(None, ("row", "col", "gz"))),
        check_vma=False,
    )
```
